32 devices in a mesh: shard: 8 (over z, y), ctx: 2 (over x), tp: 2 (over core).
Axes of the slice: x: 2, y: 2, z: 4, core: 2. Of those that a mesh axis runs over, the one named last changes fastest.
Arguments:
- hidden: bfloat16 [8, 2048, 768], P('shard', 'ctx'), may hold values from -6 to 6
- block_order: int32 [4], replicated, may hold values from 0 to 3, each once
- ln1_gain: bfloat16 [768], P('shard'), may hold values from 0.099609375 to 1.8984375
- ln1_bias: bfloat16 [768], P('shard'), may hold values from -1.5 to 1.5
- ln2_gain: bfloat16 [768], P('shard'), may hold values from 0.099609375 to 1.8984375
- ln2_bias: bfloat16 [768], P('shard'), may hold values from -1.5 to 1.5
- q_weight: bfloat16 [768, 768], P('shard', 'tp'), may hold values from -0.21875 to 0.21875
- kv_weight: bfloat16 [768, 128], P('shard'), may hold values from -0.21875 to 0.21875
- o_weight: bfloat16 [768, 768], P('shard', 'tp'), may hold values from -1.25 to 1.25
- up_weight: bfloat16 [768, 3072], P('shard', 'tp'), may hold values from -0.21875 to 0.21875
- down_weight: bfloat16 [768, 3072], P('shard', 'tp'), may hold values from -0.109375 to 0.109375
- cotangent: bfloat16 [8, 2048, 768], P('shard', 'ctx'), may hold values from -6 to 6
Outputs:
- out_tokens: bfloat16 [8, 2048, 768], P('shard', 'ctx')
- keys_out: bfloat16 [8, 2048, 64], P('shard', 'ctx')
- values_out: bfloat16 [8, 2048, 64], P('shard', 'ctx')
- hidden_grad: float32 [8, 2048, 768], P('shard', 'ctx')
- ln1_gain_grad: float32 [768], P('shard')
- ln1_bias_grad: float32 [768], P('shard')
- ln2_gain_grad: float32 [768], P('shard')
- ln2_bias_grad: float32 [768], P('shard')
- q_weight_grad: float32 [768, 768], P('shard', 'tp')
- kv_weight_grad: float32 [768, 128], P('shard')
- o_weight_grad: float32 [768, 768], P('shard', 'tp')
- up_weight_grad: float32 [768, 3072], P('shard', 'tp')
- down_weight_grad: float32 [768, 3072], P('shard', 'tp')
The draws below stay inside these ranges and needn't reach their ends.
Inputs may be any that keep to these rules, and one draw needn't show every extreme that they name: `block_order`: each of the 4 values appears once.
All inputs are finite; a program needn't handle non-finite values.
Results may differ from the reference program's by a relative error of at most 0.017.
Values may be sent and summed in bfloat16 or wider, within the bound.
A program may use at most 256 MiB of HBM per device.

```python
import jax
import jax.numpy as jnp
from jax import lax

D = 768
HEADS = 12
HEAD_DIM = 64
ROT = 16
FF = 3072
LEN = 2048
HQ = 768
SEQS = 8
BLOCKS = 4
HALF = 512


def with_spikes(entries, rng, source, target, parts, factor):
    owner, partner = [(jnp.arange(entries.shape[axis_at]) // (entries.shape[axis_at] // parts)).reshape([-1 if axis == axis_at else 1 for axis in range(entries.ndim)]) for axis_at in (source, target)]
    chosen = jax.random.permutation(rng, parts)[partner]
    strong = (owner == chosen) | (owner == (partner + parts // 2) % parts)
    return jnp.where(strong, factor * entries, entries)


def block_scale(rng, extent, cuts, least, high):
    loudness = 1.0
    for position, blocks in cuts:
        steps = jax.random.uniform(jax.random.fold_in(jax.random.fold_in(rng, 6), position), (blocks,), jnp.float32, least / len(cuts), high / len(cuts))
        loudness = loudness * jnp.repeat(jnp.exp(steps), extent[position] // blocks).reshape((-1,) + (1,) * (len(extent) - 1 - position))
    return loudness


def scatter_about(own_key, shape, width, reach, split=(), kind=jnp.bfloat16):
    level = block_scale(own_key, shape, split, -0.22, 0.18) if split else 1.0
    entries = jax.random.normal(own_key, shape, jnp.float32) * width * level
    return jnp.minimum(jnp.maximum(entries, -reach), reach).astype(kind)


def heavy_noise(own_key, extent, scale, most, pieces, heavy, held_as=jnp.bfloat16):
    entries = scale * jax.random.normal(own_key, extent, jnp.float32)
    if pieces:
        entries = entries * block_scale(own_key, extent, pieces, -0.22, 0.18)
    return jnp.clip(with_spikes(entries, jax.random.fold_in(own_key, 3), *heavy), -most, most).astype(held_as)


def setup_inputs(seed: int = 0) -> dict:
    seeds = jax.random.split(jax.random.key(seed), 13)
    return {
        "hidden": scatter_about(seeds[0], (SEQS, LEN, D), 1.0, 6.0, ((0, 8), (1, 2))),
        "block_order": jax.random.permutation(seeds[1], BLOCKS).astype(jnp.int32),
        "ln1_gain": jnp.clip(1.0 + 0.18 * jax.random.normal(seeds[2], (D,), jnp.float32), 0.099609375, 1.8984375).astype(jnp.bfloat16),
        "ln1_bias": scatter_about(seeds[3], (D,), 0.3, 1.5, ((0, 8),)),
        "ln2_gain": jnp.clip(1.0 + 0.18 * jax.random.normal(seeds[4], (D,), jnp.float32), 0.099609375, 1.8984375).astype(jnp.bfloat16),
        "ln2_bias": scatter_about(seeds[5], (D,), 0.3, 1.5, ((0, 8),)),
        "q_weight": scatter_about(seeds[6], (D, HQ), D ** -0.5, 0.21875, ((0, 8), (1, 2))),
        "kv_weight": scatter_about(seeds[7], (D, 2 * HEAD_DIM), D ** -0.5, 0.21875, ((0, 8),)),
        "o_weight": scatter_about(seeds[8], (D, HQ), (HQ // 32) ** -0.5, 1.25, ((0, 8), (1, 2))),
        "up_weight": scatter_about(seeds[9], (D, FF), D ** -0.5, 0.21875, ((0, 8), (1, 2))),
        "down_weight": scatter_about(seeds[10], (D, FF), FF ** -0.5, 0.109375, ((0, 8), (1, 2))),
        "cotangent": heavy_noise(seeds[11], (SEQS, LEN, D), 1.0, 6.0, ((0, 8), (1, 2)), (0, 2, 8, 2.0)),
    }


@jax.custom_vjp
def low(v):
    return lax.optimization_barrier(v.astype(jnp.bfloat16)).astype(jnp.float32)

@jax.custom_vjp
def low_back(v):
    return v

def low_keep(v):
    return (low(v), None)

def low_pass(kept, grad):
    return (grad,)

def back_keep(v):
    return (v, None)

def back_low(kept, grad):
    return (low(grad),)
low.defvjp(low_keep, low_pass)
low_back.defvjp(back_keep, back_low)

def layer_norm(values, gain, shift):
    center = values - lax.optimization_barrier(jnp.mean(values, axis=-1, keepdims=True))
    spread = lax.optimization_barrier(jnp.mean(center * center, axis=-1, keepdims=True))
    return center * lax.rsqrt(spread + 1e-05) * gain + shift

def rotate(tensor, places, sign):
    half_rot = ROT // 2
    freq = jnp.power(10000.0, -2.0 * jnp.arange(half_rot, dtype=jnp.float32) / ROT)
    angle = places.astype(jnp.float32)[:, None] * freq[None, :]
    cosine = jnp.cos(angle)[:, None, :]
    sine = sign * jnp.sin(angle)[:, None, :]
    first = tensor[..., :half_rot]
    second = tensor[..., half_rot:ROT]
    return jnp.concatenate([first * cosine - second * sine, second * cosine + first * sine, tensor[..., ROT:]], axis=-1)

def positions(block_order):
    rows = jnp.arange(LEN, dtype=jnp.int32)
    return block_order[rows // HALF] * HALF + rows % HALF

def product(left, right):
    return jnp.dot(left, right, precision=lax.Precision.HIGHEST, preferred_element_type=jnp.float32)

def one_sequence(params, tokens, places):
    gain_attn, bias_attn, gain_ffn, bias_ffn, w_query, w_keyval, w_output, w_up, w_down = params
    norm_attn = low(layer_norm(tokens, gain_attn, bias_attn))
    norm_ffn = low(layer_norm(tokens, gain_ffn, bias_ffn))
    query_pre = low_back(product(norm_attn, w_query)).reshape(LEN, HEADS, HEAD_DIM)
    queries = low(rotate(query_pre, places, 1.0))
    keyval_pre = low_back(product(norm_attn, w_keyval))
    keys = low(rotate(keyval_pre[:, None, :HEAD_DIM], places, 1.0)[:, 0, :])
    values = low(keyval_pre[:, HEAD_DIM:])
    scores = jnp.einsum('qhd,kd->hqk', queries, keys, precision=lax.Precision.HIGHEST, preferred_element_type=jnp.float32)
    scores = low_back(scores * HEAD_DIM ** (-0.5))
    visible = places[None, :] <= places[:, None]
    scores = jnp.where(visible[None], scores, -1e+30)
    probs = jnp.exp(scores - jax.nn.logsumexp(scores, axis=-1, keepdims=True))
    attended = jnp.einsum('hqk,kd->qhd', low(probs), values, precision=lax.Precision.HIGHEST, preferred_element_type=jnp.float32)
    attended = low(low_back(attended)).reshape(LEN, HQ)
    hidden_pre = low_back(product(norm_ffn, w_up))
    activation = low(jax.nn.gelu(hidden_pre, approximate=False))
    mixed = tokens + product(attended, w_output.T) + product(activation, w_down.T)
    return (mixed, keys, values)

def reference(hidden, block_order, ln1_gain, ln1_bias, ln2_gain, ln2_bias, q_weight, kv_weight, o_weight, up_weight, down_weight, cotangent):
    places = positions(block_order)
    params = (ln1_gain.astype(jnp.float32), ln1_bias.astype(jnp.float32), ln2_gain.astype(jnp.float32), ln2_bias.astype(jnp.float32), q_weight.astype(jnp.float32), kv_weight.astype(jnp.float32), o_weight.astype(jnp.float32), up_weight.astype(jnp.float32), down_weight.astype(jnp.float32))
    tokens_all = hidden.astype(jnp.float32)

    def forward(weights, tokens_in):

        def single(sequence):
            return one_sequence(weights, sequence, places)
        return lax.map(jax.checkpoint(single), tokens_in)
    outputs, pull = jax.vjp(forward, params, tokens_all)
    mixed, keys, values = outputs
    weight_grads, token_grads = pull((cotangent.astype(jnp.float32), jnp.zeros_like(keys), jnp.zeros_like(values)))
    return (mixed.astype(jnp.bfloat16), keys.astype(jnp.bfloat16), values.astype(jnp.bfloat16), token_grads, weight_grads[0], weight_grads[1], weight_grads[2], weight_grads[3], weight_grads[4], weight_grads[5], weight_grads[6], weight_grads[7], weight_grads[8])
```

```python
import functools

import jax
import jax.numpy as jnp
from jax import lax
from jax.experimental import pallas as pl
from jax.experimental.pallas import tpu as pltpu
from jax.sharding import PartitionSpec as P

F32 = jnp.float32
BF = jnp.bfloat16
MESH = pl.DeviceIdType.MESH

ROT = 16


def layer_norm(values, gain, shift):
    center = values - jnp.mean(values, axis=-1, keepdims=True)
    spread = jnp.mean(center * center, axis=-1, keepdims=True)
    return center * lax.rsqrt(spread + 1e-05) * gain + shift


def gelu_exact(values):
    return jax.nn.gelu(values, approximate=False)


def rotate(tensor, places, sign):
    half_rot = ROT // 2
    freq = jnp.power(10000.0, -2.0 * jnp.arange(half_rot, dtype=jnp.float32) / ROT)
    angle = places.astype(jnp.float32)[:, None] * freq[None, :]
    cosine = jnp.cos(angle)[:, None, :]
    sine = sign * jnp.sin(angle)[:, None, :]
    first = tensor[..., :half_rot]
    second = tensor[..., half_rot:ROT]
    return jnp.concatenate(
        [first * cosine - second * sine, second * cosine + first * sine, tensor[..., ROT:]], axis=-1
    )


def tok_positions(block_order, rows, half_block):
    index = rows // half_block
    table = jnp.arange(block_order.shape[0], dtype=jnp.int32)
    picked = jnp.sum(jnp.where(index[:, None] == table[None, :], block_order[None, :], 0), axis=1)
    return picked * half_block + rows % half_block


def right_product(left, right):
    return lax.dot_general(
        left, right, (((1,), (1,)), ((), ())), preferred_element_type=jnp.float32
    )


def left_product(left, right):
    return lax.dot_general(
        left, right, (((0,), (0,)), ((), ())), preferred_element_type=jnp.float32
    )


def on_device(
    hidden,
    block_order,
    ln1_gain,
    ln1_bias,
    ln2_gain,
    ln2_bias,
    q_weight,
    kv_weight,
    o_weight,
    up_weight,
    down_weight,
    cotangent,
):
    seqs, span, width = hidden.shape
    half_block = span // 2
    head_size = kv_weight.shape[1] // 2
    local_heads = q_weight.shape[1] // head_size
    row_count = seqs * span
    query_rows = span * local_heads
    scale = head_size ** (-0.5)
    gathered = (
        lax.all_gather(ln1_gain, "shard", axis=0, tiled=True),
        lax.all_gather(ln1_bias, "shard", axis=0, tiled=True),
        lax.all_gather(ln2_gain, "shard", axis=0, tiled=True),
        lax.all_gather(ln2_bias, "shard", axis=0, tiled=True),
        lax.all_gather(q_weight, "shard", axis=0, tiled=True),
        lax.all_gather(kv_weight, "shard", axis=0, tiled=True),
        lax.all_gather(o_weight, "shard", axis=0, tiled=True),
        lax.all_gather(up_weight, "shard", axis=0, tiled=True),
        lax.all_gather(down_weight, "shard", axis=0, tiled=True),
    )
    gain_attn, bias_attn, gain_ffn, bias_ffn, w_query, w_keyval, w_output, w_up, w_down = gathered
    offset = lax.axis_index("ctx") * span
    query_places = tok_positions(
        block_order, offset + jnp.arange(span, dtype=jnp.int32), half_block
    )
    row_places = jnp.repeat(query_places, local_heads)
    tokens = hidden.astype(jnp.float32).reshape(row_count, width)
    norm_attn = layer_norm(
        tokens, gain_attn.astype(jnp.float32), bias_attn.astype(jnp.float32)
    ).astype(jnp.bfloat16)
    norm_ffn = layer_norm(
        tokens, gain_ffn.astype(jnp.float32), bias_ffn.astype(jnp.float32)
    ).astype(jnp.bfloat16)
    query_pre = jnp.dot(norm_attn, w_query, preferred_element_type=jnp.float32).reshape(
        seqs, span, local_heads, head_size
    )
    queries = (
        rotate(query_pre, query_places, 1.0)
        .astype(jnp.bfloat16)
        .reshape(seqs, query_rows, head_size)
    )
    keyval_pre = jnp.dot(norm_attn, w_keyval, preferred_element_type=jnp.float32).reshape(
        seqs, span, 2 * head_size
    )
    keys = rotate(keyval_pre[:, :, None, :head_size], query_places, 1.0)[:, :, 0, :].astype(
        jnp.bfloat16
    )
    values = keyval_pre[:, :, head_size:].astype(jnp.bfloat16)
    start_state = (
        jnp.full((seqs, query_rows), -1e30, jnp.float32),
        jnp.zeros((seqs, query_rows), jnp.float32),
        jnp.zeros((seqs, query_rows, head_size), jnp.float32),
    )
    key_piece = lax.all_gather(keys, "ctx", axis=1, tiled=True)
    value_piece = lax.all_gather(values, "ctx", axis=1, tiled=True)
    count = key_piece.shape[1]
    key_places = tok_positions(block_order, jnp.arange(count, dtype=jnp.int32), half_block)
    visible = key_places[None, :] <= row_places[:, None]

    def one_block(args):
        peak, total, accum, query_block, key_block, value_block = args
        scores = (
            jnp.einsum("qd,kd->qk", query_block, key_block, preferred_element_type=jnp.float32)
            * scale
        )
        scores = jnp.where(visible, scores, -1e30)
        new_peak = jnp.maximum(peak, jnp.max(scores, axis=1))
        factor = jnp.exp(peak - new_peak)
        weights = jnp.where(visible, jnp.exp(scores - new_peak[:, None]), 0.0)
        total = total * factor + jnp.sum(weights, axis=1)
        accum = accum * factor[:, None] + jnp.einsum(
            "qk,kd->qd",
            weights.astype(jnp.bfloat16),
            value_block,
            preferred_element_type=jnp.float32,
        )
        return (new_peak, total, accum)

    peak, total, accum = lax.map(
        one_block, (start_state[0], start_state[1], start_state[2], queries, key_piece, value_piece)
    )
    attended = (
        (accum / total[:, :, None]).astype(jnp.bfloat16).reshape(row_count, local_heads * head_size)
    )
    log_total = peak + jnp.log(total)
    hidden_pre = jnp.dot(norm_ffn, w_up, preferred_element_type=jnp.float32)
    activation_full, gelu_pull = jax.vjp(gelu_exact, hidden_pre)
    activation = activation_full.astype(jnp.bfloat16)
    branch = right_product(attended, w_output) + right_product(activation, w_down)
    branch = lax.psum(branch.astype(jnp.bfloat16), "tp").astype(jnp.float32)
    mixed = (tokens + branch).astype(jnp.bfloat16).reshape(seqs, span, width)
    regathered = (
        lax.all_gather(ln1_gain, "shard", axis=0, tiled=True),
        lax.all_gather(ln2_gain, "shard", axis=0, tiled=True),
        lax.all_gather(q_weight, "shard", axis=0, tiled=True),
        lax.all_gather(kv_weight, "shard", axis=0, tiled=True),
        lax.all_gather(o_weight, "shard", axis=0, tiled=True),
        lax.all_gather(up_weight, "shard", axis=0, tiled=True),
        lax.all_gather(down_weight, "shard", axis=0, tiled=True),
    )
    gain_attn, gain_ffn, w_query, w_keyval, w_output, w_up, w_down = regathered
    grad_out = cotangent.reshape(row_count, width)
    grad_attended = (
        jnp.dot(grad_out, w_output, preferred_element_type=jnp.float32)
        .astype(jnp.bfloat16)
        .reshape(seqs, query_rows, head_size)
    )
    grad_activation = jnp.dot(grad_out, w_down, preferred_element_type=jnp.float32)
    grad_hidden = gelu_pull(grad_activation)[0].astype(jnp.bfloat16)
    grad_w_output = left_product(grad_out, attended)
    grad_w_down = left_product(grad_out, activation)
    grad_w_up = left_product(norm_ffn, grad_hidden)
    grad_norm_ffn = right_product(grad_hidden, w_up)
    all_keys, all_values = (
        lax.all_gather(keys, "ctx", axis=1, tiled=True),
        lax.all_gather(values, "ctx", axis=1, tiled=True),
    )
    key_count = all_keys.shape[1]
    key_places = tok_positions(block_order, jnp.arange(key_count, dtype=jnp.int32), half_block)
    visible_all = key_places[None, :] <= row_places[:, None]

    def backward_one(args):
        query_block, key_block, value_block, grad_block, log_block = args
        scores = (
            jnp.einsum("qd,kd->qk", query_block, key_block, preferred_element_type=jnp.float32)
            * scale
        )
        probs = jnp.where(visible_all, jnp.exp(scores - log_block[:, None]), 0.0)
        grad_probs = jnp.einsum(
            "qd,kd->qk", grad_block, value_block, preferred_element_type=jnp.float32
        )
        delta = jnp.sum(probs * grad_probs, axis=1, keepdims=True)
        grad_scores = (probs * (grad_probs - delta)).astype(jnp.bfloat16)
        grad_query = (
            jnp.einsum("qk,kd->qd", grad_scores, key_block, preferred_element_type=jnp.float32)
            * scale
        )
        grad_key = (
            jnp.einsum("qk,qd->kd", grad_scores, query_block, preferred_element_type=jnp.float32)
            * scale
        )
        grad_value = jnp.einsum(
            "qk,qd->kd", probs.astype(jnp.bfloat16), grad_block, preferred_element_type=jnp.float32
        )
        return (grad_query, jnp.concatenate([grad_key, grad_value], axis=1))

    grad_queries, grad_keyvals = lax.map(
        backward_one, (queries, all_keys, all_values, grad_attended, log_total)
    )
    grad_keyvals = lax.psum_scatter(
        grad_keyvals.astype(jnp.bfloat16), "ctx", scatter_dimension=1, tiled=True
    ).astype(jnp.float32)
    grad_keyvals = lax.psum(grad_keyvals.astype(jnp.bfloat16), "tp").astype(jnp.float32)
    grad_key_pre = rotate(grad_keyvals[:, :, None, :head_size], query_places, -1.0)[:, :, 0, :]
    grad_keyval_pre = (
        jnp.concatenate([grad_key_pre, grad_keyvals[:, :, head_size:]], axis=2)
        .astype(jnp.bfloat16)
        .reshape(row_count, 2 * head_size)
    )
    grad_query_pre = (
        rotate(grad_queries.reshape(seqs, span, local_heads, head_size), query_places, -1.0)
        .astype(jnp.bfloat16)
        .reshape(row_count, local_heads * head_size)
    )
    grad_w_query = left_product(norm_attn, grad_query_pre)
    grad_w_keyval = left_product(norm_attn, grad_keyval_pre)
    grad_norm_attn = right_product(grad_query_pre, w_query)
    shared_term = right_product(grad_keyval_pre, w_keyval)
    zero_shift = jnp.zeros((width,), jnp.float32)
    attn_pull = jax.vjp(layer_norm, tokens, gain_attn.astype(jnp.float32), zero_shift)[1]
    ffn_pull = jax.vjp(layer_norm, tokens, gain_ffn.astype(jnp.float32), zero_shift)[1]
    grad_norm_attn, grad_norm_ffn = (
        lax.psum(grad_norm_attn.astype(jnp.bfloat16), "tp").astype(jnp.float32),
        lax.psum(grad_norm_ffn.astype(jnp.bfloat16), "tp").astype(jnp.float32),
    )
    grad_norm_attn = grad_norm_attn + shared_term
    grad_tok_attn, grad_gain_attn, grad_shift_attn = attn_pull(grad_norm_attn)
    grad_tok_ffn, grad_gain_ffn, grad_shift_ffn = ffn_pull(grad_norm_ffn)
    grad_tok_norms = grad_tok_attn + grad_tok_ffn
    grad_tokens = (grad_out.astype(jnp.float32) + grad_tok_norms).reshape(seqs, span, width)
    grads = (
        grad_gain_attn,
        grad_shift_attn,
        grad_gain_ffn,
        grad_shift_ffn,
        grad_w_query,
        grad_w_keyval,
        grad_w_output,
        grad_w_up,
        grad_w_down,
    )
    owned = (
        lax.psum_scatter(
            grads[0].astype(jnp.bfloat16), "shard", scatter_dimension=0, tiled=True
        ).astype(jnp.float32),
        lax.psum_scatter(
            grads[1].astype(jnp.bfloat16), "shard", scatter_dimension=0, tiled=True
        ).astype(jnp.float32),
        lax.psum_scatter(
            grads[2].astype(jnp.bfloat16), "shard", scatter_dimension=0, tiled=True
        ).astype(jnp.float32),
        lax.psum_scatter(
            grads[3].astype(jnp.bfloat16), "shard", scatter_dimension=0, tiled=True
        ).astype(jnp.float32),
        lax.psum_scatter(
            grads[4].astype(jnp.bfloat16), "shard", scatter_dimension=0, tiled=True
        ).astype(jnp.float32),
        lax.psum_scatter(
            grads[5].astype(jnp.bfloat16), "shard", scatter_dimension=0, tiled=True
        ).astype(jnp.float32),
        lax.psum_scatter(
            grads[6].astype(jnp.bfloat16), "shard", scatter_dimension=0, tiled=True
        ).astype(jnp.float32),
        lax.psum_scatter(
            grads[7].astype(jnp.bfloat16), "shard", scatter_dimension=0, tiled=True
        ).astype(jnp.float32),
        lax.psum_scatter(
            grads[8].astype(jnp.bfloat16), "shard", scatter_dimension=0, tiled=True
        ).astype(jnp.float32),
    )
    owned = (
        lax.psum(owned[0].astype(jnp.bfloat16), "ctx").astype(jnp.float32),
        lax.psum(owned[1].astype(jnp.bfloat16), "ctx").astype(jnp.float32),
        lax.psum(owned[2].astype(jnp.bfloat16), "ctx").astype(jnp.float32),
        lax.psum(owned[3].astype(jnp.bfloat16), "ctx").astype(jnp.float32),
        lax.psum(owned[4].astype(jnp.bfloat16), "ctx").astype(jnp.float32),
        lax.psum(owned[5].astype(jnp.bfloat16), "ctx").astype(jnp.float32),
        lax.psum(owned[6].astype(jnp.bfloat16), "ctx").astype(jnp.float32),
        lax.psum(owned[7].astype(jnp.bfloat16), "ctx").astype(jnp.float32),
        lax.psum(owned[8].astype(jnp.bfloat16), "ctx").astype(jnp.float32),
    )
    return (
        mixed,
        keys,
        values,
        grad_tokens,
        owned[0],
        owned[1],
        owned[2],
        owned[3],
        owned[4],
        owned[5],
        owned[6],
        owned[7],
        owned[8],
    )


NY=2
def place(nz):
    s=lax.axis_index("shard"); x=lax.axis_index("ctx")
    return s//NY, s%NY, x

def rcopy(src,dst,ss,rs,dev):
    return pltpu.make_async_remote_copy(src_ref=src,dst_ref=dst,send_sem=ss,recv_sem=rs,device_id=dev,device_id_type=MESH)

class Gather:
    def __init__(self, chunks, rows, nz, sems):
        self.ch=chunks; self.rows=rows; self.nz=nz
        self.zs,self.ys,self.xs,self.zr,self.yr,self.xr=sems
        self.z,self.y,self.x=place(nz)
    def block(self,c,zz,yy):
        return self.ch[c].at[pl.ds(pl.multiple_of((zz*NY+yy)*self.rows,16),self.rows)]
    def half(self,c,zz,yy,h):
        hr=self.rows//2
        return self.ch[c].at[pl.ds(pl.multiple_of((zz*NY+yy)*self.rows+h*hr,16),hr)]
    def up(self,c,zz):
        b=self.block(c,zz,self.y); return rcopy(b,b,self.zs.at[c,0,zz],self.zr.at[c,zz],{"shard":(self.z+1)*NY+self.y})
    def dn(self,c,zz):
        b=self.block(c,zz,self.y); return rcopy(b,b,self.zs.at[c,1,zz],self.zr.at[c,zz],{"shard":(self.z-1)*NY+self.y})
    def ycp(self,c,zz,yy,h):
        b=self.half(c,zz,yy,h); return rcopy(b,b,self.ys.at[c,zz],self.yr.at[c,zz],{"shard":self.z*NY+1-self.y})
    def xcp(self,c,zz,h):
        b=self.half(c,zz,1-self.y,h); return rcopy(b,b,self.xs.at[c,zz],self.xr.at[c,zz],{"ctx":1-self.x})
    def own(self,c):
        z,nz=self.z,self.nz
        @pl.when(z<nz-1)
        def _(): self.up(c,z).start()
        @pl.when(z>0)
        def _(): self.dn(c,z).start()
        self.ycp(c,z,self.y,self.x).start()
    def dirs(self,d):
        z,nz=self.z,self.nz
        return ((z-d>=0, z-d, True),(z+d<nz, z+d, False))
    def Z(self,c,d):
        z,nz=self.z,self.nz
        for ok,zz,isup in self.dirs(d):
            @pl.when(ok)
            def _():
                self.up(c,zz).wait_recv()
                if isup:
                    @pl.when(z<nz-1)
                    def _(): self.up(c,zz).start()
                else:
                    @pl.when(z>0)
                    def _(): self.dn(c,zz).start()
                self.ycp(c,zz,self.y,self.x).start()
    def _each(self,d,f):
        if d==0: f(self.z)
        else:
            for ok,zz,_ in self.dirs(d):
                pl.when(ok)(functools.partial(f,zz))
    def Y(self,c,d):
        def f(zz):
            self.ycp(c,zz,1-self.y,self.x).wait_recv()
            self.xcp(c,zz,self.x).start()
        self._each(d,f)
    def X(self,c,d):
        self._each(d,lambda zz: self.xcp(c,zz,1-self.x).wait_recv())
    def finish(self,c):
        z,nz=self.z,self.nz
        @pl.when(z<nz-1)
        def _(): self.up(c,z).wait_send()
        @pl.when(z>0)
        def _(): self.dn(c,z).wait_send()
        for d in range(1,nz):
            for ok,zz,isup in self.dirs(d):
                if isup: pl.when(jnp.logical_and(ok,z<nz-1))(lambda: self.up(c,zz).wait_send())
                else: pl.when(jnp.logical_and(ok,z>0))(lambda: self.dn(c,zz).wait_send())
        for zz in range(nz):
            self.ycp(c,zz,self.y,self.x).wait_send()
            self.xcp(c,zz,self.x).wait_send()
    @staticmethod
    def sem_shapes(nc,nz):
        D=pltpu.SemaphoreType.DMA
        return [D((nc,2,nz)),D((nc,nz)),D((nc,nz)),D((nc,nz)),D((nc,nz)),D((nc,nz))]

class Scatter:
    def __init__(self, chunks, bufs, rows, nz, sems):
        self.ch=chunks; self.rows=rows; self.nz=nz
        self.xb,self.yb,self.zb,self.fb=bufs
        self.xs,self.ys,self.zs,self.fs,self.xr,self.yr,self.zr,self.fr=sems
        self.z,self.y,self.x=place(nz)
    block=Gather.block; half=Gather.half
    def xcp(self,c,zz):
        return rcopy(self.half(c,zz,1-self.y,1-self.x),self.xb[c].at[zz],self.xs.at[c,zz],self.xr.at[c,zz],{"ctx":1-self.x})
    def ycp(self,c,zz):
        return rcopy(self.half(c,zz,1-self.y,self.x),self.yb[c].at[zz],self.ys.at[c,zz],self.yr.at[c,zz],{"shard":self.z*NY+1-self.y})
    def zcp(self,c,i,zz,src):
        to=self.z+1 if i==0 else self.z-1
        return rcopy(src,self.zb[c].at[i,zz],self.zs.at[c,i,zz],self.zr.at[c,i,zz],{"shard":to*NY+self.y})
    def fcp(self,c):
        return rcopy(self.fb[c].at[0],self.fb[c].at[1],self.fs.at[c],self.fr.at[c],{"ctx":1-self.x})
    def start(self,c):
        for zz in range(self.nz): self.xcp(c,zz).start()
    def X(self,c,zz):
        self.xcp(c,zz).wait_recv()
        h=self.half(c,zz,1-self.y,self.x)
        h[...]=(h[...].astype(F32)+self.xb[c][zz].astype(F32)).astype(BF)
        self.ycp(c,zz).start()
    def Y(self,c,zz):
        z,nz=self.z,self.nz
        self.ycp(c,zz).wait_recv()
        h=self.half(c,zz,self.y,self.x)
        h[...]=(h[...].astype(F32)+self.yb[c][zz].astype(F32)).astype(BF)
        if zz>0: pl.when(z==0)(lambda: self.zcp(c,0,zz,self.block(c,zz,self.y)).start())
        if zz<nz-1: pl.when(z==nz-1)(lambda: self.zcp(c,1,zz,self.block(c,zz,self.y)).start())
    def Z(self,c,k):
        z,nz=self.z,self.nz; zm=nz-1-z
        for i,ok,zz in ((0,jnp.logical_and(z>=1,k>=z),nz-1-k+z),(1,jnp.logical_and(zm>=1,k>=zm),k-zm)):
            @pl.when(ok)
            def _():
                self.zcp(c,i,zz,self.block(c,zz,self.y)).wait_recv()
                @pl.when(zz!=z)
                def _():
                    slot=self.zb[c].at[i,zz]
                    slot[...]=(slot[...].astype(F32)+self.block(c,zz,self.y)[...].astype(F32)).astype(BF)
                    self.zcp(c,i,zz,slot).start()
    def F(self,c):
        z,nz=self.z,self.nz
        own=self.block(c,z,self.y)
        a=own[...].astype(F32)
        u=self.zb[c][0,z].astype(F32); d=self.zb[c][1,z].astype(F32)
        a=a+jnp.where(z>0,u,0.0)+jnp.where(z<nz-1,d,0.0)
        self.fb[c][0]=a.astype(BF)
        self.fcp(c).start()
    def G(self,c):
        self.fcp(c).wait_recv()
        return self.fb[c][0].astype(F32)+self.fb[c][1].astype(F32)
    def finish(self,c):
        z,nz=self.z,self.nz
        for zz in range(nz):
            self.xcp(c,zz).wait_send(); self.ycp(c,zz).wait_send()
            pl.when(jnp.logical_and(z<nz-1,zz>z))(lambda: self.zcp(c,0,zz,self.block(c,zz,self.y)).wait_send())
            pl.when(jnp.logical_and(z>0,zz<z))(lambda: self.zcp(c,1,zz,self.block(c,zz,self.y)).wait_send())
        self.fcp(c).wait_send()
    @staticmethod
    def sem_shapes(nc,nz):
        D=pltpu.SemaphoreType.DMA
        return [D((nc,nz)),D((nc,nz)),D((nc,2,nz)),D((nc,)),D((nc,nz)),D((nc,nz)),D((nc,2,nz)),D((nc,))]

def entry(nz,all_shards,all_ctx=False):
    bar=pltpu.get_barrier_semaphore()
    s=lax.axis_index("shard"); x=lax.axis_index("ctx"); n=nz*NY
    for k in range(1,n):
        pl.semaphore_signal(bar,inc=1,device_id={"shard":lax.rem(s+k,n)},device_id_type=MESH)
        if all_ctx: pl.semaphore_signal(bar,inc=1,device_id={"shard":lax.rem(s+k,n),"ctx":1-x},device_id_type=MESH)
    pl.semaphore_signal(bar,inc=1,device_id={"ctx":1-x},device_id_type=MESH)
    pl.semaphore_wait(bar,n+(n-1 if all_ctx else 0))

def gather_rounds(g,nc,nz):
    for r in range(nc+1):
        if r+2<nc: g.own(r+2)
        for k in range(1,nz):
            if r<nc:
                g.Z(r,k); g.Y(r,k-1)
            if r>0: g.X(r-1,k-1)
            if k==1 and r>0: g.Y(r-1,nz-1)
        if r>0: g.X(r-1,nz-1)

def ag_kernel(nz,nc,rows,fc,ca,lnp,up,dw,q,o,kv,lno,wu,wd,wq,wo,wkv,G,GA,lb,ls,lr,sem0,sem1,*sems):
    s=lax.axis_index("shard"); n=nz*NY
    chunks=[G.at[c] for c in range(nc)]+[GA]
    g=Gather(chunks,rows,nz,sems)
    own=pl.ds(pl.multiple_of(s*rows,16),rows)
    cps=[]
    for c in range(nc):
        cps.append((up.at[:,pl.ds(c*fc,fc)],G.at[c,own,pl.ds(0,fc)]))
        cps.append((dw.at[:,pl.ds(c*fc,fc)],G.at[c,own,pl.ds(fc,fc)]))
    cps+= [(q,GA.at[own,pl.ds(0,ca)]),(o,GA.at[own,pl.ds(ca,ca)]),(kv,GA.at[own,pl.ds(2*ca,kv.shape[1])]),(lnp,lb.at[s])]
    cps=[pltpu.make_async_copy(a,b,sem0.at[i]) for i,(a,b) in enumerate(cps)]
    for c in cps: c.start()
    entry(nz,True)
    for c in cps: c.wait()
    lns=[rcopy(lb.at[s],lb.at[s],ls.at[k-1],lr.at[s],{"shard":lax.rem(s+k,n)}) for k in range(1,n)]
    for c in lns: c.start()
    g.own(0); g.own(1)
    gather_rounds(g,nc+1,nz)
    for k in range(1,n):
        f=lax.rem(s+n-k,n)
        rcopy(lb.at[f],lb.at[f],ls.at[0],lr.at[f],{"shard":f}).wait_recv()
    outs=[]
    for c in range(nc):
        outs.append((G.at[c,:,pl.ds(0,fc)],wu.at[:,pl.ds(c*fc,fc)])); outs.append((G.at[c,:,pl.ds(fc,fc)],wd.at[:,pl.ds(c*fc,fc)]))
    outs+=[(GA.at[:,pl.ds(0,ca)],wq),(GA.at[:,pl.ds(ca,ca)],wo),(GA.at[:,pl.ds(2*ca,wkv.shape[1])],wkv),(lb,lno)]
    outs=[pltpu.make_async_copy(a,b,sem1.at[i]) for i,(a,b) in enumerate(outs)]
    for c in outs: c.start()
    for c in outs: c.wait()
    for c in lns: c.wait_send()
    for c in range(nc+1): g.finish(c)

def ag_call(lnp,up,dw,q,o,kv,nz,nc,cid):
    rows,cu=up.shape; n=nz*NY; ca=q.shape[1]; fc=cu//nc; A=pl.BlockSpec(memory_space=pl.ANY); D=pltpu.SemaphoreType.DMA
    T=n*rows; ck=kv.shape[1]
    sd=lambda *sh:jax.ShapeDtypeStruct(sh,BF)
    return pl.pallas_call(functools.partial(ag_kernel,nz,nc,rows,fc,ca),
        out_shape=(jax.ShapeDtypeStruct((n,)+lnp.shape,lnp.dtype),sd(T,cu),sd(T,cu),sd(T,ca),sd(T,ca),sd(T,ck)),
        in_specs=[A]*6,out_specs=(A,)*6,
        scratch_shapes=[pltpu.VMEM((nc,T,2*fc),BF),pltpu.VMEM((T,2*ca+ck),BF),pltpu.VMEM((n,)+lnp.shape,lnp.dtype),
            D((n-1,)),D((n,)),D((2*nc+4,)),D((2*nc+4,))]+Gather.sem_shapes(nc+1,nz),
        compiler_params=pltpu.CompilerParams(collective_id=cid,has_side_effects=True,vmem_limit_bytes=60<<20),name="gather")(lnp,up,dw,q,o,kv)

def scatter_rounds(r,nc,nz,out):
    for t in range(nc+3):
        if t+2<nc: r.start(t+2)
        for k in range(nz):
            if t<nc: r.X(t,k)
            if 0<=t-1<nc: r.Y(t-1,k)
            if k>0 and 0<=t-2<nc: r.Z(t-2,k)
        if 0<=t-2<nc: r.F(t-2)
        if 0<=t-3<nc: out(t-3,r.G(t-3))

def rs_kernel(nz,nc,rows,fc,ca,lng,gu,gd,gq,go,gkv,lno,ou,od,oq,oo,okv,*scr):
    G,GA=scr[:2]; xb=scr[2:4]; yb=scr[4:6]; zb=scr[6:8]; fb=scr[8:10]; lb,ls,lr,sem0=scr[10:14]; sems=scr[14:]
    s=lax.axis_index("shard"); x=lax.axis_index("ctx"); n=nz*NY; ck=gkv.shape[1]
    chunks=[G.at[c] for c in range(nc)]+[GA]
    bufs=[[b[0].at[c] for c in range(nc)]+[b[1]] for b in (xb,yb,zb,fb)]
    r=Scatter(chunks,bufs,rows,nz,sems)
    cps=[]
    for c in range(nc):
        cps.append((gu.at[:,pl.ds(c*fc,fc)],G.at[c,:,pl.ds(0,fc)]))
        cps.append((gd.at[:,pl.ds(c*fc,fc)],G.at[c,:,pl.ds(fc,fc)]))
    cps+= [(gq,GA.at[:,pl.ds(0,ca)]),(go,GA.at[:,pl.ds(ca,ca)]),(gkv,GA.at[:,pl.ds(2*ca,ck)])]
    cps=[pltpu.make_async_copy(a,b,sem0.at[i]) for i,(a,b) in enumerate(cps)]
    for c in cps: c.start()
    entry(nz,True,True)
    me=x*n+s
    peers=[(s,1-x)]+[(lax.rem(s+k,n),xx) for k in range(1,n) for xx in (x,1-x)]
    lns=[rcopy(lng.at[ps],lb.at[me],ls.at[i],lr.at[me],{"shard":ps,"ctx":px}) for i,(ps,px) in enumerate(peers)]
    for c in lns: c.start()
    for c in cps: c.wait()
    r.start(0); r.start(1)
    def out(c,v):
        if c<nc:
            ou[:,c*fc:(c+1)*fc]=v[:,:fc]; od[:,c*fc:(c+1)*fc]=v[:,fc:]
        else:
            oq[...]=v[:,:ca]; oo[...]=v[:,ca:2*ca]; okv[...]=v[:,2*ca:]
    scatter_rounds(r,nc+1,nz,out)
    for i,(ps,px) in enumerate(peers):
        rcopy(lng.at[ps],lb.at[px*n+ps],ls.at[i],lr.at[px*n+ps],{"shard":ps,"ctx":px}).wait_recv()
    pltpu.sync_copy(lng.at[s],lb.at[me])
    t=lb[0]
    for i in range(1,2*n): t=t+lb[i]
    lno[...]=t
    for c in lns: c.wait_send()
    for c in range(nc+1): r.finish(c)

def rs_call(lng,gu,gd,gq,go,gkv,nz,nc,cid):
    T,cu=gu.shape; n=nz*NY; rows=T//n; ca=gq.shape[1]; ck=gkv.shape[1]; fc=cu//nc
    A=pl.BlockSpec(memory_space=pl.ANY); V=pl.BlockSpec(memory_space=pltpu.VMEM); D=pltpu.SemaphoreType.DMA
    cf,cA=2*fc,2*ca+ck; hr=rows//2
    sd=lambda *sh:jax.ShapeDtypeStruct(sh,F32)
    vm=lambda *sh:pltpu.VMEM(sh,BF)
    return pl.pallas_call(functools.partial(rs_kernel,nz,nc,rows,fc,ca),
        out_shape=(sd(*lng.shape[1:]),sd(rows,cu),sd(rows,cu),sd(rows,ca),sd(rows,ca),sd(rows,ck)),
        in_specs=[A]*6,out_specs=(V,)*6,
        scratch_shapes=[vm(nc,T,cf),vm(T,cA),vm(nc,nz,hr,cf),vm(nz,hr,cA),vm(nc,nz,hr,cf),vm(nz,hr,cA),
            vm(nc,2,nz,rows,cf),vm(2,nz,rows,cA),vm(nc,2,rows,cf),vm(2,rows,cA),
            pltpu.VMEM((2*n,)+lng.shape[1:],F32),D((2*n-1,)),D((2*n,)),D((2*nc+3,))]+Scatter.sem_shapes(nc+1,nz),
        compiler_params=pltpu.CompilerParams(collective_id=cid,has_side_effects=True,vmem_limit_bytes=60<<20),name="scatter")(lng,gu,gd,gq,go,gkv)

NEG=-1e30
def dot_nt(a,b): return lax.dot_general(a,b,(((1,),(1,)),((),())),preferred_element_type=F32)
def dot(a,b): return lax.dot_general(a,b,(((1,),(0,)),((),())),preferred_element_type=F32)

def attn_step(step, half, npair, qx, dox, qt, dot_, kx, k0, v0, att, dq, dkt, dvt, s_scr, dp_scr, p_scr, ds_scr, BQ, BK):
    tile = step // npair
    sub = half // BQ
    own = tile // sub
    r0 = (tile % sub) * BQ
    nk = kx.shape[0]//BK
    offs=[]
    per = half//BK
    for j in range(nk):
        if j < per: o = own*half + j*BK
        elif j < 2*per: o = (1-own)*half + (j-per)*BK
        else: o = j*BK
        offs.append(pl.multiple_of(o,BK) if not isinstance(o,int) else o)
    q = qx[step]; do = dox[step]
    m = None
    R = q.shape[0]
    for j in range(nk):
        s = dot_nt(q, kx[pl.ds(offs[j],BK),:])
        if j < per:
            row = lax.broadcasted_iota(jnp.int32,(R,BK),0) % BQ + r0
            col = lax.broadcasted_iota(jnp.int32,(R,BK),1) + j*BK
            s = jnp.where(col<=row, s, NEG)
        s_scr[:, j*BK:(j+1)*BK] = s
        mj = s[:, :128]
        for t in range(1,BK//128): mj = jnp.maximum(mj, s[:, t*128:(t+1)*128])
        m = mj if m is None else jnp.maximum(m,mj)
    m = jnp.max(m,axis=1,keepdims=True)
    l = None; o = None
    for j in range(nk):
        p = jnp.exp(s_scr[:, j*BK:(j+1)*BK]-m)
        s_scr[:, j*BK:(j+1)*BK] = p
        lj = p[:, :128]
        for t in range(1,BK//128): lj = lj + p[:, t*128:(t+1)*128]
        l = lj if l is None else l+lj
        pb = p.astype(BF)
        p_scr[:, j*BK:(j+1)*BK] = pb
        oj = dot(pb, v0[pl.ds(offs[j],BK),:])
        o = oj if o is None else o+oj
    l = jnp.sum(l,axis=1,keepdims=True)
    inv = 1.0/l
    o = o*inv
    delta = jnp.sum(o*do.astype(F32),axis=1,keepdims=True)
    dqa = None
    inv_row = jnp.transpose(jnp.broadcast_to(inv,(R,128)))[:1,:]
    qs = (qt[step].astype(F32)*inv_row).astype(BF)
    dos = (dot_[step].astype(F32)*inv_row).astype(BF)
    for j in range(nk):
        dp = dot_nt(do, v0[pl.ds(offs[j],BK),:])
        ds = (s_scr[:, j*BK:(j+1)*BK]*(dp-delta)).astype(BF)
        dj = dot(ds, k0[pl.ds(offs[j],BK),:])
        dqa = dj if dqa is None else dqa+dj
        dkt[:, pl.ds(offs[j],BK)] += dot(qs, ds)
        dvt[:, pl.ds(offs[j],BK)] += dot(dos, p_scr[:, j*BK:(j+1)*BK])
    dqa = dqa*(inv*0.125)
    def pairup(x):
        return x[:BQ] + pltpu.roll(x[BQ:],64,1)
    att[step] = pairup(o).astype(att.dtype)
    dq[step] = pairup(dqa)

def attn_kernel(half, npair, BQ, BK, qx, dox, qt, dot_, kx, k0, v0, att, dq, dkt, dvt, s_scr, dp_scr, p_scr, ds_scr):
    dkt[...] = jnp.zeros_like(dkt); dvt[...] = jnp.zeros_like(dvt)
    @pl.loop(0, qx.shape[0])
    def _(step):
        attn_step(step, half, npair, qx, dox, qt, dot_, kx, k0, v0, att, dq, dkt, dvt, s_scr, dp_scr, p_scr, ds_scr, BQ, BK)

def attn_call(qx, dox, qt, dot_, kx, k0, v0, half, npair, BQ, BK, name="attn"):
    ns=qx.shape[0]; nk=kx.shape[0]; R=qx.shape[1]
    V=pl.BlockSpec(memory_space=pltpu.VMEM)
    return pl.pallas_call(functools.partial(attn_kernel,half,npair,BQ,BK),
      out_shape=(jax.ShapeDtypeStruct((ns,R//2,128),BF),jax.ShapeDtypeStruct((ns,R//2,128),F32),
                 jax.ShapeDtypeStruct((64,nk),F32),jax.ShapeDtypeStruct((64,nk),F32)),
      in_specs=[V]*7,out_specs=(V,)*4,
      scratch_shapes=[pltpu.VMEM((R,nk),F32),pltpu.VMEM((8,128),F32),pltpu.VMEM((R,nk),BF),pltpu.VMEM((8,128),BF)],
      compiler_params=pltpu.CompilerParams(vmem_limit_bytes=60<<20),name=name)(qx,dox,qt,dot_,kx,k0,v0)

def fits(mesh):
    return mesh.shape["shard"] == 8 and mesh.shape["ctx"] == 2


def fast_device(hidden, block_order, ln1_gain, ln1_bias, ln2_gain, ln2_bias, q_weight, kv_weight, o_weight, up_weight, down_weight, cotangent):
    seqs, span, width = hidden.shape
    half = span // 2
    hd = kv_weight.shape[1] // 2
    heads = q_weight.shape[1] // hd
    npair = heads // 2
    BQ = 256
    nt = span // BQ
    ns = nt * npair
    x = lax.axis_index("ctx")
    rows = ln1_gain.shape[0]
    n = width // rows
    nz = n // NY
    lnp = jnp.pad(jnp.stack([ln1_gain, ln1_bias, ln2_gain, ln2_bias]).astype(F32), ((0, 4), (0, 128 - rows)))
    lno, w_up, w_down, w_query, w_output, w_keyval = ag_call(lnp, up_weight, down_weight, q_weight, o_weight, kv_weight, nz, 4, 1)
    params = lno[:, :4, :rows].transpose(1, 0, 2).reshape(4, width)
    gain_attn, bias_attn, gain_ffn, bias_ffn = params[0], params[1], params[2], params[3]
    tokens = hidden.astype(F32).reshape(span, width)
    cot = cotangent.reshape(span, width)
    norm_attn = layer_norm(tokens, gain_attn, bias_attn).astype(BF)
    norm_ffn = layer_norm(tokens, gain_ffn, bias_ffn).astype(BF)
    places = tok_positions(block_order, x * span + jnp.arange(span, dtype=jnp.int32), half)
    query_pre = jnp.dot(norm_attn, w_query, preferred_element_type=F32).reshape(span, heads, hd)
    queries = rotate(query_pre, places, 1.0).astype(BF)
    keyval_pre = jnp.dot(norm_attn, w_keyval, preferred_element_type=F32)
    keys = rotate(keyval_pre[:, None, :hd], places, 1.0)[:, 0].astype(BF)
    values = keyval_pre[:, hd:].astype(BF)
    kv = jnp.concatenate([keys, values], axis=1)
    kv_other = lax.ppermute(kv, "ctx", [(0, 1), (1, 0)])
    kvs = jnp.concatenate([kv, kv_other], axis=0)
    grad_att = jnp.dot(cot, w_output, preferred_element_type=F32).astype(BF).reshape(span, heads, hd)

    def stepmajor(a):
        return a.reshape(nt, BQ, npair, 2, hd).transpose(0, 2, 3, 1, 4).reshape(ns, 2 * BQ, hd)

    own = lax.dynamic_slice(block_order, (2 * x,), (2,))
    oth = lax.dynamic_slice(block_order, (2 * (1 - x),), (2,))
    order = jnp.concatenate([own, oth])
    hide = jnp.where(order[None, :] <= own[:, None], 0.0, NEG)
    blk = (jnp.arange(ns) // npair) * BQ // half
    lanes = jnp.pad(hide[blk], ((0, 0), (0, hd - 4))).astype(BF)
    qs = stepmajor(queries * jnp.asarray(hd**-0.5, BF))
    ds = stepmajor(grad_att)
    qx = jnp.concatenate([qs, jnp.broadcast_to(lanes[:, None, :], (ns, 2 * BQ, hd))], axis=-1)
    dox = jnp.concatenate([ds, jnp.zeros_like(ds)], axis=-1)
    nk = kvs.shape[0]
    hot = (jnp.arange(nk)[:, None] // half == jnp.arange(hd)[None, :]).astype(BF)
    zero = jnp.zeros((nk, hd), BF)
    kk, vv = kvs[:, :hd], kvs[:, hd:]
    att, dq, dkt, dvt = attn_call(qx, dox, qs.transpose(0, 2, 1), ds.transpose(0, 2, 1), jnp.concatenate([kk, hot], -1), jnp.concatenate([kk, zero], -1), jnp.concatenate([vv, zero], -1), half, npair, BQ, 512)

    def unstep(a):
        return a.reshape(nt, npair, BQ, 2, hd).transpose(0, 2, 1, 3, 4).reshape(span, heads, hd)

    attended = unstep(att).reshape(span, heads * hd)
    hidden_pre = jnp.dot(norm_ffn, w_up, preferred_element_type=F32)
    activation_full, gelu_pull = jax.vjp(gelu_exact, hidden_pre)
    activation = activation_full.astype(BF)
    branch = right_product(attended, w_output) + right_product(activation, w_down)
    branch = lax.psum(branch.astype(BF), "tp").astype(F32)
    mixed = (tokens + branch).astype(BF).reshape(seqs, span, width)
    grad_activation = jnp.dot(cot, w_down, preferred_element_type=F32)
    grad_hidden = gelu_pull(grad_activation)[0].astype(BF)
    gwo = left_product(cot, attended)
    gwd = left_product(cot, activation)
    gwu = left_product(norm_ffn, grad_hidden)
    gnf = right_product(grad_hidden, w_up)
    gkv = jnp.concatenate([dkt, dvt], axis=0).T.astype(BF)
    gkv = lax.psum(gkv.astype(F32), "tp").astype(BF)
    gkv_mine = gkv[:span].astype(F32) + lax.ppermute(gkv[span:], "ctx", [(0, 1), (1, 0)]).astype(F32)
    gk = rotate(gkv_mine[:, None, :hd], places, -1.0)[:, 0]
    gkv_pre = jnp.concatenate([gk, gkv_mine[:, hd:]], axis=1).astype(BF)
    gq_pre = rotate(unstep(dq), places, -1.0).astype(BF).reshape(span, heads * hd)
    gwq = left_product(norm_attn, gq_pre)
    gwkv = left_product(norm_attn, gkv_pre)
    gna = right_product(gq_pre, w_query)
    shared = right_product(gkv_pre, w_keyval)
    zero_shift = jnp.zeros((width,), F32)
    attn_pull = jax.vjp(layer_norm, tokens, gain_attn, zero_shift)[1]
    ffn_pull = jax.vjp(layer_norm, tokens, gain_ffn, zero_shift)[1]
    gna = lax.psum(gna.astype(BF), "tp").astype(F32) + shared
    gnf = lax.psum(gnf.astype(BF), "tp").astype(F32)
    gta, gga, gsa = attn_pull(gna)
    gtf, ggf, gsf = ffn_pull(gnf)
    grad_tokens = (cot.astype(F32) + gta + gtf).reshape(seqs, span, width)
    lng = jnp.pad(jnp.stack([gga, gsa, ggf, gsf]).reshape(4, n, rows).transpose(1, 0, 2), ((0, 0), (0, 4), (0, 128 - rows)))
    bf = lambda a: a.astype(BF)
    lo, ou, od, oq, oo, okv = rs_call(lng, bf(gwu), bf(gwd), bf(gwq), bf(gwo), bf(gwkv), nz, 4, 2)
    return (mixed, keys.reshape(seqs, span, hd), values.reshape(seqs, span, hd), grad_tokens, lo[0, :rows], lo[1, :rows], lo[2, :rows], lo[3, :rows], oq, okv, oo, ou, od)


def solution(mesh):
    return jax.shard_map(
        fast_device if fits(mesh) else on_device,
        mesh=mesh,
        in_specs=(
            P("shard", "ctx", None),
            P(),
            P("shard"),
            P("shard"),
            P("shard"),
            P("shard"),
            P("shard", "tp"),
            P("shard", None),
            P("shard", "tp"),
            P("shard", "tp"),
            P("shard", "tp"),
            P("shard", "ctx", None),
        ),
        out_specs=(
            P("shard", "ctx", None),
            P("shard", "ctx", None),
            P("shard", "ctx", None),
            P("shard", "ctx", None),
            P("shard"),
            P("shard"),
            P("shard"),
            P("shard"),
            P("shard", "tp"),
            P("shard", None),
            P("shard", "tp"),
            P("shard", "tp"),
            P("shard", "tp"),
        ),
        check_vma=False,
    )
```

```python
import functools
import types

import jax
import jax.numpy as jnp
import numpy as np
from jax import lax
from jax.experimental import pallas as pl
from jax.experimental.pallas import tpu as pltpu
from jax.sharding import PartitionSpec as P

F32 = jnp.float32
BF = jnp.bfloat16
MESH = pl.DeviceIdType.MESH

ROT = 16


def layer_norm(values, gain, shift):
    center = values - jnp.mean(values, axis=-1, keepdims=True)
    spread = jnp.mean(center * center, axis=-1, keepdims=True)
    return center * lax.rsqrt(spread + 1e-05) * gain + shift


def gelu_exact(values):
    return jax.nn.gelu(values, approximate=False)


def rotate(tensor, places, sign):
    half_rot = ROT // 2
    freq = jnp.power(10000.0, -2.0 * jnp.arange(half_rot, dtype=jnp.float32) / ROT)
    angle = places.astype(jnp.float32)[:, None] * freq[None, :]
    cosine = jnp.cos(angle)[:, None, :]
    sine = sign * jnp.sin(angle)[:, None, :]
    first = tensor[..., :half_rot]
    second = tensor[..., half_rot:ROT]
    return jnp.concatenate(
        [first * cosine - second * sine, second * cosine + first * sine, tensor[..., ROT:]], axis=-1
    )


def tok_positions(block_order, rows, half_block):
    index = rows // half_block
    table = jnp.arange(block_order.shape[0], dtype=jnp.int32)
    picked = jnp.sum(jnp.where(index[:, None] == table[None, :], block_order[None, :], 0), axis=1)
    return picked * half_block + rows % half_block


def right_product(left, right):
    return lax.dot_general(
        left, right, (((1,), (1,)), ((), ())), preferred_element_type=jnp.float32
    )


def left_product(left, right):
    return lax.dot_general(
        left, right, (((0,), (0,)), ((), ())), preferred_element_type=jnp.float32
    )


def on_device(
    hidden,
    block_order,
    ln1_gain,
    ln1_bias,
    ln2_gain,
    ln2_bias,
    q_weight,
    kv_weight,
    o_weight,
    up_weight,
    down_weight,
    cotangent,
):
    seqs, span, width = hidden.shape
    half_block = span // 2
    head_size = kv_weight.shape[1] // 2
    local_heads = q_weight.shape[1] // head_size
    row_count = seqs * span
    query_rows = span * local_heads
    scale = head_size ** (-0.5)
    gathered = (
        lax.all_gather(ln1_gain, "shard", axis=0, tiled=True),
        lax.all_gather(ln1_bias, "shard", axis=0, tiled=True),
        lax.all_gather(ln2_gain, "shard", axis=0, tiled=True),
        lax.all_gather(ln2_bias, "shard", axis=0, tiled=True),
        lax.all_gather(q_weight, "shard", axis=0, tiled=True),
        lax.all_gather(kv_weight, "shard", axis=0, tiled=True),
        lax.all_gather(o_weight, "shard", axis=0, tiled=True),
        lax.all_gather(up_weight, "shard", axis=0, tiled=True),
        lax.all_gather(down_weight, "shard", axis=0, tiled=True),
    )
    gain_attn, bias_attn, gain_ffn, bias_ffn, w_query, w_keyval, w_output, w_up, w_down = gathered
    offset = lax.axis_index("ctx") * span
    query_places = tok_positions(
        block_order, offset + jnp.arange(span, dtype=jnp.int32), half_block
    )
    row_places = jnp.repeat(query_places, local_heads)
    tokens = hidden.astype(jnp.float32).reshape(row_count, width)
    norm_attn = layer_norm(
        tokens, gain_attn.astype(jnp.float32), bias_attn.astype(jnp.float32)
    ).astype(jnp.bfloat16)
    norm_ffn = layer_norm(
        tokens, gain_ffn.astype(jnp.float32), bias_ffn.astype(jnp.float32)
    ).astype(jnp.bfloat16)
    query_pre = jnp.dot(norm_attn, w_query, preferred_element_type=jnp.float32).reshape(
        seqs, span, local_heads, head_size
    )
    queries = (
        rotate(query_pre, query_places, 1.0)
        .astype(jnp.bfloat16)
        .reshape(seqs, query_rows, head_size)
    )
    keyval_pre = jnp.dot(norm_attn, w_keyval, preferred_element_type=jnp.float32).reshape(
        seqs, span, 2 * head_size
    )
    keys = rotate(keyval_pre[:, :, None, :head_size], query_places, 1.0)[:, :, 0, :].astype(
        jnp.bfloat16
    )
    values = keyval_pre[:, :, head_size:].astype(jnp.bfloat16)
    start_state = (
        jnp.full((seqs, query_rows), -1e30, jnp.float32),
        jnp.zeros((seqs, query_rows), jnp.float32),
        jnp.zeros((seqs, query_rows, head_size), jnp.float32),
    )
    key_piece = lax.all_gather(keys, "ctx", axis=1, tiled=True)
    value_piece = lax.all_gather(values, "ctx", axis=1, tiled=True)
    count = key_piece.shape[1]
    key_places = tok_positions(block_order, jnp.arange(count, dtype=jnp.int32), half_block)
    visible = key_places[None, :] <= row_places[:, None]

    def one_block(args):
        peak, total, accum, query_block, key_block, value_block = args
        scores = (
            jnp.einsum("qd,kd->qk", query_block, key_block, preferred_element_type=jnp.float32)
            * scale
        )
        scores = jnp.where(visible, scores, -1e30)
        new_peak = jnp.maximum(peak, jnp.max(scores, axis=1))
        factor = jnp.exp(peak - new_peak)
        weights = jnp.where(visible, jnp.exp(scores - new_peak[:, None]), 0.0)
        total = total * factor + jnp.sum(weights, axis=1)
        accum = accum * factor[:, None] + jnp.einsum(
            "qk,kd->qd",
            weights.astype(jnp.bfloat16),
            value_block,
            preferred_element_type=jnp.float32,
        )
        return (new_peak, total, accum)

    peak, total, accum = lax.map(
        one_block, (start_state[0], start_state[1], start_state[2], queries, key_piece, value_piece)
    )
    attended = (
        (accum / total[:, :, None]).astype(jnp.bfloat16).reshape(row_count, local_heads * head_size)
    )
    log_total = peak + jnp.log(total)
    hidden_pre = jnp.dot(norm_ffn, w_up, preferred_element_type=jnp.float32)
    activation_full, gelu_pull = jax.vjp(gelu_exact, hidden_pre)
    activation = activation_full.astype(jnp.bfloat16)
    branch = right_product(attended, w_output) + right_product(activation, w_down)
    branch = lax.psum(branch.astype(jnp.bfloat16), "tp").astype(jnp.float32)
    mixed = (tokens + branch).astype(jnp.bfloat16).reshape(seqs, span, width)
    regathered = (
        lax.all_gather(ln1_gain, "shard", axis=0, tiled=True),
        lax.all_gather(ln2_gain, "shard", axis=0, tiled=True),
        lax.all_gather(q_weight, "shard", axis=0, tiled=True),
        lax.all_gather(kv_weight, "shard", axis=0, tiled=True),
        lax.all_gather(o_weight, "shard", axis=0, tiled=True),
        lax.all_gather(up_weight, "shard", axis=0, tiled=True),
        lax.all_gather(down_weight, "shard", axis=0, tiled=True),
    )
    gain_attn, gain_ffn, w_query, w_keyval, w_output, w_up, w_down = regathered
    grad_out = cotangent.reshape(row_count, width)
    grad_attended = (
        jnp.dot(grad_out, w_output, preferred_element_type=jnp.float32)
        .astype(jnp.bfloat16)
        .reshape(seqs, query_rows, head_size)
    )
    grad_activation = jnp.dot(grad_out, w_down, preferred_element_type=jnp.float32)
    grad_hidden = gelu_pull(grad_activation)[0].astype(jnp.bfloat16)
    grad_w_output = left_product(grad_out, attended)
    grad_w_down = left_product(grad_out, activation)
    grad_w_up = left_product(norm_ffn, grad_hidden)
    grad_norm_ffn = right_product(grad_hidden, w_up)
    all_keys, all_values = (
        lax.all_gather(keys, "ctx", axis=1, tiled=True),
        lax.all_gather(values, "ctx", axis=1, tiled=True),
    )
    key_count = all_keys.shape[1]
    key_places = tok_positions(block_order, jnp.arange(key_count, dtype=jnp.int32), half_block)
    visible_all = key_places[None, :] <= row_places[:, None]

    def backward_one(args):
        query_block, key_block, value_block, grad_block, log_block = args
        scores = (
            jnp.einsum("qd,kd->qk", query_block, key_block, preferred_element_type=jnp.float32)
            * scale
        )
        probs = jnp.where(visible_all, jnp.exp(scores - log_block[:, None]), 0.0)
        grad_probs = jnp.einsum(
            "qd,kd->qk", grad_block, value_block, preferred_element_type=jnp.float32
        )
        delta = jnp.sum(probs * grad_probs, axis=1, keepdims=True)
        grad_scores = (probs * (grad_probs - delta)).astype(jnp.bfloat16)
        grad_query = (
            jnp.einsum("qk,kd->qd", grad_scores, key_block, preferred_element_type=jnp.float32)
            * scale
        )
        grad_key = (
            jnp.einsum("qk,qd->kd", grad_scores, query_block, preferred_element_type=jnp.float32)
            * scale
        )
        grad_value = jnp.einsum(
            "qk,qd->kd", probs.astype(jnp.bfloat16), grad_block, preferred_element_type=jnp.float32
        )
        return (grad_query, jnp.concatenate([grad_key, grad_value], axis=1))

    grad_queries, grad_keyvals = lax.map(
        backward_one, (queries, all_keys, all_values, grad_attended, log_total)
    )
    grad_keyvals = lax.psum_scatter(
        grad_keyvals.astype(jnp.bfloat16), "ctx", scatter_dimension=1, tiled=True
    ).astype(jnp.float32)
    grad_keyvals = lax.psum(grad_keyvals.astype(jnp.bfloat16), "tp").astype(jnp.float32)
    grad_key_pre = rotate(grad_keyvals[:, :, None, :head_size], query_places, -1.0)[:, :, 0, :]
    grad_keyval_pre = (
        jnp.concatenate([grad_key_pre, grad_keyvals[:, :, head_size:]], axis=2)
        .astype(jnp.bfloat16)
        .reshape(row_count, 2 * head_size)
    )
    grad_query_pre = (
        rotate(grad_queries.reshape(seqs, span, local_heads, head_size), query_places, -1.0)
        .astype(jnp.bfloat16)
        .reshape(row_count, local_heads * head_size)
    )
    grad_w_query = left_product(norm_attn, grad_query_pre)
    grad_w_keyval = left_product(norm_attn, grad_keyval_pre)
    grad_norm_attn = right_product(grad_query_pre, w_query)
    shared_term = right_product(grad_keyval_pre, w_keyval)
    zero_shift = jnp.zeros((width,), jnp.float32)
    attn_pull = jax.vjp(layer_norm, tokens, gain_attn.astype(jnp.float32), zero_shift)[1]
    ffn_pull = jax.vjp(layer_norm, tokens, gain_ffn.astype(jnp.float32), zero_shift)[1]
    grad_norm_attn, grad_norm_ffn = (
        lax.psum(grad_norm_attn.astype(jnp.bfloat16), "tp").astype(jnp.float32),
        lax.psum(grad_norm_ffn.astype(jnp.bfloat16), "tp").astype(jnp.float32),
    )
    grad_norm_attn = grad_norm_attn + shared_term
    grad_tok_attn, grad_gain_attn, grad_shift_attn = attn_pull(grad_norm_attn)
    grad_tok_ffn, grad_gain_ffn, grad_shift_ffn = ffn_pull(grad_norm_ffn)
    grad_tok_norms = grad_tok_attn + grad_tok_ffn
    grad_tokens = (grad_out.astype(jnp.float32) + grad_tok_norms).reshape(seqs, span, width)
    grads = (
        grad_gain_attn,
        grad_shift_attn,
        grad_gain_ffn,
        grad_shift_ffn,
        grad_w_query,
        grad_w_keyval,
        grad_w_output,
        grad_w_up,
        grad_w_down,
    )
    owned = (
        lax.psum_scatter(
            grads[0].astype(jnp.bfloat16), "shard", scatter_dimension=0, tiled=True
        ).astype(jnp.float32),
        lax.psum_scatter(
            grads[1].astype(jnp.bfloat16), "shard", scatter_dimension=0, tiled=True
        ).astype(jnp.float32),
        lax.psum_scatter(
            grads[2].astype(jnp.bfloat16), "shard", scatter_dimension=0, tiled=True
        ).astype(jnp.float32),
        lax.psum_scatter(
            grads[3].astype(jnp.bfloat16), "shard", scatter_dimension=0, tiled=True
        ).astype(jnp.float32),
        lax.psum_scatter(
            grads[4].astype(jnp.bfloat16), "shard", scatter_dimension=0, tiled=True
        ).astype(jnp.float32),
        lax.psum_scatter(
            grads[5].astype(jnp.bfloat16), "shard", scatter_dimension=0, tiled=True
        ).astype(jnp.float32),
        lax.psum_scatter(
            grads[6].astype(jnp.bfloat16), "shard", scatter_dimension=0, tiled=True
        ).astype(jnp.float32),
        lax.psum_scatter(
            grads[7].astype(jnp.bfloat16), "shard", scatter_dimension=0, tiled=True
        ).astype(jnp.float32),
        lax.psum_scatter(
            grads[8].astype(jnp.bfloat16), "shard", scatter_dimension=0, tiled=True
        ).astype(jnp.float32),
    )
    owned = (
        lax.psum(owned[0].astype(jnp.bfloat16), "ctx").astype(jnp.float32),
        lax.psum(owned[1].astype(jnp.bfloat16), "ctx").astype(jnp.float32),
        lax.psum(owned[2].astype(jnp.bfloat16), "ctx").astype(jnp.float32),
        lax.psum(owned[3].astype(jnp.bfloat16), "ctx").astype(jnp.float32),
        lax.psum(owned[4].astype(jnp.bfloat16), "ctx").astype(jnp.float32),
        lax.psum(owned[5].astype(jnp.bfloat16), "ctx").astype(jnp.float32),
        lax.psum(owned[6].astype(jnp.bfloat16), "ctx").astype(jnp.float32),
        lax.psum(owned[7].astype(jnp.bfloat16), "ctx").astype(jnp.float32),
        lax.psum(owned[8].astype(jnp.bfloat16), "ctx").astype(jnp.float32),
    )
    return (
        mixed,
        keys,
        values,
        grad_tokens,
        owned[0],
        owned[1],
        owned[2],
        owned[3],
        owned[4],
        owned[5],
        owned[6],
        owned[7],
        owned[8],
    )


NY = 2
NEG = -1e30


def rcopy(src, dst, ss, rs, dev):
    return pltpu.make_async_remote_copy(src_ref=src, dst_ref=dst, send_sem=ss, recv_sem=rs, device_id=dev, device_id_type=MESH)


def dot_nt(a, b):
    return lax.dot_general(a, b, (((1,), (1,)), ((), ())), preferred_element_type=F32)


def dot(a, b):
    return lax.dot_general(a, b, (((1,), (0,)), ((), ())), preferred_element_type=F32)


def both(a, b):
    return jnp.logical_and(a, b)


class Gather:
    def __init__(self, ref, rows, nz, sems):
        self.ref, self.rows, self.nz = ref, rows, nz
        self.zs, self.ys, self.xs, self.zr, self.yr, self.xr = sems
        s = lax.axis_index("shard")
        self.z, self.y, self.x = s // NY, s % NY, lax.axis_index("ctx")

    def block(self, c, zz, yy):
        return self.ref.at[c, pl.ds(pl.multiple_of((zz * NY + yy) * self.rows, 16), self.rows)]

    def half(self, c, zz, yy, h):
        hr = self.rows // 2
        return self.ref.at[c, pl.ds(pl.multiple_of((zz * NY + yy) * self.rows + h * hr, 16), hr)]

    def up(self, c, zz):
        b = self.block(c, zz, self.y)
        return rcopy(b, b, self.zs.at[c, 0, zz], self.zr.at[c, zz], {"shard": (self.z + 1) * NY + self.y})

    def dn(self, c, zz):
        b = self.block(c, zz, self.y)
        return rcopy(b, b, self.zs.at[c, 1, zz], self.zr.at[c, zz], {"shard": (self.z - 1) * NY + self.y})

    def ycp(self, c, zz, yy, h):
        b = self.half(c, zz, yy, h)
        return rcopy(b, b, self.ys.at[c, zz], self.yr.at[c, zz], {"shard": self.z * NY + 1 - self.y})

    def xcp(self, c, zz, h):
        b = self.half(c, zz, 1 - self.y, h)
        return rcopy(b, b, self.xs.at[c, zz], self.xr.at[c, zz], {"ctx": 1 - self.x})

    def own(self, c):
        z, nz = self.z, self.nz

        @pl.when(z < nz - 1)
        def _():
            self.up(c, z).start()

        @pl.when(z > 0)
        def _():
            self.dn(c, z).start()

        self.ycp(c, z, self.y, self.x).start()

    def dirs(self, d):
        return ((self.z - d >= 0, self.z - d, True), (self.z + d < self.nz, self.z + d, False))

    def Z(self, c, d):
        z, nz = self.z, self.nz
        for ok, zz, isup in self.dirs(d):

            @pl.when(ok)
            def _():
                self.up(c, zz).wait_recv()
                if isup:
                    pl.when(z < nz - 1)(lambda: self.up(c, zz).start())
                else:
                    pl.when(z > 0)(lambda: self.dn(c, zz).start())
                self.ycp(c, zz, self.y, self.x).start()

    def each(self, d, f):
        if d == 0:
            f(self.z)
        else:
            for ok, zz, _ in self.dirs(d):
                pl.when(ok)(functools.partial(f, zz))

    def Y(self, c, d):
        def f(zz):
            self.ycp(c, zz, 1 - self.y, self.x).wait_recv()
            self.xcp(c, zz, self.x).start()

        self.each(d, f)

    def X(self, c, d):
        self.each(d, lambda zz: self.xcp(c, zz, 1 - self.x).wait_recv())

    def finish(self, c):
        z, nz = self.z, self.nz
        pl.when(z < nz - 1)(lambda: self.up(c, z).wait_send())
        pl.when(z > 0)(lambda: self.dn(c, z).wait_send())
        for d in range(1, nz):
            for ok, zz, isup in self.dirs(d):
                if isup:
                    pl.when(both(ok, z < nz - 1))(lambda: self.up(c, zz).wait_send())
                else:
                    pl.when(both(ok, z > 0))(lambda: self.dn(c, zz).wait_send())
        for zz in range(nz):
            self.ycp(c, zz, self.y, self.x).wait_send()
            self.xcp(c, zz, self.x).wait_send()

    @staticmethod
    def sems(nc, nz):
        D = pltpu.SemaphoreType.DMA
        return [D((nc, 2, nz)), D((nc, nz)), D((nc, nz)), D((nc, nz)), D((nc, nz)), D((nc, nz))]


class Scatter:
    block, half = Gather.block, Gather.half

    def __init__(self, ref, bufs, rows, nz, sems):
        self.ref, self.rows, self.nz = ref, rows, nz
        self.xb, self.yb, self.zb, self.fb = bufs
        self.xs, self.ys, self.zs, self.fs, self.xr, self.yr, self.zr, self.fr = sems
        s = lax.axis_index("shard")
        self.z, self.y, self.x = s // NY, s % NY, lax.axis_index("ctx")

    def xcp(self, c, zz):
        return rcopy(self.half(c, zz, 1 - self.y, 1 - self.x), self.xb.at[c, zz], self.xs.at[c, zz], self.xr.at[c, zz], {"ctx": 1 - self.x})

    def ycp(self, c, zz):
        return rcopy(self.half(c, zz, 1 - self.y, self.x), self.yb.at[c, zz], self.ys.at[c, zz], self.yr.at[c, zz], {"shard": self.z * NY + 1 - self.y})

    def zcp(self, c, i, zz, src):
        to = self.z + 1 if i == 0 else self.z - 1
        slot = zz if i == 0 else jnp.where(zz == to, self.nz, zz)
        return rcopy(src, self.zb.at[c, slot], self.zs.at[c, i, zz], self.zr.at[c, i, zz], {"shard": to * NY + self.y})

    def fcp(self, c):
        return rcopy(self.fb.at[c, 0], self.fb.at[c, 1], self.fs.at[c], self.fr.at[c], {"ctx": 1 - self.x})

    def start(self, c):
        for zz in range(self.nz):
            self.xcp(c, zz).start()

    def X(self, c):
        for zz in range(self.nz):
            self.xcp(c, zz).wait_recv()
            h = self.half(c, zz, 1 - self.y, self.x)
            h[...] = (h[...].astype(F32) + self.xb[c, zz].astype(F32)).astype(BF)
            self.ycp(c, zz).start()

    def Y(self, c):
        z, nz = self.z, self.nz
        for zz in range(nz):
            self.ycp(c, zz).wait_recv()
            h = self.half(c, zz, self.y, self.x)
            h[...] = (h[...].astype(F32) + self.yb[c, zz].astype(F32)).astype(BF)
            if zz > 0:
                pl.when(z == 0)(lambda: self.zcp(c, 0, zz, self.block(c, zz, self.y)).start())
            if zz < nz - 1:
                pl.when(z == nz - 1)(lambda: self.zcp(c, 1, zz, self.block(c, zz, self.y)).start())

    def Z(self, c, k):
        z, nz = self.z, self.nz
        zm = nz - 1 - z
        for i, ok, zz in ((0, both(z >= 1, k >= z), nz - 1 - k + z), (1, both(zm >= 1, k >= zm), k - zm)):

            @pl.when(ok)
            def _():
                slot = zz if i == 0 else jnp.where(zz == z, nz, zz)
                ref = self.zb.at[c, slot]
                rcopy(ref, ref, self.zs.at[c, i, zz], self.zr.at[c, i, zz], {"ctx": self.x}).wait_recv()

                @pl.when(zz != z)
                def _():
                    ref[...] = (ref[...].astype(F32) + self.block(c, zz, self.y)[...].astype(F32)).astype(BF)
                    self.zcp(c, i, zz, ref).start()

    def F(self, c):
        z, nz = self.z, self.nz
        fb0 = self.fb.at[c, 0]
        fb0[...] = self.block(c, z, self.y)[...]

        @pl.when(z > 0)
        def _():
            fb0[...] = (fb0[...].astype(F32) + self.zb[c, z].astype(F32)).astype(BF)

        @pl.when(z < nz - 1)
        def _():
            fb0[...] = (fb0[...].astype(F32) + self.zb[c, nz].astype(F32)).astype(BF)

        self.fcp(c).start()

    def G(self, c):
        self.fcp(c).wait_recv()
        return self.fb[c, 0].astype(F32) + self.fb[c, 1].astype(F32)

    def finish(self, c):
        z, nz = self.z, self.nz
        for zz in range(nz):
            self.xcp(c, zz).wait_send()
            self.ycp(c, zz).wait_send()
            b = self.block(c, zz, self.y)
            pl.when(both(z < nz - 1, zz > z))(lambda: self.zcp(c, 0, zz, b).wait_send())
            pl.when(both(z > 0, zz < z))(lambda: self.zcp(c, 1, zz, b).wait_send())
        self.fcp(c).wait_send()

    @staticmethod
    def sems(nc, nz):
        D = pltpu.SemaphoreType.DMA
        return [D((nc, nz)), D((nc, nz)), D((nc, 2, nz)), D((nc,)), D((nc, nz)), D((nc, nz)), D((nc, 2, nz)), D((nc,))]


def block_kernel(names, nz, NC, half, BQ, BK, *refs):
    w = types.SimpleNamespace(**dict(zip(names, refs)))
    T, D = w.hb.shape
    n = nz * NY
    rows = D // n
    hr = rows // 2
    FC = w.act.shape[2]
    CA = w.attd.shape[1]
    QO = NC
    npair = CA // 128
    nt = T // BQ
    ns = nt * npair
    sub = half // BQ
    s, x, t = lax.axis_index("shard"), lax.axis_index("ctx"), lax.axis_index("tp")
    me = x * n + s
    g = Gather(w.G, rows, nz, [getattr(w, f"ga{i}") for i in range(6)])
    gk = Gather(w.gkv, rows, nz, [getattr(w, f"gb{i}") for i in range(6)])
    r = Scatter(w.GR, (w.xb, w.yb, w.zb, w.fb), rows, nz, [getattr(w, f"sc{i}") for i in range(8)])
    lane = lax.broadcasted_iota(jnp.int32, (BQ, 128), 1)
    low = lane < 64

    def tile(i):
        return pl.ds(pl.multiple_of(i * BQ, BQ), BQ)

    own = pl.ds(pl.multiple_of(s * rows, 16), rows)
    loads = [(w.q, w.G.at[QO, own, pl.ds(0, CA)]), (w.o, w.G.at[QO, own, pl.ds(CA, CA)]), (w.kv, w.gkv.at[0, own]), (w.lnp, w.lb.at[s]), (w.hidden, w.hb), (w.cot, w.cb)]
    for c in range(NC):
        loads.append((w.up.at[:, pl.ds(c * FC, FC)], w.G.at[c, own, pl.ds(0, FC)]))
        loads.append((w.dw.at[:, pl.ds(c * FC, FC)], w.G.at[c, own, pl.ds(FC, FC)]))
    loads = [pltpu.make_async_copy(a, b, w.lsem.at[i]) for i, (a, b) in enumerate(loads)]
    for c in loads:
        c.start()

    peers = [(s, 1 - x)] + [(lax.rem(s + k, n), xx) for k in range(1, n) for xx in (x, 1 - x)]
    bar = pltpu.get_barrier_semaphore()
    for ps, px in peers:
        pl.semaphore_signal(bar, inc=1, device_id={"shard": ps, "ctx": px}, device_id_type=MESH)
    pl.semaphore_signal(bar, inc=1, device_id={"tp": 1 - t}, device_id_type=MESH)
    pl.semaphore_wait(bar, 2 * n)

    for c in loads[:4]:
        c.wait()
    lns = [rcopy(w.lb.at[s], w.lb.at[s], w.lns.at[k - 1], w.lnr.at[s], {"shard": lax.rem(s + k, n)}) for k in range(1, n)]
    for c in lns:
        c.start()
    gk.own(0)
    g.own(QO)
    for c in loads[4:]:
        c.wait()

    @pl.loop(0, nt)
    def _(i):
        base = w.bo[2 * x + i // sub] * half + lax.rem(i, sub) * BQ
        pos = (base + lax.broadcasted_iota(jnp.int32, (BQ, 128), 0)).astype(F32)
        ang = pos * w.freq[0:1, :]
        l64 = lax.rem(lane, 64)
        w.tc[tile(i), :] = jnp.where(l64 < 16, jnp.cos(ang), 1.0)
        sn = jnp.sin(ang)
        w.ts[tile(i), :] = jnp.where(l64 < 8, -sn, jnp.where(l64 < 16, sn, 0.0))
        w.ct[:, tile(i)] = w.cb[tile(i), :].T

    def rotated(v, i, sign):
        sw = jnp.where(lax.rem(lane, 16) < 8, pltpu.roll(v, 120, 1), pltpu.roll(v, 8, 1))
        turn = sw * w.ts[tile(i), :]
        return v * w.tc[tile(i), :] + (turn if sign > 0 else -turn)

    def head(d):
        for e in (gk, g):
            c = 0 if e is gk else QO
            if d < nz:
                e.Z(c, d)
            e.Y(c, d - 1)
            if d > 1:
                e.X(c, d - 2)

    head(1)
    g.own(0)
    for k in range(1, n):
        f = lax.rem(s + n - k, n)
        rcopy(w.lb.at[f], w.lb.at[f], w.lns.at[0], w.lnr.at[f], {"shard": f}).wait_recv()
    prm = None
    for k in range(n):
        piece = jnp.concatenate([w.lb[k], jnp.zeros((8, D - 128), F32)], axis=1)
        piece = pltpu.roll(piece, k * rows, 1) if k else piece
        prm = piece if prm is None else prm + piece
    w.prm[...] = prm

    def standardized(i):
        v = w.hb[tile(i), :].astype(F32)
        v = v - jnp.mean(v, axis=1, keepdims=True)
        rstd = lax.rsqrt(jnp.mean(v * v, axis=1, keepdims=True) + 1e-05)
        return v * rstd, rstd

    @pl.loop(0, nt)
    def _(i):
        xh, _ = standardized(i)
        na = (xh * w.prm[0:1, :] + w.prm[1:2, :]).astype(BF)
        nf = (xh * w.prm[2:3, :] + w.prm[3:4, :]).astype(BF)
        w.na[tile(i), :] = na
        w.nf[tile(i), :] = nf
        w.nat[:, tile(i)] = na.T
        w.nft[:, tile(i)] = nf.T

    for d in range(2, nz + 2):
        if d <= nz:
            head(d)
    for e, c in ((gk, 0), (g, QO)):
        e.X(c, nz - 1)

    def pump(c, d):
        @pl.when(c < NC)
        def _():
            if d == 1:
                pl.when(c + 1 < NC)(lambda: g.own(c + 1))
            g.Z(c, d)
            g.Y(c, d - 1)
            if d == nz - 1:
                g.X(c, 0)

        @pl.when(both(c >= 1, c <= NC))
        def _():
            if d == 1:
                g.Y(c - 1, nz - 1)
            g.X(c - 1, d)

    @pl.loop(0, nt)
    def _(i):
        kvp = dot(w.na[tile(i), :], w.gkv[0])
        kvp = jnp.where(low, rotated(kvp, i, 1), kvp).astype(BF)
        w.kvb[0, tile(i), :] = kvp
        w.keys[tile(i), :] = kvp[:, :64]
        w.values[tile(i), :] = pltpu.roll(kvp.astype(F32), 64, 1)[:, :64].astype(BF)

    kvx = rcopy(w.kvb.at[0], w.kvb.at[1], w.es.at[0], w.er.at[0], {"ctx": 1 - x})
    kvx.start()

    order = [w.bo[2 * x], w.bo[2 * x + 1], w.bo[2 * (1 - x)], w.bo[2 * (1 - x) + 1]]
    lane1 = lax.broadcasted_iota(jnp.int32, (1, 128), 1)

    @pl.loop(0, nt)
    def _(i):
        qp = dot(w.na[tile(i), :], w.G[QO, :, 0:CA])
        ga = dot(w.cb[tile(i), :], w.G[QO, :, CA : 2 * CA])
        mine = w.bo[2 * x + i // sub]
        hide = jnp.zeros((1, 128), F32)
        for j in range(4):
            hide = jnp.where(lane1 == 64 + j, jnp.where(order[j] <= mine, 0.0, NEG), hide)
        for p in range(npair):
            st = i * npair + p
            qs = rotated(qp[:, 128 * p : 128 * p + 128], i, 1).astype(BF).astype(F32) * 0.125
            w.qx[st, 0:BQ, :] = jnp.where(low, qs, hide).astype(BF)
            w.qx[st, BQ : 2 * BQ, :] = jnp.where(low, pltpu.roll(qs, 64, 1), hide).astype(BF)
            qt = qs.astype(BF).T
            w.qt[st, :, 0:BQ] = qt[:64]
            w.qt[st, :, BQ : 2 * BQ] = qt[64:]
            gp = ga[:, 128 * p : 128 * p + 128]
            w.dox[st, 0:BQ, :] = jnp.where(low, gp, 0.0).astype(BF)
            w.dox[st, BQ : 2 * BQ, :] = jnp.where(low, pltpu.roll(gp, 64, 1), 0.0).astype(BF)
            gt = gp.astype(BF).T
            w.dt[st, :, 0:BQ] = gt[:64]
            w.dt[st, :, BQ : 2 * BQ] = gt[64:]
        for d in range(1, nz):
            pl.when(i == d - 1)(functools.partial(pump, 0, d))

    kvx.wait_recv()

    @pl.loop(0, 2 * nt)
    def _(i):
        kvf = w.kvb[i // nt, tile(lax.rem(i, nt)), :].astype(F32)
        hot = jnp.where(lane == 64 + i // sub, 1.0, 0.0)
        w.kx[tile(i), :] = jnp.where(low, kvf, hot).astype(BF)
        w.k0[tile(i), :] = jnp.where(low, kvf, 0.0).astype(BF)
        w.v0[tile(i), :] = jnp.where(low, pltpu.roll(kvf, 64, 1), 0.0).astype(BF)

    w.acc[...] = jnp.zeros_like(w.acc)

    def feed_forward():
        @pl.loop(0, NC)
        def _(c):
            @pl.loop(0, nt)
            def _(i):
                hp = dot(w.nf[tile(i), :], w.G[c, :, 0:FC])
                da = dot(w.cb[tile(i), :], w.G[c, :, FC : 2 * FC])
                cdf = 0.5 + 0.5 * lax.erf(hp * 0.7071067811865476)
                pdf = jnp.exp(-0.5 * hp * hp) * 0.3989422804014327
                w.act[c, tile(i), :] = (hp * cdf).astype(BF)
                w.dh[c, tile(i), :] = (da * (cdf + hp * pdf)).astype(BF)
                pl.when(i == 1)(lambda: pump(c + 2, 1))
                pl.when(i == 3)(lambda: pump(c + 2, 2))

            pl.when(c >= 1)(lambda: r.X(c - 1))

            @pl.loop(0, D // BQ)
            def _(m):
                w.GR[c, tile(m), 0:FC] = dot(w.nft[tile(m), :], w.dh[c]).astype(BF)
                w.GR[c, tile(m), FC : 2 * FC] = dot(w.ct[tile(m), :], w.act[c]).astype(BF)

            r.start(c)
            pump(c + 2, 3)
            pl.when(c >= 2)(lambda: r.Y(c - 2))

        @pl.loop(0, nt)
        def _(i):
            dn = dot_nt(w.dh[0, tile(i), :], w.G[0, :, 0:FC])
            br = dot_nt(w.act[0, tile(i), :], w.G[0, :, FC : 2 * FC])
            for c in range(1, NC):
                dn = dn + dot_nt(w.dh[c, tile(i), :], w.G[c, :, 0:FC])
                br = br + dot_nt(w.act[c, tile(i), :], w.G[c, :, FC : 2 * FC])
            w.na[tile(i), :] = dn.astype(BF)
            w.act[0, tile(i), :] = br[:, :FC].astype(BF)
            w.act[1, tile(i), :] = br[:, FC:].astype(BF)

        dnx.start()
        r.X(NC - 1)
        r.Y(NC - 2)

    dnx = rcopy(w.na, w.dnr, w.es.at[1], w.er.at[1], {"tp": 1 - t})

    def own_out(c, v):
        cols = pl.ds(pl.multiple_of(c * FC, FC), FC)
        w.ou[:, cols] = v[:, :FC]
        w.od[:, cols] = v[:, FC:]

    def within(h, f):
        pl.when(both(h >= 0, h < NC))(lambda: f(h))

    def scatter_step(i):
        pl.when(i == 0)(lambda: r.Y(NC - 1))
        h = i // 2

        @pl.when(lax.rem(i, 2) == 0)
        def _():
            within(h, lambda c: r.Z(c, 1))
            within(h - 1, lambda c: r.Z(c, 3))
            within(h - 2, lambda c: own_out(c, r.G(c)))

        @pl.when(lax.rem(i, 2) == 1)
        def _():
            within(h, lambda c: r.Z(c, 2))
            within(h - 1, lambda c: r.F(c))

    first = nz - 1

    def attention(st):
        i = st // npair
        p = lax.rem(st, npair)
        own_b = i // sub
        r0 = lax.rem(i, sub) * BQ
        R = 2 * BQ
        nk = w.kx.shape[0] // BK
        per = half // BK
        offs = []
        for j in range(nk):
            if j < per:
                off = own_b * half + j * BK
            elif j < 2 * per:
                off = (1 - own_b) * half + (j - per) * BK
            else:
                off = j * BK
            offs.append(pl.ds(pl.multiple_of(off, BK), BK))
        cols = [slice(j * BK, (j + 1) * BK) for j in range(nk)]
        q, do = w.qx[st], w.dox[st]
        m = None
        for j in range(nk):
            sc = dot_nt(q, w.kx[offs[j], :])
            if j < per:
                row = lax.rem(lax.broadcasted_iota(jnp.int32, (R, BK), 0), BQ) + r0
                col = lax.broadcasted_iota(jnp.int32, (R, BK), 1) + j * BK
                sc = jnp.where(col <= row, sc, NEG)
            w.ss[:, cols[j]] = sc
            for k in range(BK // 128):
                mk = sc[:, k * 128 : (k + 1) * 128]
                m = mk if m is None else jnp.maximum(m, mk)
        m = jnp.max(m, axis=1, keepdims=True)
        l = o = None
        for j in range(nk):
            e = jnp.exp(w.ss[:, cols[j]] - m)
            w.ss[:, cols[j]] = e
            for k in range(BK // 128):
                lk = e[:, k * 128 : (k + 1) * 128]
                l = lk if l is None else l + lk
            eb = e.astype(BF)
            w.ps[:, cols[j]] = eb
            oj = dot(eb, w.v0[offs[j], :])
            o = oj if o is None else o + oj
        inv = 1.0 / jnp.sum(l, axis=1, keepdims=True)
        o = o * inv
        delta = jnp.sum(o * do.astype(F32), axis=1, keepdims=True)
        inv_row = jnp.transpose(jnp.broadcast_to(inv, (R, 128)))[:1, :]
        qs = (w.qt[st].astype(F32) * inv_row).astype(BF)
        dos = (w.dt[st].astype(F32) * inv_row).astype(BF)
        dq = None
        for j in range(nk):
            dp = dot_nt(do, w.v0[offs[j], :])
            ds = (w.ss[:, cols[j]] * (dp - delta)).astype(BF)
            dj = dot(ds, w.k0[offs[j], :])
            dq = dj if dq is None else dq + dj
            w.acc[0:64, offs[j]] += dot(qs, ds)
            w.acc[64:128, offs[j]] += dot(dos, w.ps[:, cols[j]])
        dq = dq * (inv * 0.125)
        pair = pl.ds(pl.multiple_of(p * 128, 128), 128)
        w.attd[tile(i), pair] = (o[:BQ] + pltpu.roll(o[BQ:], 64, 1)).astype(BF)
        w.gq[tile(i), pair] = rotated(dq[:BQ] + pltpu.roll(dq[BQ:], 64, 1), i, -1).astype(BF)

    @pl.loop(0, ns)
    def _(st):
        for d in range(1, nz):
            pl.when(st == d - 1)(functools.partial(pump, 1, d))
        pl.when(st == first)(feed_forward)
        pl.when(st >= first)(lambda: scatter_step(st - first))
        attention(st)

    for i in range(2):
        w.dS[i] = w.acc[:, i * T : (i + 1) * T].astype(BF)
    dtp = rcopy(w.dS, w.dR, w.es.at[2], w.er.at[2], {"tp": 1 - t})
    dtp.start()
    dnx.wait_recv()

    @pl.loop(0, nt)
    def _(i):
        br = dot_nt(w.attd[tile(i), :], w.G[QO, :, CA : 2 * CA])
        w.act[0, tile(i), :] = (w.act[0, tile(i), :].astype(F32) + br[:, :FC]).astype(BF)
        w.act[1, tile(i), :] = (w.act[1, tile(i), :].astype(F32) + br[:, FC:]).astype(BF)

    brx = rcopy(w.act.at[pl.ds(0, 2)], w.dh.at[pl.ds(0, 2)], w.es.at[3], w.er.at[3], {"tp": 1 - t})
    brx.start()

    @pl.loop(0, D // BQ)
    def _(m):
        w.GR[QO, tile(m), 0:CA] = dot(w.nat[tile(m), :], w.gq[...]).astype(BF)
        w.GR[QO, tile(m), CA : 2 * CA] = dot(w.ct[tile(m), :], w.attd[...]).astype(BF)

    r.start(QO)
    dtp.wait_recv()
    w.dX[...] = (w.dS[1].astype(F32) + w.dR[1].astype(F32)).astype(BF)
    dxx = rcopy(w.dX, w.dXR, w.es.at[4], w.er.at[4], {"ctx": 1 - x})
    dxx.start()

    @pl.loop(0, nt)
    def _(i):
        ga = dot_nt(w.gq[tile(i), :], w.G[QO, :, 0:CA])
        w.act[2, tile(i), :] = ga[:, :FC].astype(BF)
        w.act[3, tile(i), :] = ga[:, FC:].astype(BF)

    gax = rcopy(w.act.at[pl.ds(2, 2)], w.dh.at[pl.ds(2, 2)], w.es.at[5], w.er.at[5], {"tp": 1 - t})
    gax.start()
    r.F(NC - 1)
    r.X(QO)
    brx.wait_recv()

    @pl.loop(0, nt)
    def _(i):
        for k in range(2):
            cs = slice(k * FC, (k + 1) * FC)
            v = w.act[k, tile(i), :].astype(F32) + w.dh[k, tile(i), :].astype(F32)
            w.nf[tile(i), cs] = (w.hb[tile(i), cs].astype(F32) + v).astype(BF)

    outx = pltpu.make_async_copy(w.nf, w.out_tokens, w.osem.at[0])
    outx.start()
    r.Y(QO)
    dxx.wait_recv()

    @pl.loop(0, nt)
    def _(i):
        v = w.dS[0, :, tile(i)].astype(F32) + w.dR[0, :, tile(i)].astype(F32) + w.dXR[:, tile(i)].astype(F32)
        v = v.T
        w.gkb[tile(i), :] = jnp.where(low, rotated(v, i, -1), v).astype(BF)

    w.kvS[...] = dot(w.nat[...], w.gkb[...]).astype(BF)

    def kv_rows(owner):
        return pl.ds(pl.multiple_of(owner * rows + t * hr, 16), hr)

    kvs = [rcopy(w.kvS.at[kv_rows(ps)], w.kvR.at[me], w.ks.at[i], w.kr.at[me], {"shard": ps, "ctx": px}) for i, (ps, px) in enumerate(peers)]
    for c in kvs:
        c.start()
    r.Z(QO, 1)
    gax.wait_recv()
    w.lg[...] = jnp.zeros_like(w.lg)

    @pl.loop(0, nt)
    def _(i):
        xh, rstd = standardized(i)
        kvg = dot_nt(w.gkb[tile(i), :], w.gkv[0])
        gn = jnp.concatenate([w.act[k, tile(i), :].astype(F32) + w.dh[k, tile(i), :].astype(F32) for k in (2, 3)], axis=1) + kvg
        gf = w.na[tile(i), :].astype(F32) + w.dnr[tile(i), :].astype(F32)
        e = gn * w.prm[0:1, :] + gf * w.prm[2:3, :]
        e = rstd * (e - jnp.mean(e, axis=1, keepdims=True) - xh * jnp.mean(e * xh, axis=1, keepdims=True))
        w.hg[tile(i), :] = w.cb[tile(i), :].astype(F32) + e
        w.lg[0:1, :] += jnp.sum(gn * xh, axis=0, keepdims=True)
        w.lg[1:2, :] += jnp.sum(gn, axis=0, keepdims=True)
        w.lg[2:3, :] += jnp.sum(gf * xh, axis=0, keepdims=True)
        w.lg[3:4, :] += jnp.sum(gf, axis=0, keepdims=True)
        pl.when(i == 1)(lambda: r.Z(QO, 2))

    lg = w.lg[...]
    keep = lax.broadcasted_iota(jnp.int32, (8, 128), 1) < rows
    for k in range(n):
        v = pltpu.roll(lg, D - k * rows, 1) if k else lg
        w.lS[k] = jnp.where(keep, v[:, :128], 0.0)
    lgs = [rcopy(w.lS.at[ps], w.lR.at[me], w.ls.at[i], w.lr.at[me], {"shard": ps, "ctx": px}) for i, (ps, px) in enumerate(peers)]
    for c in lgs:
        c.start()
    own_out(NC - 1, r.G(NC - 1))
    r.Z(QO, 3)
    r.F(QO)

    def arrived(ref, sems, i, ps, px):
        k = px * n + ps
        return rcopy(ref.at[k], ref.at[k], sems.at[i], sems.at[k], {"shard": ps, "ctx": px})

    for i, (ps, px) in enumerate(peers):
        arrived(w.kvR, w.kr, i, ps, px).wait_recv()
    w.kvR[me] = w.kvS[kv_rows(s), :]
    v = w.kvR[0].astype(F32)
    for k in range(1, 2 * n):
        v = v + w.kvR[k].astype(F32)
    w.kvF[t] = v
    kfx = rcopy(w.kvF.at[t], w.kvF.at[t], w.es.at[6], w.er.at[6], {"tp": 1 - t})
    kfx.start()
    for i, (ps, px) in enumerate(peers):
        arrived(w.lR, w.lr, i, ps, px).wait_recv()
    w.lR[me] = w.lS[s]
    v = w.lR[0]
    for k in range(1, 2 * n):
        v = v + w.lR[k]
    w.lno[...] = v
    rcopy(w.kvF.at[1 - t], w.kvF.at[1 - t], w.es.at[6], w.er.at[6], {"tp": 1 - t}).wait_recv()
    w.okv[0:hr, :] = w.kvF[0]
    w.okv[hr:rows, :] = w.kvF[1]
    v = r.G(QO)
    w.oq[...] = v[:, :CA]
    w.oo[...] = v[:, CA:]
    outx.wait()
    for c in lns + [kvx, dnx, dtp, brx, dxx, gax, kfx] + kvs + lgs:
        c.wait_send()
    gk.finish(0)
    for c in range(NC + 1):
        g.finish(c)
        r.finish(c)


def block_call(bo, freq, hidden, cot, lnp, up, dw, q, o, kv, nz, half, cid):
    T, D = hidden.shape
    rows, CU = up.shape
    CA, CK = q.shape[1], kv.shape[1]
    FC = CA
    NC = CU // FC
    n = nz * NY
    hr = rows // 2
    BQ, BK = 256, 512
    ns = T // BQ * (CA // 128)
    A = pl.BlockSpec(memory_space=pl.ANY)
    V = pl.BlockSpec(memory_space=pltpu.VMEM)
    S = pl.BlockSpec(memory_space=pltpu.SMEM)
    Dm = pltpu.SemaphoreType.DMA
    ins = ["bo", "freq", "hidden", "cot", "lnp", "up", "dw", "q", "o", "kv"]
    sd = jax.ShapeDtypeStruct
    outs = {
        "out_tokens": (sd((T, D), BF), A), "keys": (sd((T, 64), BF), V), "values": (sd((T, 64), BF), V), "hg": (sd((T, D), F32), V),
        "lno": (sd((8, 128), F32), V), "oq": (sd((rows, CA), F32), V), "okv": (sd((rows, CK), F32), V), "oo": (sd((rows, CA), F32), V),
        "ou": (sd((rows, CU), F32), V), "od": (sd((rows, CU), F32), V),
    }
    b = lambda *sh: pltpu.VMEM(sh, BF)
    f = lambda *sh: pltpu.VMEM(sh, F32)
    scr = {
        "hb": b(T, D), "cb": b(T, D), "ct": b(D, T), "na": b(T, D), "nf": b(T, D), "nft": b(D, T), "nat": b(D, T),
        "G": b(NC + 1, D, 2 * FC), "gkv": b(1, D, CK), "GR": b(NC + 1, D, 2 * FC),
        "xb": b(NC + 1, nz, hr, 2 * FC), "yb": b(NC + 1, nz, hr, 2 * FC), "zb": b(NC + 1, nz + 1, rows, 2 * FC), "fb": b(NC + 1, 2, rows, 2 * FC),
        "lb": f(n, 8, 128), "act": b(NC, T, FC), "dh": b(NC, T, FC), "dnr": b(T, D),
        "qx": b(ns, 2 * BQ, 128), "dox": b(ns, 2 * BQ, 128), "qt": b(ns, 64, 2 * BQ), "dt": b(ns, 64, 2 * BQ),
        "kvb": b(2, T, CK), "kx": b(2 * T, 128), "k0": b(2 * T, 128), "v0": b(2 * T, 128),
        "ss": f(2 * BQ, 2 * T), "ps": b(2 * BQ, 2 * T), "attd": b(T, CA), "gq": b(T, CA), "acc": f(128, 2 * T),
        "tc": f(T, 128), "ts": f(T, 128), "dS": b(2, 128, T), "dR": b(2, 128, T), "dX": b(128, T), "dXR": b(128, T), "gkb": b(T, 128),
        "kvS": b(D, CK), "kvR": b(2 * n, hr, CK), "kvF": f(2, hr, CK), "lS": f(n, 8, 128), "lR": f(2 * n, 8, 128), "prm": f(8, D), "lg": f(8, D),
        "lsem": Dm((6 + 2 * NC,)), "lns": Dm((n - 1,)), "lnr": Dm((n,)), "es": Dm((7,)), "er": Dm((7,)), "osem": Dm((1,)),
        "ks": Dm((2 * n - 1,)), "kr": Dm((2 * n,)), "ls": Dm((2 * n - 1,)), "lr": Dm((2 * n,)),
    }
    scr.update({f"ga{i}": v for i, v in enumerate(Gather.sems(NC + 1, nz))})
    scr.update({f"gb{i}": v for i, v in enumerate(Gather.sems(1, nz))})
    scr.update({f"sc{i}": v for i, v in enumerate(Scatter.sems(NC + 1, nz))})
    names = ins + list(outs) + list(scr)
    res = pl.pallas_call(
        functools.partial(block_kernel, names, nz, NC, half, BQ, BK),
        out_shape=tuple(v[0] for v in outs.values()),
        in_specs=[S, V] + [A] * 8,
        out_specs=tuple(v[1] for v in outs.values()),
        scratch_shapes=list(scr.values()),
        compiler_params=pltpu.CompilerParams(collective_id=cid, has_side_effects=True, vmem_limit_bytes=67043328),
        name="block",
    )(bo, freq, hidden, cot, lnp, up, dw, q, o, kv)
    return dict(zip(outs, res))


def fits(mesh):
    return mesh.shape["shard"] == 8 and mesh.shape["ctx"] == 2


def fast_device(hidden, block_order, ln1_gain, ln1_bias, ln2_gain, ln2_bias, q_weight, kv_weight, o_weight, up_weight, down_weight, cotangent):
    seqs, span, width = hidden.shape
    hd = kv_weight.shape[1] // 2
    rows = ln1_gain.shape[0]
    lnp = jnp.pad(jnp.stack([ln1_gain, ln1_bias, ln2_gain, ln2_bias]).astype(F32), ((0, 4), (0, 128 - rows)))
    freq = 10000.0 ** (-2.0 * (np.arange(128) % (ROT // 2)) / ROT)
    freq = jnp.asarray(np.broadcast_to(freq, (8, 128)), F32)
    v = block_call(block_order, freq, hidden.reshape(span, width), cotangent.reshape(span, width), lnp, up_weight, down_weight, q_weight, o_weight, kv_weight, width // rows // NY, span // 2, 1)
    lo = v["lno"]
    return (v["out_tokens"][None], v["keys"][None], v["values"][None], v["hg"][None], lo[0, :rows], lo[1, :rows], lo[2, :rows], lo[3, :rows], v["oq"], v["okv"], v["oo"], v["ou"], v["od"])


def solution(mesh):
    return jax.shard_map(
        fast_device if fits(mesh) else on_device,
        mesh=mesh,
        in_specs=(
            P("shard", "ctx", None),
            P(),
            P("shard"),
            P("shard"),
            P("shard"),
            P("shard"),
            P("shard", "tp"),
            P("shard", None),
            P("shard", "tp"),
            P("shard", "tp"),
            P("shard", "tp"),
            P("shard", "ctx", None),
        ),
        out_specs=(
            P("shard", "ctx", None),
            P("shard", "ctx", None),
            P("shard", "ctx", None),
            P("shard", "ctx", None),
            P("shard"),
            P("shard"),
            P("shard"),
            P("shard"),
            P("shard", "tp"),
            P("shard", None),
            P("shard", "tp"),
            P("shard", "tp"),
            P("shard", "tp"),
        ),
        check_vma=False,
    )
```

```python
import functools
import types

import jax
import jax.numpy as jnp
import numpy as np
from jax import lax
from jax.experimental import pallas as pl
from jax.experimental.pallas import tpu as pltpu
from jax.sharding import PartitionSpec as P

F32 = jnp.float32
BF = jnp.bfloat16
MESH = pl.DeviceIdType.MESH

ROT = 16


def layer_norm(values, gain, shift):
    center = values - jnp.mean(values, axis=-1, keepdims=True)
    spread = jnp.mean(center * center, axis=-1, keepdims=True)
    return center * lax.rsqrt(spread + 1e-05) * gain + shift


def gelu_exact(values):
    return jax.nn.gelu(values, approximate=False)


def rotate(tensor, places, sign):
    half_rot = ROT // 2
    freq = jnp.power(10000.0, -2.0 * jnp.arange(half_rot, dtype=jnp.float32) / ROT)
    angle = places.astype(jnp.float32)[:, None] * freq[None, :]
    cosine = jnp.cos(angle)[:, None, :]
    sine = sign * jnp.sin(angle)[:, None, :]
    first = tensor[..., :half_rot]
    second = tensor[..., half_rot:ROT]
    return jnp.concatenate(
        [first * cosine - second * sine, second * cosine + first * sine, tensor[..., ROT:]], axis=-1
    )


def tok_positions(block_order, rows, half_block):
    index = rows // half_block
    table = jnp.arange(block_order.shape[0], dtype=jnp.int32)
    picked = jnp.sum(jnp.where(index[:, None] == table[None, :], block_order[None, :], 0), axis=1)
    return picked * half_block + rows % half_block


def right_product(left, right):
    return lax.dot_general(
        left, right, (((1,), (1,)), ((), ())), preferred_element_type=jnp.float32
    )


def left_product(left, right):
    return lax.dot_general(
        left, right, (((0,), (0,)), ((), ())), preferred_element_type=jnp.float32
    )


def on_device(
    hidden,
    block_order,
    ln1_gain,
    ln1_bias,
    ln2_gain,
    ln2_bias,
    q_weight,
    kv_weight,
    o_weight,
    up_weight,
    down_weight,
    cotangent,
):
    seqs, span, width = hidden.shape
    half_block = span // 2
    head_size = kv_weight.shape[1] // 2
    local_heads = q_weight.shape[1] // head_size
    row_count = seqs * span
    query_rows = span * local_heads
    scale = head_size ** (-0.5)
    gathered = (
        lax.all_gather(ln1_gain, "shard", axis=0, tiled=True),
        lax.all_gather(ln1_bias, "shard", axis=0, tiled=True),
        lax.all_gather(ln2_gain, "shard", axis=0, tiled=True),
        lax.all_gather(ln2_bias, "shard", axis=0, tiled=True),
        lax.all_gather(q_weight, "shard", axis=0, tiled=True),
        lax.all_gather(kv_weight, "shard", axis=0, tiled=True),
        lax.all_gather(o_weight, "shard", axis=0, tiled=True),
        lax.all_gather(up_weight, "shard", axis=0, tiled=True),
        lax.all_gather(down_weight, "shard", axis=0, tiled=True),
    )
    gain_attn, bias_attn, gain_ffn, bias_ffn, w_query, w_keyval, w_output, w_up, w_down = gathered
    offset = lax.axis_index("ctx") * span
    query_places = tok_positions(
        block_order, offset + jnp.arange(span, dtype=jnp.int32), half_block
    )
    row_places = jnp.repeat(query_places, local_heads)
    tokens = hidden.astype(jnp.float32).reshape(row_count, width)
    norm_attn = layer_norm(
        tokens, gain_attn.astype(jnp.float32), bias_attn.astype(jnp.float32)
    ).astype(jnp.bfloat16)
    norm_ffn = layer_norm(
        tokens, gain_ffn.astype(jnp.float32), bias_ffn.astype(jnp.float32)
    ).astype(jnp.bfloat16)
    query_pre = jnp.dot(norm_attn, w_query, preferred_element_type=jnp.float32).reshape(
        seqs, span, local_heads, head_size
    )
    queries = (
        rotate(query_pre, query_places, 1.0)
        .astype(jnp.bfloat16)
        .reshape(seqs, query_rows, head_size)
    )
    keyval_pre = jnp.dot(norm_attn, w_keyval, preferred_element_type=jnp.float32).reshape(
        seqs, span, 2 * head_size
    )
    keys = rotate(keyval_pre[:, :, None, :head_size], query_places, 1.0)[:, :, 0, :].astype(
        jnp.bfloat16
    )
    values = keyval_pre[:, :, head_size:].astype(jnp.bfloat16)
    start_state = (
        jnp.full((seqs, query_rows), -1e30, jnp.float32),
        jnp.zeros((seqs, query_rows), jnp.float32),
        jnp.zeros((seqs, query_rows, head_size), jnp.float32),
    )
    key_piece = lax.all_gather(keys, "ctx", axis=1, tiled=True)
    value_piece = lax.all_gather(values, "ctx", axis=1, tiled=True)
    count = key_piece.shape[1]
    key_places = tok_positions(block_order, jnp.arange(count, dtype=jnp.int32), half_block)
    visible = key_places[None, :] <= row_places[:, None]

    def one_block(args):
        peak, total, accum, query_block, key_block, value_block = args
        scores = (
            jnp.einsum("qd,kd->qk", query_block, key_block, preferred_element_type=jnp.float32)
            * scale
        )
        scores = jnp.where(visible, scores, -1e30)
        new_peak = jnp.maximum(peak, jnp.max(scores, axis=1))
        factor = jnp.exp(peak - new_peak)
        weights = jnp.where(visible, jnp.exp(scores - new_peak[:, None]), 0.0)
        total = total * factor + jnp.sum(weights, axis=1)
        accum = accum * factor[:, None] + jnp.einsum(
            "qk,kd->qd",
            weights.astype(jnp.bfloat16),
            value_block,
            preferred_element_type=jnp.float32,
        )
        return (new_peak, total, accum)

    peak, total, accum = lax.map(
        one_block, (start_state[0], start_state[1], start_state[2], queries, key_piece, value_piece)
    )
    attended = (
        (accum / total[:, :, None]).astype(jnp.bfloat16).reshape(row_count, local_heads * head_size)
    )
    log_total = peak + jnp.log(total)
    hidden_pre = jnp.dot(norm_ffn, w_up, preferred_element_type=jnp.float32)
    activation_full, gelu_pull = jax.vjp(gelu_exact, hidden_pre)
    activation = activation_full.astype(jnp.bfloat16)
    branch = right_product(attended, w_output) + right_product(activation, w_down)
    branch = lax.psum(branch.astype(jnp.bfloat16), "tp").astype(jnp.float32)
    mixed = (tokens + branch).astype(jnp.bfloat16).reshape(seqs, span, width)
    regathered = (
        lax.all_gather(ln1_gain, "shard", axis=0, tiled=True),
        lax.all_gather(ln2_gain, "shard", axis=0, tiled=True),
        lax.all_gather(q_weight, "shard", axis=0, tiled=True),
        lax.all_gather(kv_weight, "shard", axis=0, tiled=True),
        lax.all_gather(o_weight, "shard", axis=0, tiled=True),
        lax.all_gather(up_weight, "shard", axis=0, tiled=True),
        lax.all_gather(down_weight, "shard", axis=0, tiled=True),
    )
    gain_attn, gain_ffn, w_query, w_keyval, w_output, w_up, w_down = regathered
    grad_out = cotangent.reshape(row_count, width)
    grad_attended = (
        jnp.dot(grad_out, w_output, preferred_element_type=jnp.float32)
        .astype(jnp.bfloat16)
        .reshape(seqs, query_rows, head_size)
    )
    grad_activation = jnp.dot(grad_out, w_down, preferred_element_type=jnp.float32)
    grad_hidden = gelu_pull(grad_activation)[0].astype(jnp.bfloat16)
    grad_w_output = left_product(grad_out, attended)
    grad_w_down = left_product(grad_out, activation)
    grad_w_up = left_product(norm_ffn, grad_hidden)
    grad_norm_ffn = right_product(grad_hidden, w_up)
    all_keys, all_values = (
        lax.all_gather(keys, "ctx", axis=1, tiled=True),
        lax.all_gather(values, "ctx", axis=1, tiled=True),
    )
    key_count = all_keys.shape[1]
    key_places = tok_positions(block_order, jnp.arange(key_count, dtype=jnp.int32), half_block)
    visible_all = key_places[None, :] <= row_places[:, None]

    def backward_one(args):
        query_block, key_block, value_block, grad_block, log_block = args
        scores = (
            jnp.einsum("qd,kd->qk", query_block, key_block, preferred_element_type=jnp.float32)
            * scale
        )
        probs = jnp.where(visible_all, jnp.exp(scores - log_block[:, None]), 0.0)
        grad_probs = jnp.einsum(
            "qd,kd->qk", grad_block, value_block, preferred_element_type=jnp.float32
        )
        delta = jnp.sum(probs * grad_probs, axis=1, keepdims=True)
        grad_scores = (probs * (grad_probs - delta)).astype(jnp.bfloat16)
        grad_query = (
            jnp.einsum("qk,kd->qd", grad_scores, key_block, preferred_element_type=jnp.float32)
            * scale
        )
        grad_key = (
            jnp.einsum("qk,qd->kd", grad_scores, query_block, preferred_element_type=jnp.float32)
            * scale
        )
        grad_value = jnp.einsum(
            "qk,qd->kd", probs.astype(jnp.bfloat16), grad_block, preferred_element_type=jnp.float32
        )
        return (grad_query, jnp.concatenate([grad_key, grad_value], axis=1))

    grad_queries, grad_keyvals = lax.map(
        backward_one, (queries, all_keys, all_values, grad_attended, log_total)
    )
    grad_keyvals = lax.psum_scatter(
        grad_keyvals.astype(jnp.bfloat16), "ctx", scatter_dimension=1, tiled=True
    ).astype(jnp.float32)
    grad_keyvals = lax.psum(grad_keyvals.astype(jnp.bfloat16), "tp").astype(jnp.float32)
    grad_key_pre = rotate(grad_keyvals[:, :, None, :head_size], query_places, -1.0)[:, :, 0, :]
    grad_keyval_pre = (
        jnp.concatenate([grad_key_pre, grad_keyvals[:, :, head_size:]], axis=2)
        .astype(jnp.bfloat16)
        .reshape(row_count, 2 * head_size)
    )
    grad_query_pre = (
        rotate(grad_queries.reshape(seqs, span, local_heads, head_size), query_places, -1.0)
        .astype(jnp.bfloat16)
        .reshape(row_count, local_heads * head_size)
    )
    grad_w_query = left_product(norm_attn, grad_query_pre)
    grad_w_keyval = left_product(norm_attn, grad_keyval_pre)
    grad_norm_attn = right_product(grad_query_pre, w_query)
    shared_term = right_product(grad_keyval_pre, w_keyval)
    zero_shift = jnp.zeros((width,), jnp.float32)
    attn_pull = jax.vjp(layer_norm, tokens, gain_attn.astype(jnp.float32), zero_shift)[1]
    ffn_pull = jax.vjp(layer_norm, tokens, gain_ffn.astype(jnp.float32), zero_shift)[1]
    grad_norm_attn, grad_norm_ffn = (
        lax.psum(grad_norm_attn.astype(jnp.bfloat16), "tp").astype(jnp.float32),
        lax.psum(grad_norm_ffn.astype(jnp.bfloat16), "tp").astype(jnp.float32),
    )
    grad_norm_attn = grad_norm_attn + shared_term
    grad_tok_attn, grad_gain_attn, grad_shift_attn = attn_pull(grad_norm_attn)
    grad_tok_ffn, grad_gain_ffn, grad_shift_ffn = ffn_pull(grad_norm_ffn)
    grad_tok_norms = grad_tok_attn + grad_tok_ffn
    grad_tokens = (grad_out.astype(jnp.float32) + grad_tok_norms).reshape(seqs, span, width)
    grads = (
        grad_gain_attn,
        grad_shift_attn,
        grad_gain_ffn,
        grad_shift_ffn,
        grad_w_query,
        grad_w_keyval,
        grad_w_output,
        grad_w_up,
        grad_w_down,
    )
    owned = (
        lax.psum_scatter(
            grads[0].astype(jnp.bfloat16), "shard", scatter_dimension=0, tiled=True
        ).astype(jnp.float32),
        lax.psum_scatter(
            grads[1].astype(jnp.bfloat16), "shard", scatter_dimension=0, tiled=True
        ).astype(jnp.float32),
        lax.psum_scatter(
            grads[2].astype(jnp.bfloat16), "shard", scatter_dimension=0, tiled=True
        ).astype(jnp.float32),
        lax.psum_scatter(
            grads[3].astype(jnp.bfloat16), "shard", scatter_dimension=0, tiled=True
        ).astype(jnp.float32),
        lax.psum_scatter(
            grads[4].astype(jnp.bfloat16), "shard", scatter_dimension=0, tiled=True
        ).astype(jnp.float32),
        lax.psum_scatter(
            grads[5].astype(jnp.bfloat16), "shard", scatter_dimension=0, tiled=True
        ).astype(jnp.float32),
        lax.psum_scatter(
            grads[6].astype(jnp.bfloat16), "shard", scatter_dimension=0, tiled=True
        ).astype(jnp.float32),
        lax.psum_scatter(
            grads[7].astype(jnp.bfloat16), "shard", scatter_dimension=0, tiled=True
        ).astype(jnp.float32),
        lax.psum_scatter(
            grads[8].astype(jnp.bfloat16), "shard", scatter_dimension=0, tiled=True
        ).astype(jnp.float32),
    )
    owned = (
        lax.psum(owned[0].astype(jnp.bfloat16), "ctx").astype(jnp.float32),
        lax.psum(owned[1].astype(jnp.bfloat16), "ctx").astype(jnp.float32),
        lax.psum(owned[2].astype(jnp.bfloat16), "ctx").astype(jnp.float32),
        lax.psum(owned[3].astype(jnp.bfloat16), "ctx").astype(jnp.float32),
        lax.psum(owned[4].astype(jnp.bfloat16), "ctx").astype(jnp.float32),
        lax.psum(owned[5].astype(jnp.bfloat16), "ctx").astype(jnp.float32),
        lax.psum(owned[6].astype(jnp.bfloat16), "ctx").astype(jnp.float32),
        lax.psum(owned[7].astype(jnp.bfloat16), "ctx").astype(jnp.float32),
        lax.psum(owned[8].astype(jnp.bfloat16), "ctx").astype(jnp.float32),
    )
    return (
        mixed,
        keys,
        values,
        grad_tokens,
        owned[0],
        owned[1],
        owned[2],
        owned[3],
        owned[4],
        owned[5],
        owned[6],
        owned[7],
        owned[8],
    )


NY = 2
NEG = -1e30


def rcopy(src, dst, ss, rs, dev):
    return pltpu.make_async_remote_copy(src_ref=src, dst_ref=dst, send_sem=ss, recv_sem=rs, device_id=dev, device_id_type=MESH)


def dot_nt(a, b):
    return lax.dot_general(a, b, (((1,), (1,)), ((), ())), preferred_element_type=F32)


def dot(a, b):
    return lax.dot_general(a, b, (((1,), (0,)), ((), ())), preferred_element_type=F32)


def both(a, b):
    return jnp.logical_and(a, b)


class Gather:
    def __init__(self, ref, rows, nz, sems, fixed=None, cols=None):
        self.ref, self.rows, self.nz, self.fixed, self.cols = ref, rows, nz, fixed, cols
        self.zs, self.ys, self.xs, self.zr, self.yr, self.xr = sems
        s = lax.axis_index("shard")
        self.z, self.y, self.x = s // NY, s % NY, lax.axis_index("ctx")

    def view(self, c, rows):
        if self.cols is None:
            return self.ref.at[c, rows]
        return self.ref.at[self.fixed, rows, pl.ds(c * self.cols, self.cols)]

    def block(self, c, zz, yy):
        return self.view(c, pl.ds(pl.multiple_of((zz * NY + yy) * self.rows, 16), self.rows))

    def half(self, c, zz, yy, h):
        hr = self.rows // 2
        return self.view(c, pl.ds(pl.multiple_of((zz * NY + yy) * self.rows + h * hr, 16), hr))

    def up(self, c, zz):
        b = self.block(c, zz, self.y)
        return rcopy(b, b, self.zs.at[c, 0, zz], self.zr.at[c, zz], {"shard": (self.z + 1) * NY + self.y})

    def dn(self, c, zz):
        b = self.block(c, zz, self.y)
        return rcopy(b, b, self.zs.at[c, 1, zz], self.zr.at[c, zz], {"shard": (self.z - 1) * NY + self.y})

    def ycp(self, c, zz, yy, h):
        b = self.half(c, zz, yy, h)
        return rcopy(b, b, self.ys.at[c, zz], self.yr.at[c, zz], {"shard": self.z * NY + 1 - self.y})

    def xcp(self, c, zz, h):
        b = self.half(c, zz, 1 - self.y, h)
        return rcopy(b, b, self.xs.at[c, zz], self.xr.at[c, zz], {"ctx": 1 - self.x})

    def own(self, c):
        z, nz = self.z, self.nz

        @pl.when(z < nz - 1)
        def _():
            self.up(c, z).start()

        @pl.when(z > 0)
        def _():
            self.dn(c, z).start()

        self.ycp(c, z, self.y, self.x).start()

    def dirs(self, d):
        return ((self.z - d >= 0, self.z - d, True), (self.z + d < self.nz, self.z + d, False))

    def Z(self, c, d):
        z, nz = self.z, self.nz
        for ok, zz, isup in self.dirs(d):

            @pl.when(ok)
            def _():
                self.up(c, zz).wait_recv()
                if isup:
                    pl.when(z < nz - 1)(lambda: self.up(c, zz).start())
                else:
                    pl.when(z > 0)(lambda: self.dn(c, zz).start())
                self.ycp(c, zz, self.y, self.x).start()

    def each(self, d, f):
        if d == 0:
            f(self.z)
        else:
            for ok, zz, _ in self.dirs(d):
                pl.when(ok)(functools.partial(f, zz))

    def Y(self, c, d):
        def f(zz):
            self.ycp(c, zz, 1 - self.y, self.x).wait_recv()
            self.xcp(c, zz, self.x).start()

        self.each(d, f)

    def X(self, c, d):
        self.each(d, lambda zz: self.xcp(c, zz, 1 - self.x).wait_recv())

    def finish(self, c):
        z, nz = self.z, self.nz
        pl.when(z < nz - 1)(lambda: self.up(c, z).wait_send())
        pl.when(z > 0)(lambda: self.dn(c, z).wait_send())
        for d in range(1, nz):
            for ok, zz, isup in self.dirs(d):
                if isup:
                    pl.when(both(ok, z < nz - 1))(lambda: self.up(c, zz).wait_send())
                else:
                    pl.when(both(ok, z > 0))(lambda: self.dn(c, zz).wait_send())
        for zz in range(nz):
            self.ycp(c, zz, self.y, self.x).wait_send()
            self.xcp(c, zz, self.x).wait_send()

    @staticmethod
    def sems(nc, nz):
        D = pltpu.SemaphoreType.DMA
        return [D((nc, 2, nz)), D((nc, nz)), D((nc, nz)), D((nc, nz)), D((nc, nz)), D((nc, nz))]


class Scatter:
    view, block, half = Gather.view, Gather.block, Gather.half

    def __init__(self, ref, bufs, rows, nz, sems):
        self.ref, self.rows, self.nz, self.cols = ref, rows, nz, None
        self.xb, self.yb, self.zb, self.fb = bufs
        self.xs, self.ys, self.zs, self.fs, self.xr, self.yr, self.zr, self.fr = sems
        s = lax.axis_index("shard")
        self.z, self.y, self.x = s // NY, s % NY, lax.axis_index("ctx")

    def xcp(self, c, zz):
        return rcopy(self.half(c, zz, 1 - self.y, 1 - self.x), self.xb.at[c, zz], self.xs.at[c, zz], self.xr.at[c, zz], {"ctx": 1 - self.x})

    def ycp(self, c, zz):
        return rcopy(self.half(c, zz, 1 - self.y, self.x), self.yb.at[c, zz], self.ys.at[c, zz], self.yr.at[c, zz], {"shard": self.z * NY + 1 - self.y})

    def zcp(self, c, i, zz, src):
        to = self.z + 1 if i == 0 else self.z - 1
        slot = zz if i == 0 else jnp.where(zz == to, self.nz, zz)
        return rcopy(src, self.zb.at[c, slot], self.zs.at[c, i, zz], self.zr.at[c, i, zz], {"shard": to * NY + self.y})

    def fcp(self, c):
        return rcopy(self.fb.at[c, 0], self.fb.at[c, 1], self.fs.at[c], self.fr.at[c], {"ctx": 1 - self.x})

    def start(self, c):
        for zz in range(self.nz):
            self.xcp(c, zz).start()

    def X(self, c):
        for zz in range(self.nz):
            self.xcp(c, zz).wait_recv()
            h = self.half(c, zz, 1 - self.y, self.x)
            h[...] = (h[...].astype(F32) + self.xb[c, zz].astype(F32)).astype(BF)
            self.ycp(c, zz).start()

    def Y(self, c):
        z, nz = self.z, self.nz
        for zz in range(nz):
            self.ycp(c, zz).wait_recv()
            h = self.half(c, zz, self.y, self.x)
            h[...] = (h[...].astype(F32) + self.yb[c, zz].astype(F32)).astype(BF)
            if zz > 0:
                pl.when(z == 0)(lambda: self.zcp(c, 0, zz, self.block(c, zz, self.y)).start())
            if zz < nz - 1:
                pl.when(z == nz - 1)(lambda: self.zcp(c, 1, zz, self.block(c, zz, self.y)).start())

    def Z(self, c, k):
        z, nz = self.z, self.nz
        zm = nz - 1 - z
        for i, ok, zz in ((0, both(z >= 1, k >= z), nz - 1 - k + z), (1, both(zm >= 1, k >= zm), k - zm)):

            @pl.when(ok)
            def _():
                slot = zz if i == 0 else jnp.where(zz == z, nz, zz)
                ref = self.zb.at[c, slot]
                rcopy(ref, ref, self.zs.at[c, i, zz], self.zr.at[c, i, zz], {"ctx": self.x}).wait_recv()

                @pl.when(zz != z)
                def _():
                    ref[...] = (ref[...].astype(F32) + self.block(c, zz, self.y)[...].astype(F32)).astype(BF)
                    self.zcp(c, i, zz, ref).start()

    def F(self, c):
        z, nz = self.z, self.nz
        fb0 = self.fb.at[c, 0]
        fb0[...] = self.block(c, z, self.y)[...]

        @pl.when(z > 0)
        def _():
            fb0[...] = (fb0[...].astype(F32) + self.zb[c, z].astype(F32)).astype(BF)

        @pl.when(z < nz - 1)
        def _():
            fb0[...] = (fb0[...].astype(F32) + self.zb[c, nz].astype(F32)).astype(BF)

        self.fcp(c).start()

    def G(self, c):
        self.fcp(c).wait_recv()
        return self.fb[c, 0].astype(F32) + self.fb[c, 1].astype(F32)

    def finish(self, c):
        z, nz = self.z, self.nz
        for zz in range(nz):
            self.xcp(c, zz).wait_send()
            self.ycp(c, zz).wait_send()
            b = self.block(c, zz, self.y)
            pl.when(both(z < nz - 1, zz > z))(lambda: self.zcp(c, 0, zz, b).wait_send())
            pl.when(both(z > 0, zz < z))(lambda: self.zcp(c, 1, zz, b).wait_send())
        self.fcp(c).wait_send()

    @staticmethod
    def sems(nc, nz):
        D = pltpu.SemaphoreType.DMA
        return [D((nc, nz)), D((nc, nz)), D((nc, 2, nz)), D((nc,)), D((nc, nz)), D((nc, nz)), D((nc, 2, nz)), D((nc,))]


def block_kernel(names, nz, NC, half, BQ, *refs):
    w = types.SimpleNamespace(**dict(zip(names, refs)))
    T, D = w.hb.shape
    n = nz * NY
    rows = D // n
    hr = rows // 2
    FC = w.act.shape[2]
    CA = w.attd.shape[1]
    QO = NC
    npair = CA // 128
    nt = T // BQ
    sub = half // BQ
    s, x, t = lax.axis_index("shard"), lax.axis_index("ctx"), lax.axis_index("tp")
    me = x * n + s
    g = Gather(w.G, rows, nz, [getattr(w, f"ga{i}") for i in range(6)])
    gq = Gather(w.G, rows, nz, [getattr(w, f"gc{i}") for i in range(6)], QO, 256)
    gk = Gather(w.gkv, rows, nz, [getattr(w, f"gb{i}") for i in range(6)])
    r = Scatter(w.GR, (w.xb, w.yb, w.zb, w.fb), rows, nz, [getattr(w, f"sc{i}") for i in range(8)])
    rq = Scatter(w.GQ, (w.xq, w.yq, w.zq, w.fq), rows, nz, [getattr(w, f"sq{i}") for i in range(8)])
    lane = lax.broadcasted_iota(jnp.int32, (BQ, 128), 1)
    low = lane < 64

    def tile(i):
        return pl.ds(pl.multiple_of(i * BQ, BQ), BQ)

    own = pl.ds(pl.multiple_of(s * rows, 16), rows)
    loads = [(w.q, w.G.at[QO, own, pl.ds(0, CA)]), (w.o, w.G.at[QO, own, pl.ds(CA, CA)]), (w.kv, w.gkv.at[0, own]), (w.cot, w.cb), (w.hidden, w.hb)]
    for c in range(NC):
        loads.append((w.up.at[:, pl.ds(c * FC, FC)], w.G.at[c, own, pl.ds(0, FC)]))
        loads.append((w.dw.at[:, pl.ds(c * FC, FC)], w.G.at[c, own, pl.ds(FC, FC)]))
    loads = [pltpu.make_async_copy(a, b, w.lsem.at[i]) for i, (a, b) in enumerate(loads)]
    for c in loads:
        c.start()

    w.lb[s] = jnp.zeros((8, 128), F32)
    for k, ref in enumerate((w.g1, w.b1, w.g2, w.b2)):
        w.lb[s, k : k + 1, 0:rows] = ref[...].astype(F32)

    peers = [(s, 1 - x)] + [(lax.rem(s + k, n), xx) for k in range(1, n) for xx in (x, 1 - x)]
    bar = pltpu.get_barrier_semaphore()
    for ps, px in peers:
        pl.semaphore_signal(bar, inc=1, device_id={"shard": ps, "ctx": px}, device_id_type=MESH)
    pl.semaphore_signal(bar, inc=1, device_id={"tp": 1 - t}, device_id_type=MESH)
    for c in loads[:3]:
        c.wait()
    pl.semaphore_wait(bar, 2 * n)

    gk.own(0)
    lns = [rcopy(w.lb.at[s], w.lb.at[s], w.lns.at[k - 1], w.lnr.at[s], {"shard": lax.rem(s + k, n)}) for k in range(1, n)]
    for c in lns:
        c.start()
    for c in range(npair):
        gq.own(c)
    for c in loads[3:]:
        c.wait()

    first = jnp.minimum(w.bo[2 * x], w.bo[2 * x + 1])
    second = jnp.maximum(w.bo[2 * x], w.bo[2 * x + 1])
    swap = w.bo[2 * x] > w.bo[2 * x + 1]

    def pick(a, b):
        return jnp.where(swap, b, a)

    def flip(i):
        return lax.rem(i + sub, 2 * sub)

    @pl.loop(0, nt)
    def _(i):
        base = jnp.where(i < sub, first, second) * half + lax.rem(i, sub) * BQ
        pos = (base + lax.broadcasted_iota(jnp.int32, (BQ, 128), 0)).astype(F32)
        ang = pos * w.freq[0:1, :]
        l64 = lax.rem(lane, 64)
        w.tc[tile(i), :] = jnp.where(l64 < 16, jnp.cos(ang), 1.0)
        sn = jnp.sin(ang)
        w.ts[tile(i), :] = jnp.where(l64 < 8, -sn, jnp.where(l64 < 16, sn, 0.0))
        w.ct[:, tile(i)] = w.cb[tile(i), :].T

    def rotated(v, i, sign, layout=False):
        sw = jnp.where(lax.rem(lane, 16) < 8, pltpu.roll(v, 120, 1), pltpu.roll(v, 8, 1))
        cs, sn = w.tc[tile(i), :], w.ts[tile(i), :]
        if layout:
            cs, sn = pick(cs, w.tc[tile(flip(i)), :]), pick(sn, w.ts[tile(flip(i)), :])
        turn = sw * sn
        return v * cs + (turn if sign > 0 else -turn)

    pieces = [(gk, 0)] + [(gq, c) for c in range(npair)]

    def head(d):
        for e, c in pieces:
            if d < nz:
                e.Z(c, d)
            if d <= nz:
                e.Y(c, d - 1)
            if d > 1:
                e.X(c, d - 2)

    head(1)
    g.own(0)
    for k in range(1, n):
        f = lax.rem(s + n - k, n)
        rcopy(w.lb.at[f], w.lb.at[f], w.lns.at[0], w.lnr.at[f], {"shard": f}).wait_recv()
    prm = None
    for k in range(n):
        piece = jnp.concatenate([w.lb[k], jnp.zeros((8, D - 128), F32)], axis=1)
        piece = pltpu.roll(piece, k * rows, 1) if k else piece
        prm = piece if prm is None else prm + piece
    w.prm[...] = prm

    def standardized(i):
        v = w.hb[tile(i), :].astype(F32)
        v = v - jnp.mean(v, axis=1, keepdims=True)
        rstd = lax.rsqrt(jnp.mean(v * v, axis=1, keepdims=True) + 1e-05)
        return v * rstd, rstd

    @pl.loop(0, nt)
    def _(i):
        xh, _ = standardized(i)
        na = (xh * w.prm[0:1, :] + w.prm[1:2, :]).astype(BF)
        nf = (xh * w.prm[2:3, :] + w.prm[3:4, :]).astype(BF)
        w.na[tile(i), :] = na
        w.nf[tile(i), :] = nf
        w.nat[:, tile(i)] = na.T
        w.nft[:, tile(i)] = nf.T
        pl.when(i == 0)(lambda: head(2))
        pl.when(i == 2)(lambda: head(3))

    for d in range(4, nz + 2):
        head(d)

    def within(c, f):
        @pl.when(both(c >= 0, c < NC))
        def _():
            f(c)

    def even(a):
        within(a + 1, g.own)
        within(a - 2, lambda c: g.X(c, 3))
        within(a - 1, lambda c: (g.Z(c, 3), g.Y(c, 2), g.X(c, 1)))
        within(a, lambda c: (g.Z(c, 1), g.Y(c, 0)))

    def odd(a):
        within(a - 1, lambda c: (g.Y(c, 3), g.X(c, 2)))
        within(a, lambda c: (g.Z(c, 2), g.Y(c, 1), g.X(c, 0)))

    @pl.loop(0, nt)
    def _(i):
        kvp = dot(w.na[tile(i), :], w.gkv[0])
        w.kvb[0, tile(i), :] = jnp.where(low, rotated(kvp, i, 1, True), kvp).astype(BF)

    kvx = rcopy(w.kvb.at[0], w.kvb.at[1], w.es.at[0], w.er.at[0], {"ctx": 1 - x})
    kvx.start()
    kvo = pltpu.make_async_copy(w.kvb.at[0], w.kvout, w.osem.at[0])
    kvo.start()

    lane1 = lax.broadcasted_iota(jnp.int32, (1, 128), 1)

    @pl.loop(0, nt)
    def _(i):
        qp = dot(pick(w.na[tile(i), :], w.na[tile(flip(i)), :]), w.G[QO, :, 0:CA])
        ga = dot(pick(w.cb[tile(i), :], w.cb[tile(flip(i)), :]), w.G[QO, :, CA : 2 * CA])
        mine = jnp.where(i < sub, first, second)
        hide = jnp.zeros((1, 128), F32)
        for j in range(2):
            hide = jnp.where(lane1 == 64 + j, jnp.where(w.bo[2 * (1 - x) + j] <= mine, 0.0, NEG), hide)
        for p in range(npair):
            st = p * nt + i
            qs = rotated(qp[:, 128 * p : 128 * p + 128], i, 1).astype(BF).astype(F32) * 0.125
            w.qx[st, 0:BQ, :] = jnp.where(low, qs, hide).astype(BF)
            w.qx[st, BQ : 2 * BQ, :] = jnp.where(low, pltpu.roll(qs, 64, 1), hide).astype(BF)
            qt = qs.astype(BF).T
            w.qt[st, :, 0:BQ] = qt[:64]
            w.qt[st, :, BQ : 2 * BQ] = qt[64:]
            gp = ga[:, 128 * p : 128 * p + 128]
            w.dox[st, 0:BQ, :] = jnp.where(low, gp, 0.0).astype(BF)
            w.dox[st, BQ : 2 * BQ, :] = jnp.where(low, pltpu.roll(gp, 64, 1), 0.0).astype(BF)
            gt = gp.astype(BF).T
            w.dt[st, :, 0:BQ] = gt[:64]
            w.dt[st, :, BQ : 2 * BQ] = gt[64:]

    even(0)
    kvx.wait_recv()

    def keep_keys(i, kv, hot):
        kvf = kv.astype(F32)
        w.kx[tile(i), :] = jnp.where(low, kvf, hot).astype(BF)
        w.k0[tile(i), :] = jnp.where(low, kvf, 0.0).astype(BF)
        w.v0[tile(i), :] = jnp.where(low, pltpu.roll(kvf, 64, 1), 0.0).astype(BF)

    @pl.loop(0, nt)
    def _(i):
        keep_keys(i, pick(w.kvb[0, tile(i), :], w.kvb[0, tile(flip(i)), :]), 0.0)
        keep_keys(nt + i, w.kvb[1, tile(i), :], jnp.where(lane == 64 + i // sub, 1.0, 0.0))

    w.acc[...] = jnp.zeros_like(w.acc)
    dnx = rcopy(w.na, w.dnr, w.es.at[1], w.er.at[1], {"tp": 1 - t})

    def own_out(c, v):
        cols = pl.ds(pl.multiple_of(c * FC, FC), FC)
        w.ou[:, cols] = v[:, :FC]
        w.od[:, cols] = v[:, FC:]

    def pair_out(p):
        v = rq.G(p)
        w.oq[:, p * 128 : p * 128 + 128] = v[:, :128]
        w.oo[:, p * 128 : p * 128 + 128] = v[:, 128:]

    def pair_grads(p):
        cols = slice(p * 128, p * 128 + 128)
        for ref, src, to in ((w.nat, w.gq, 0), (w.ct, w.attd, 128)):
            a, b = src[0:half, cols], src[half:T, cols]
            v = dot(ref[:, 0:half], pick(a, b)) + dot(ref[:, half:T], pick(b, a))
            w.GQ[p, :, to : to + 128] = v.astype(BF)
        rq.start(p)

    def feed_forward():
        @pl.loop(0, NC)
        def _(c):
            @pl.loop(0, nt)
            def _(i):
                hp = dot(w.nf[tile(i), :], w.G[c, :, 0:FC])
                da = dot(w.cb[tile(i), :], w.G[c, :, FC : 2 * FC])
                cdf = 0.5 + 0.5 * lax.erf(hp * 0.7071067811865476)
                pdf = jnp.exp(-0.5 * hp * hp) * 0.3989422804014327
                w.act[c, tile(i), :] = (hp * cdf).astype(BF)
                w.dh[c, tile(i), :] = (da * (cdf + hp * pdf)).astype(BF)

                @pl.when(i == 2)
                def _():
                    odd(c + 2)
                    pl.when(c == 0)(lambda: rq.X(0))
                    pl.when(c == 1)(lambda: rq.Y(0))
                    pl.when(c == 2)(lambda: rq.Z(0, 1))
                    pl.when(c == 3)(lambda: rq.Z(0, 2))
                    pl.when(c >= 2)(lambda: r.X(c - 2))
                    pl.when(c >= 3)(lambda: r.Y(c - 3))

            @pl.loop(0, D // BQ)
            def _(m):
                w.GR[c, tile(m), 0:FC] = dot(w.nft[tile(m), :], w.dh[c]).astype(BF)
                w.GR[c, tile(m), FC : 2 * FC] = dot(w.ct[tile(m), :], w.act[c]).astype(BF)

            r.start(c)
            even(c + 3)

        @pl.loop(0, nt)
        def _(i):
            dn = dot_nt(w.dh[0, tile(i), :], w.G[0, :, 0:FC])
            br = dot_nt(w.act[0, tile(i), :], w.G[0, :, FC : 2 * FC])
            for c in range(1, NC):
                dn = dn + dot_nt(w.dh[c, tile(i), :], w.G[c, :, 0:FC])
                br = br + dot_nt(w.act[c, tile(i), :], w.G[c, :, FC : 2 * FC])
            w.na[tile(i), :] = dn.astype(BF)
            w.act[0, tile(i), :] = br[:, :FC].astype(BF)
            w.act[1, tile(i), :] = br[:, FC:].astype(BF)

            @pl.when(i == 2)
            def _():
                rq.Z(0, 3)
                rq.F(0)
                r.X(2)
                r.Y(1)

        dnx.start()

    def scatter_step(p, k):
        def last(c):
            r.Z(c, 3)
            r.F(c)

        def out(c):
            own_out(c, r.G(c))

        if p == 1:
            todo = {0: [(r.Z, 0, 1), (pair_out, 0)], 1: [(r.X, 3), (r.Y, 2), (r.Z, 0, 2)], 2: [(last, 0), (r.Z, 1, 1)], 3: [(r.Y, 3), (r.Z, 1, 2), (out, 0)]}
        else:
            todo = {0: [(last, 1), (r.Z, 2, 1)], 1: [(rq.X, 1), (r.Z, 2, 2), (out, 1)], 2: [(rq.Y, 1), (last, 2), (r.Z, 3, 1)], 3: [(rq.Z, 1, 1), (r.Z, 3, 2), (out, 2)]}
        for f, *a in todo[k]:
            f(*a)

    def attention(p, k):
        st = p * nt + k
        R = 2 * BQ
        b, rr = k // sub, k % sub
        spans = [(0, half, False)] if b else []
        spans += [(b * half + i * BQ, BQ, False) for i in range(rr)]
        spans += [(b * half + rr * BQ, BQ, True), (2 * half, half, False), (3 * half, half, False)]
        parts, at = [], 0
        for off, size, tri in spans:
            parts.append((slice(off, off + size), slice(at, at + size), tri))
            at += size
        q, do = w.qx[st], w.dox[st]
        m = None
        for ks, cs, tri in parts:
            sc = dot_nt(q, w.kx[ks, :])
            if tri:
                row = lax.rem(lax.broadcasted_iota(jnp.int32, (R, BQ), 0), BQ)
                sc = jnp.where(lax.broadcasted_iota(jnp.int32, (R, BQ), 1) <= row, sc, NEG)
            w.ss[:, cs] = sc
            for j in range(sc.shape[1] // 128):
                mj = sc[:, j * 128 : (j + 1) * 128]
                m = mj if m is None else jnp.maximum(m, mj)
        m = jnp.max(m, axis=1, keepdims=True)
        l = o = None
        for ks, cs, _ in parts:
            e = jnp.exp(w.ss[:, cs] - m)
            w.ss[:, cs] = e
            for j in range(e.shape[1] // 128):
                lj = e[:, j * 128 : (j + 1) * 128]
                l = lj if l is None else l + lj
            eb = e.astype(BF)
            w.ps[:, cs] = eb
            oj = dot(eb, w.v0[ks, :])
            o = oj if o is None else o + oj
        inv = 1.0 / jnp.sum(l, axis=1, keepdims=True)
        o = o * inv
        delta = jnp.sum(o * do.astype(F32), axis=1, keepdims=True)
        inv_row = jnp.transpose(jnp.broadcast_to(inv, (R, 128)))[:1, :]
        qs = (w.qt[st].astype(F32) * inv_row).astype(BF)
        dos = (w.dt[st].astype(F32) * inv_row).astype(BF)
        dq = None
        for ks, cs, _ in parts:
            dp = dot_nt(do, w.v0[ks, :])
            ds = (w.ss[:, cs] * (dp - delta)).astype(BF)
            dj = dot(ds, w.k0[ks, :])
            dq = dj if dq is None else dq + dj
            w.acc[0:64, ks] += dot(qs, ds)
            w.acc[64:128, ks] += dot(dos, w.ps[:, cs])
        dq = dq * (inv * 0.125)
        pair = pl.ds(pl.multiple_of(p * 128, 128), 128)
        at = slice(k * BQ, (k + 1) * BQ)
        w.attd[at, pair] = (o[:BQ] + pltpu.roll(o[BQ:], 64, 1)).astype(BF)
        w.gq[at, pair] = rotated(dq[:BQ] + pltpu.roll(dq[BQ:], 64, 1), k, -1).astype(BF)

    @pl.loop(0, npair)
    def _(p):
        @pl.when(p == 1)
        def _():
            pair_grads(0)
            feed_forward()

        pl.when(p == 2)(lambda: pair_grads(1))
        for k in range(nt):
            pl.when(p == 0)(lambda: (odd, even)[k % 2]((k + 1) // 2))
            for pp in range(1, npair):
                pl.when(p == pp)(functools.partial(scatter_step, pp, k))
            attention(p, k)

    for b in (0, 1):
        o = 1 - b
        w.dS[0, :, b * half : (b + 1) * half] = pick(w.acc[:, b * half : (b + 1) * half], w.acc[:, o * half : (o + 1) * half]).astype(BF)
    w.dS[1] = w.acc[:, T : 2 * T].astype(BF)
    dtp = rcopy(w.dS, w.dR, w.es.at[2], w.er.at[2], {"tp": 1 - t})
    dtp.start()
    pair_grads(2)
    dtp.wait_recv()
    w.dX[...] = (w.dS[1].astype(F32) + w.dR[1].astype(F32)).astype(BF)
    dxx = rcopy(w.dX, w.dXR, w.es.at[4], w.er.at[4], {"ctx": 1 - x})
    dxx.start()
    r.Z(3, 3)
    r.F(3)
    rq.Z(1, 2)
    dnx.wait_recv()

    @pl.loop(0, nt)
    def _(i):
        br = dot_nt(pick(w.attd[tile(i), :], w.attd[tile(flip(i)), :]), w.G[QO, :, CA : 2 * CA])
        w.act[0, tile(i), :] = (w.act[0, tile(i), :].astype(F32) + br[:, :FC]).astype(BF)
        w.act[1, tile(i), :] = (w.act[1, tile(i), :].astype(F32) + br[:, FC:]).astype(BF)

    brx = rcopy(w.act.at[pl.ds(0, 2)], w.dh.at[pl.ds(0, 2)], w.es.at[3], w.er.at[3], {"tp": 1 - t})
    brx.start()
    rq.X(2)

    @pl.loop(0, nt)
    def _(i):
        ga = dot_nt(pick(w.gq[tile(i), :], w.gq[tile(flip(i)), :]), w.G[QO, :, 0:CA])
        w.act[2, tile(i), :] = ga[:, :FC].astype(BF)
        w.act[3, tile(i), :] = ga[:, FC:].astype(BF)

    gax = rcopy(w.act.at[pl.ds(2, 2)], w.dh.at[pl.ds(2, 2)], w.es.at[5], w.er.at[5], {"tp": 1 - t})
    gax.start()
    rq.Z(1, 3)
    rq.F(1)
    rq.Y(2)
    brx.wait_recv()

    @pl.loop(0, nt)
    def _(i):
        for k in range(2):
            cs = slice(k * FC, (k + 1) * FC)
            v = w.act[k, tile(i), :].astype(F32) + w.dh[k, tile(i), :].astype(F32)
            w.nf[tile(i), cs] = (w.hb[tile(i), cs].astype(F32) + v).astype(BF)

    outx = pltpu.make_async_copy(w.nf, w.out_tokens, w.osem.at[1])
    outx.start()
    dxx.wait_recv()

    @pl.loop(0, nt)
    def _(i):
        v = w.dS[0, :, tile(i)].astype(F32) + w.dR[0, :, tile(i)].astype(F32) + w.dXR[:, tile(i)].astype(F32)
        v = v.T
        w.gkb[tile(i), :] = jnp.where(low, rotated(v, i, -1, True), v).astype(BF)

    w.kvS[...] = dot(w.nat[...], w.gkb[...]).astype(BF)

    def kv_rows(owner):
        return pl.ds(pl.multiple_of(owner * rows + t * hr, 16), hr)

    kvs = [rcopy(w.kvS.at[kv_rows(ps)], w.kvR.at[me], w.ks.at[i], w.kr.at[me], {"shard": ps, "ctx": px}) for i, (ps, px) in enumerate(peers)]
    for c in kvs:
        c.start()
    rq.Z(2, 1)
    gax.wait_recv()
    w.lg[...] = jnp.zeros_like(w.lg)

    def hgx(i):
        return pltpu.make_async_copy(w.hgs.at[tile(i)], w.hg.at[tile(i)], w.osem.at[2 + i])

    @pl.loop(0, nt)
    def _(i):
        xh, rstd = standardized(i)
        kvg = dot_nt(w.gkb[tile(i), :], w.gkv[0])
        gn = jnp.concatenate([w.act[k, tile(i), :].astype(F32) + w.dh[k, tile(i), :].astype(F32) for k in (2, 3)], axis=1) + kvg
        gf = w.na[tile(i), :].astype(F32) + w.dnr[tile(i), :].astype(F32)
        e = gn * w.prm[0:1, :] + gf * w.prm[2:3, :]
        e = rstd * (e - jnp.mean(e, axis=1, keepdims=True) - xh * jnp.mean(e * xh, axis=1, keepdims=True))
        w.hgs[tile(i), :] = w.cb[tile(i), :].astype(F32) + e
        hgx(i).start()
        w.lg[0:1, :] += jnp.sum(gn * xh, axis=0, keepdims=True)
        w.lg[1:2, :] += jnp.sum(gn, axis=0, keepdims=True)
        w.lg[2:3, :] += jnp.sum(gf * xh, axis=0, keepdims=True)
        w.lg[3:4, :] += jnp.sum(gf, axis=0, keepdims=True)
        pl.when(i == 2)(lambda: rq.Z(2, 2))

    lg = w.lg[...]
    keep = lax.broadcasted_iota(jnp.int32, (8, 128), 1) < rows
    for k in range(n):
        v = pltpu.roll(lg, D - k * rows, 1) if k else lg
        w.lS[k] = jnp.where(keep, v[:, :128], 0.0)
    lgs = [rcopy(w.lS.at[ps], w.lR.at[me], w.ls.at[i], w.lr.at[me], {"shard": ps, "ctx": px}) for i, (ps, px) in enumerate(peers)]
    for c in lgs:
        c.start()
    rq.Z(2, 3)
    rq.F(2)
    own_out(3, r.G(3))
    pair_out(1)

    def arrived(ref, sems, i, ps, px):
        k = px * n + ps
        return rcopy(ref.at[k], ref.at[k], sems.at[i], sems.at[k], {"shard": ps, "ctx": px})

    for i, (ps, px) in enumerate(peers):
        arrived(w.kvR, w.kr, i, ps, px).wait_recv()
    w.kvR[me] = w.kvS[kv_rows(s), :]
    v = w.kvR[0].astype(F32)
    for k in range(1, 2 * n):
        v = v + w.kvR[k].astype(F32)
    w.kvF[t] = v
    kfx = rcopy(w.kvF.at[t], w.kvF.at[t], w.es.at[6], w.er.at[6], {"tp": 1 - t})
    kfx.start()
    for i, (ps, px) in enumerate(peers):
        arrived(w.lR, w.lr, i, ps, px).wait_recv()
    w.lR[me] = w.lS[s]
    v = w.lR[0]
    for k in range(1, 2 * n):
        v = v + w.lR[k]
    w.lno[...] = v
    rcopy(w.kvF.at[1 - t], w.kvF.at[1 - t], w.es.at[6], w.er.at[6], {"tp": 1 - t}).wait_recv()
    w.okv[0:hr, :] = w.kvF[0]
    w.okv[hr:rows, :] = w.kvF[1]
    pair_out(2)
    kvo.wait()
    outx.wait()
    for i in range(nt):
        hgx(i).wait()
    for c in lns + [kvx, dnx, dtp, brx, dxx, gax, kfx] + kvs + lgs:
        c.wait_send()
    gk.finish(0)
    for c in range(npair):
        gq.finish(c)
        rq.finish(c)
    for c in range(NC):
        g.finish(c)
        r.finish(c)


def block_call(bo, freq, hidden, cot, lns, up, dw, q, o, kv, nz, half, cid):
    T, D = hidden.shape
    rows, CU = up.shape
    CA, CK = q.shape[1], kv.shape[1]
    FC = CA
    NC = CU // FC
    n = nz * NY
    hr = rows // 2
    BQ = 256
    npair = CA // 128
    ns = T // BQ * npair
    A = pl.BlockSpec(memory_space=pl.ANY)
    V = pl.BlockSpec(memory_space=pltpu.VMEM)
    S = pl.BlockSpec(memory_space=pltpu.SMEM)
    Dm = pltpu.SemaphoreType.DMA
    ins = ["bo", "freq", "g1", "b1", "g2", "b2", "hidden", "cot", "up", "dw", "q", "o", "kv"]
    sd = jax.ShapeDtypeStruct
    outs = {
        "out_tokens": (sd((T, D), BF), A), "kvout": (sd((T, CK), BF), A), "hg": (sd((T, D), F32), A),
        "lno": (sd((8, 128), F32), V), "oq": (sd((rows, CA), F32), V), "okv": (sd((rows, CK), F32), V), "oo": (sd((rows, CA), F32), V),
        "ou": (sd((rows, CU), F32), V), "od": (sd((rows, CU), F32), V),
    }
    b = lambda *sh: pltpu.VMEM(sh, BF)
    f = lambda *sh: pltpu.VMEM(sh, F32)
    scr = {
        "hb": b(T, D), "cb": b(T, D), "ct": b(D, T), "na": b(T, D), "nf": b(T, D), "nft": b(D, T), "nat": b(D, T),
        "G": b(NC + 1, D, 2 * FC), "gkv": b(1, D, CK), "GR": b(NC, D, 2 * FC), "GQ": b(npair, D, 256),
        "xb": b(NC, nz, hr, 2 * FC), "yb": b(NC, nz, hr, 2 * FC), "zb": b(NC, nz + 1, rows, 2 * FC), "fb": b(NC, 2, rows, 2 * FC),
        "xq": b(npair, nz, hr, 256), "yq": b(npair, nz, hr, 256), "zq": b(npair, nz + 1, rows, 256), "fq": b(npair, 2, rows, 256),
        "lb": f(n, 8, 128), "act": b(NC, T, FC), "dh": b(NC, T, FC), "dnr": b(T, D),
        "qx": b(ns, 2 * BQ, 128), "dox": b(ns, 2 * BQ, 128), "qt": b(ns, 64, 2 * BQ), "dt": b(ns, 64, 2 * BQ),
        "kvb": b(2, T, CK), "kx": b(2 * T, 128), "k0": b(2 * T, 128), "v0": b(2 * T, 128),
        "ss": f(2 * BQ, 2 * T), "ps": b(2 * BQ, 2 * T), "attd": b(T, CA), "gq": b(T, CA), "acc": f(128, 2 * T),
        "tc": f(T, 128), "ts": f(T, 128), "dS": b(2, 128, T), "dR": b(2, 128, T), "dX": b(128, T), "dXR": b(128, T), "gkb": b(T, 128),
        "kvS": b(D, CK), "kvR": b(2 * n, hr, CK), "kvF": f(2, hr, CK), "lS": f(n, 8, 128), "lR": f(2 * n, 8, 128), "prm": f(8, D), "lg": f(8, D), "hgs": f(T, D),
        "lsem": Dm((5 + 2 * NC,)), "lns": Dm((n - 1,)), "lnr": Dm((n,)), "es": Dm((7,)), "er": Dm((7,)), "osem": Dm((2 + T // BQ,)),
        "ks": Dm((2 * n - 1,)), "kr": Dm((2 * n,)), "ls": Dm((2 * n - 1,)), "lr": Dm((2 * n,)),
    }
    scr.update({f"ga{i}": v for i, v in enumerate(Gather.sems(NC, nz))})
    scr.update({f"gb{i}": v for i, v in enumerate(Gather.sems(1, nz))})
    scr.update({f"gc{i}": v for i, v in enumerate(Gather.sems(npair, nz))})
    scr.update({f"sc{i}": v for i, v in enumerate(Scatter.sems(NC, nz))})
    scr.update({f"sq{i}": v for i, v in enumerate(Scatter.sems(npair, nz))})
    names = ins + list(outs) + list(scr)
    res = pl.pallas_call(
        functools.partial(block_kernel, names, nz, NC, half, BQ),
        out_shape=tuple(v[0] for v in outs.values()),
        in_specs=[S, V, V, V, V, V] + [A] * 7,
        out_specs=tuple(v[1] for v in outs.values()),
        scratch_shapes=list(scr.values()),
        compiler_params=pltpu.CompilerParams(collective_id=cid, has_side_effects=True, vmem_limit_bytes=67043328),
        name="block",
    )(bo, freq, *lns, hidden, cot, up, dw, q, o, kv)
    return dict(zip(outs, res))


def results_kernel(nt, tok, hg, kv, lno, oq, okv, oo, ou, od, tok_o, k_o, v_o, hg_o, a_o, b_o, c_o, d_o, oq_o, okv_o, oo_o, ou_o, od_o, tb, hb, sin, sout):
    BQ = tok.shape[0] // nt
    moves = []
    for i in range(nt):
        t = pl.ds(i * BQ, BQ)
        moves.append((hg.at[t], hb.at[t], hg_o.at[t]))
        moves.append((tok.at[t], tb.at[t], tok_o.at[t]))
    ins = [pltpu.make_async_copy(a, b, sin.at[i]) for i, (a, b, _) in enumerate(moves)]
    outs = [pltpu.make_async_copy(b, c, sout.at[i]) for i, (_, b, c) in enumerate(moves)]
    for c in ins:
        c.start()
    for a, b in zip(ins, outs):
        a.wait()
        b.start()
    k_o[...] = kv[:, :64]
    v_o[...] = pltpu.roll(kv[...].astype(F32), 64, 1)[:, :64].astype(BF)
    for k, ref in enumerate((a_o, b_o, c_o, d_o)):
        ref[...] = lno[k, : ref.shape[0]]
    for a, b in ((oq, oq_o), (okv, okv_o), (oo, oo_o), (ou, ou_o), (od, od_o)):
        b[...] = a[...]
    for c in outs:
        c.wait()


def results(v, rows):
    T, D = v["hg"].shape
    A = pl.BlockSpec(memory_space=pl.ANY)
    V = pl.BlockSpec(memory_space=pltpu.VMEM)
    sd = jax.ShapeDtypeStruct
    like = lambda k: sd(v[k].shape, v[k].dtype)
    nt = 4
    Dm = pltpu.SemaphoreType.DMA
    order = ("out_tokens", "hg", "kvout", "lno", "oq", "okv", "oo", "ou", "od")
    return pl.pallas_call(
        functools.partial(results_kernel, nt),
        out_shape=(like("out_tokens"), sd((T, 64), BF), sd((T, 64), BF), like("hg")) + (sd((rows,), F32),) * 4 + tuple(like(k) for k in order[4:]),
        in_specs=[A, A] + [V] * 7,
        out_specs=(A, V, V, A) + (V,) * 9,
        scratch_shapes=[pltpu.VMEM((T, D), BF), pltpu.VMEM((T, D), F32), Dm((2 * nt,)), Dm((2 * nt,))],
        name="results",
    )(*[v[k] for k in order])


def fits(mesh):
    return mesh.shape["shard"] == 8 and mesh.shape["ctx"] == 2


def fast_device(hidden, block_order, ln1_gain, ln1_bias, ln2_gain, ln2_bias, q_weight, kv_weight, o_weight, up_weight, down_weight, cotangent):
    seqs, span, width = hidden.shape
    rows = ln1_gain.shape[0]
    freq = 10000.0 ** (-2.0 * (np.arange(128) % (ROT // 2)) / ROT)
    freq = jnp.asarray(np.broadcast_to(freq, (8, 128)), F32)
    lns = [a.reshape(1, rows) for a in (ln1_gain, ln1_bias, ln2_gain, ln2_bias)]
    v = block_call(block_order, freq, hidden.reshape(span, width), cotangent.reshape(span, width), lns, up_weight, down_weight, q_weight, o_weight, kv_weight, width // rows // NY, span // 2, 1)
    tok, keys, values, hg, a, b, c, d, oq, okv, oo, ou, od = results(v, rows)
    return (tok[None], keys[None], values[None], hg[None], a, b, c, d, oq, okv, oo, ou, od)


def solution(mesh):
    return jax.shard_map(
        fast_device if fits(mesh) else on_device,
        mesh=mesh,
        in_specs=(
            P("shard", "ctx", None),
            P(),
            P("shard"),
            P("shard"),
            P("shard"),
            P("shard"),
            P("shard", "tp"),
            P("shard", None),
            P("shard", "tp"),
            P("shard", "tp"),
            P("shard", "tp"),
            P("shard", "ctx", None),
        ),
        out_specs=(
            P("shard", "ctx", None),
            P("shard", "ctx", None),
            P("shard", "ctx", None),
            P("shard", "ctx", None),
            P("shard"),
            P("shard"),
            P("shard"),
            P("shard"),
            P("shard", "tp"),
            P("shard", None),
            P("shard", "tp"),
            P("shard", "tp"),
            P("shard", "tp"),
        ),
        check_vma=False,
    )
```

```python
import functools
import types

import jax
import jax.numpy as jnp
import numpy as np
from jax import lax
from jax.experimental import pallas as pl
from jax.experimental.pallas import tpu as pltpu
from jax.sharding import PartitionSpec as P

F32 = jnp.float32
BF = jnp.bfloat16
MESH = pl.DeviceIdType.MESH

ROT = 16


def layer_norm(values, gain, shift):
    center = values - jnp.mean(values, axis=-1, keepdims=True)
    spread = jnp.mean(center * center, axis=-1, keepdims=True)
    return center * lax.rsqrt(spread + 1e-05) * gain + shift


def gelu_exact(values):
    return jax.nn.gelu(values, approximate=False)


def rotate(tensor, places, sign):
    half_rot = ROT // 2
    freq = jnp.power(10000.0, -2.0 * jnp.arange(half_rot, dtype=jnp.float32) / ROT)
    angle = places.astype(jnp.float32)[:, None] * freq[None, :]
    cosine = jnp.cos(angle)[:, None, :]
    sine = sign * jnp.sin(angle)[:, None, :]
    first = tensor[..., :half_rot]
    second = tensor[..., half_rot:ROT]
    return jnp.concatenate(
        [first * cosine - second * sine, second * cosine + first * sine, tensor[..., ROT:]], axis=-1
    )


def tok_positions(block_order, rows, half_block):
    index = rows // half_block
    table = jnp.arange(block_order.shape[0], dtype=jnp.int32)
    picked = jnp.sum(jnp.where(index[:, None] == table[None, :], block_order[None, :], 0), axis=1)
    return picked * half_block + rows % half_block


def right_product(left, right):
    return lax.dot_general(
        left, right, (((1,), (1,)), ((), ())), preferred_element_type=jnp.float32
    )


def left_product(left, right):
    return lax.dot_general(
        left, right, (((0,), (0,)), ((), ())), preferred_element_type=jnp.float32
    )


def on_device(
    hidden,
    block_order,
    ln1_gain,
    ln1_bias,
    ln2_gain,
    ln2_bias,
    q_weight,
    kv_weight,
    o_weight,
    up_weight,
    down_weight,
    cotangent,
):
    seqs, span, width = hidden.shape
    half_block = span // 2
    head_size = kv_weight.shape[1] // 2
    local_heads = q_weight.shape[1] // head_size
    row_count = seqs * span
    query_rows = span * local_heads
    scale = head_size ** (-0.5)
    gathered = (
        lax.all_gather(ln1_gain, "shard", axis=0, tiled=True),
        lax.all_gather(ln1_bias, "shard", axis=0, tiled=True),
        lax.all_gather(ln2_gain, "shard", axis=0, tiled=True),
        lax.all_gather(ln2_bias, "shard", axis=0, tiled=True),
        lax.all_gather(q_weight, "shard", axis=0, tiled=True),
        lax.all_gather(kv_weight, "shard", axis=0, tiled=True),
        lax.all_gather(o_weight, "shard", axis=0, tiled=True),
        lax.all_gather(up_weight, "shard", axis=0, tiled=True),
        lax.all_gather(down_weight, "shard", axis=0, tiled=True),
    )
    gain_attn, bias_attn, gain_ffn, bias_ffn, w_query, w_keyval, w_output, w_up, w_down = gathered
    offset = lax.axis_index("ctx") * span
    query_places = tok_positions(
        block_order, offset + jnp.arange(span, dtype=jnp.int32), half_block
    )
    row_places = jnp.repeat(query_places, local_heads)
    tokens = hidden.astype(jnp.float32).reshape(row_count, width)
    norm_attn = layer_norm(
        tokens, gain_attn.astype(jnp.float32), bias_attn.astype(jnp.float32)
    ).astype(jnp.bfloat16)
    norm_ffn = layer_norm(
        tokens, gain_ffn.astype(jnp.float32), bias_ffn.astype(jnp.float32)
    ).astype(jnp.bfloat16)
    query_pre = jnp.dot(norm_attn, w_query, preferred_element_type=jnp.float32).reshape(
        seqs, span, local_heads, head_size
    )
    queries = (
        rotate(query_pre, query_places, 1.0)
        .astype(jnp.bfloat16)
        .reshape(seqs, query_rows, head_size)
    )
    keyval_pre = jnp.dot(norm_attn, w_keyval, preferred_element_type=jnp.float32).reshape(
        seqs, span, 2 * head_size
    )
    keys = rotate(keyval_pre[:, :, None, :head_size], query_places, 1.0)[:, :, 0, :].astype(
        jnp.bfloat16
    )
    values = keyval_pre[:, :, head_size:].astype(jnp.bfloat16)
    start_state = (
        jnp.full((seqs, query_rows), -1e30, jnp.float32),
        jnp.zeros((seqs, query_rows), jnp.float32),
        jnp.zeros((seqs, query_rows, head_size), jnp.float32),
    )
    key_piece = lax.all_gather(keys, "ctx", axis=1, tiled=True)
    value_piece = lax.all_gather(values, "ctx", axis=1, tiled=True)
    count = key_piece.shape[1]
    key_places = tok_positions(block_order, jnp.arange(count, dtype=jnp.int32), half_block)
    visible = key_places[None, :] <= row_places[:, None]

    def one_block(args):
        peak, total, accum, query_block, key_block, value_block = args
        scores = (
            jnp.einsum("qd,kd->qk", query_block, key_block, preferred_element_type=jnp.float32)
            * scale
        )
        scores = jnp.where(visible, scores, -1e30)
        new_peak = jnp.maximum(peak, jnp.max(scores, axis=1))
        factor = jnp.exp(peak - new_peak)
        weights = jnp.where(visible, jnp.exp(scores - new_peak[:, None]), 0.0)
        total = total * factor + jnp.sum(weights, axis=1)
        accum = accum * factor[:, None] + jnp.einsum(
            "qk,kd->qd",
            weights.astype(jnp.bfloat16),
            value_block,
            preferred_element_type=jnp.float32,
        )
        return (new_peak, total, accum)

    peak, total, accum = lax.map(
        one_block, (start_state[0], start_state[1], start_state[2], queries, key_piece, value_piece)
    )
    attended = (
        (accum / total[:, :, None]).astype(jnp.bfloat16).reshape(row_count, local_heads * head_size)
    )
    log_total = peak + jnp.log(total)
    hidden_pre = jnp.dot(norm_ffn, w_up, preferred_element_type=jnp.float32)
    activation_full, gelu_pull = jax.vjp(gelu_exact, hidden_pre)
    activation = activation_full.astype(jnp.bfloat16)
    branch = right_product(attended, w_output) + right_product(activation, w_down)
    branch = lax.psum(branch.astype(jnp.bfloat16), "tp").astype(jnp.float32)
    mixed = (tokens + branch).astype(jnp.bfloat16).reshape(seqs, span, width)
    regathered = (
        lax.all_gather(ln1_gain, "shard", axis=0, tiled=True),
        lax.all_gather(ln2_gain, "shard", axis=0, tiled=True),
        lax.all_gather(q_weight, "shard", axis=0, tiled=True),
        lax.all_gather(kv_weight, "shard", axis=0, tiled=True),
        lax.all_gather(o_weight, "shard", axis=0, tiled=True),
        lax.all_gather(up_weight, "shard", axis=0, tiled=True),
        lax.all_gather(down_weight, "shard", axis=0, tiled=True),
    )
    gain_attn, gain_ffn, w_query, w_keyval, w_output, w_up, w_down = regathered
    grad_out = cotangent.reshape(row_count, width)
    grad_attended = (
        jnp.dot(grad_out, w_output, preferred_element_type=jnp.float32)
        .astype(jnp.bfloat16)
        .reshape(seqs, query_rows, head_size)
    )
    grad_activation = jnp.dot(grad_out, w_down, preferred_element_type=jnp.float32)
    grad_hidden = gelu_pull(grad_activation)[0].astype(jnp.bfloat16)
    grad_w_output = left_product(grad_out, attended)
    grad_w_down = left_product(grad_out, activation)
    grad_w_up = left_product(norm_ffn, grad_hidden)
    grad_norm_ffn = right_product(grad_hidden, w_up)
    all_keys, all_values = (
        lax.all_gather(keys, "ctx", axis=1, tiled=True),
        lax.all_gather(values, "ctx", axis=1, tiled=True),
    )
    key_count = all_keys.shape[1]
    key_places = tok_positions(block_order, jnp.arange(key_count, dtype=jnp.int32), half_block)
    visible_all = key_places[None, :] <= row_places[:, None]

    def backward_one(args):
        query_block, key_block, value_block, grad_block, log_block = args
        scores = (
            jnp.einsum("qd,kd->qk", query_block, key_block, preferred_element_type=jnp.float32)
            * scale
        )
        probs = jnp.where(visible_all, jnp.exp(scores - log_block[:, None]), 0.0)
        grad_probs = jnp.einsum(
            "qd,kd->qk", grad_block, value_block, preferred_element_type=jnp.float32
        )
        delta = jnp.sum(probs * grad_probs, axis=1, keepdims=True)
        grad_scores = (probs * (grad_probs - delta)).astype(jnp.bfloat16)
        grad_query = (
            jnp.einsum("qk,kd->qd", grad_scores, key_block, preferred_element_type=jnp.float32)
            * scale
        )
        grad_key = (
            jnp.einsum("qk,qd->kd", grad_scores, query_block, preferred_element_type=jnp.float32)
            * scale
        )
        grad_value = jnp.einsum(
            "qk,qd->kd", probs.astype(jnp.bfloat16), grad_block, preferred_element_type=jnp.float32
        )
        return (grad_query, jnp.concatenate([grad_key, grad_value], axis=1))

    grad_queries, grad_keyvals = lax.map(
        backward_one, (queries, all_keys, all_values, grad_attended, log_total)
    )
    grad_keyvals = lax.psum_scatter(
        grad_keyvals.astype(jnp.bfloat16), "ctx", scatter_dimension=1, tiled=True
    ).astype(jnp.float32)
    grad_keyvals = lax.psum(grad_keyvals.astype(jnp.bfloat16), "tp").astype(jnp.float32)
    grad_key_pre = rotate(grad_keyvals[:, :, None, :head_size], query_places, -1.0)[:, :, 0, :]
    grad_keyval_pre = (
        jnp.concatenate([grad_key_pre, grad_keyvals[:, :, head_size:]], axis=2)
        .astype(jnp.bfloat16)
        .reshape(row_count, 2 * head_size)
    )
    grad_query_pre = (
        rotate(grad_queries.reshape(seqs, span, local_heads, head_size), query_places, -1.0)
        .astype(jnp.bfloat16)
        .reshape(row_count, local_heads * head_size)
    )
    grad_w_query = left_product(norm_attn, grad_query_pre)
    grad_w_keyval = left_product(norm_attn, grad_keyval_pre)
    grad_norm_attn = right_product(grad_query_pre, w_query)
    shared_term = right_product(grad_keyval_pre, w_keyval)
    zero_shift = jnp.zeros((width,), jnp.float32)
    attn_pull = jax.vjp(layer_norm, tokens, gain_attn.astype(jnp.float32), zero_shift)[1]
    ffn_pull = jax.vjp(layer_norm, tokens, gain_ffn.astype(jnp.float32), zero_shift)[1]
    grad_norm_attn, grad_norm_ffn = (
        lax.psum(grad_norm_attn.astype(jnp.bfloat16), "tp").astype(jnp.float32),
        lax.psum(grad_norm_ffn.astype(jnp.bfloat16), "tp").astype(jnp.float32),
    )
    grad_norm_attn = grad_norm_attn + shared_term
    grad_tok_attn, grad_gain_attn, grad_shift_attn = attn_pull(grad_norm_attn)
    grad_tok_ffn, grad_gain_ffn, grad_shift_ffn = ffn_pull(grad_norm_ffn)
    grad_tok_norms = grad_tok_attn + grad_tok_ffn
    grad_tokens = (grad_out.astype(jnp.float32) + grad_tok_norms).reshape(seqs, span, width)
    grads = (
        grad_gain_attn,
        grad_shift_attn,
        grad_gain_ffn,
        grad_shift_ffn,
        grad_w_query,
        grad_w_keyval,
        grad_w_output,
        grad_w_up,
        grad_w_down,
    )
    owned = (
        lax.psum_scatter(
            grads[0].astype(jnp.bfloat16), "shard", scatter_dimension=0, tiled=True
        ).astype(jnp.float32),
        lax.psum_scatter(
            grads[1].astype(jnp.bfloat16), "shard", scatter_dimension=0, tiled=True
        ).astype(jnp.float32),
        lax.psum_scatter(
            grads[2].astype(jnp.bfloat16), "shard", scatter_dimension=0, tiled=True
        ).astype(jnp.float32),
        lax.psum_scatter(
            grads[3].astype(jnp.bfloat16), "shard", scatter_dimension=0, tiled=True
        ).astype(jnp.float32),
        lax.psum_scatter(
            grads[4].astype(jnp.bfloat16), "shard", scatter_dimension=0, tiled=True
        ).astype(jnp.float32),
        lax.psum_scatter(
            grads[5].astype(jnp.bfloat16), "shard", scatter_dimension=0, tiled=True
        ).astype(jnp.float32),
        lax.psum_scatter(
            grads[6].astype(jnp.bfloat16), "shard", scatter_dimension=0, tiled=True
        ).astype(jnp.float32),
        lax.psum_scatter(
            grads[7].astype(jnp.bfloat16), "shard", scatter_dimension=0, tiled=True
        ).astype(jnp.float32),
        lax.psum_scatter(
            grads[8].astype(jnp.bfloat16), "shard", scatter_dimension=0, tiled=True
        ).astype(jnp.float32),
    )
    owned = (
        lax.psum(owned[0].astype(jnp.bfloat16), "ctx").astype(jnp.float32),
        lax.psum(owned[1].astype(jnp.bfloat16), "ctx").astype(jnp.float32),
        lax.psum(owned[2].astype(jnp.bfloat16), "ctx").astype(jnp.float32),
        lax.psum(owned[3].astype(jnp.bfloat16), "ctx").astype(jnp.float32),
        lax.psum(owned[4].astype(jnp.bfloat16), "ctx").astype(jnp.float32),
        lax.psum(owned[5].astype(jnp.bfloat16), "ctx").astype(jnp.float32),
        lax.psum(owned[6].astype(jnp.bfloat16), "ctx").astype(jnp.float32),
        lax.psum(owned[7].astype(jnp.bfloat16), "ctx").astype(jnp.float32),
        lax.psum(owned[8].astype(jnp.bfloat16), "ctx").astype(jnp.float32),
    )
    return (
        mixed,
        keys,
        values,
        grad_tokens,
        owned[0],
        owned[1],
        owned[2],
        owned[3],
        owned[4],
        owned[5],
        owned[6],
        owned[7],
        owned[8],
    )


NY = 2
NEG = -1e30


def rcopy(src, dst, ss, rs, dev):
    return pltpu.make_async_remote_copy(src_ref=src, dst_ref=dst, send_sem=ss, recv_sem=rs, device_id=dev, device_id_type=MESH)


def dot_nt(a, b):
    return lax.dot_general(a, b, (((1,), (1,)), ((), ())), preferred_element_type=F32)


def dot(a, b):
    return lax.dot_general(a, b, (((1,), (0,)), ((), ())), preferred_element_type=F32)


def both(a, b):
    return jnp.logical_and(a, b)


class Gather:
    def __init__(self, ref, rows, nz, sems, fixed=None, cols=None):
        self.ref, self.rows, self.nz, self.fixed, self.cols = ref, rows, nz, fixed, cols
        self.zs, self.ys, self.xs, self.zr, self.yr, self.xr = sems
        s = lax.axis_index("shard")
        self.z, self.y, self.x = s // NY, s % NY, lax.axis_index("ctx")

    def view(self, c, rows):
        if self.cols is None:
            return self.ref.at[c, rows]
        return self.ref.at[self.fixed, rows, pl.ds(c * self.cols, self.cols)]

    def block(self, c, zz, yy):
        return self.view(c, pl.ds(pl.multiple_of((zz * NY + yy) * self.rows, 16), self.rows))

    def half(self, c, zz, yy, h):
        hr = self.rows // 2
        return self.view(c, pl.ds(pl.multiple_of((zz * NY + yy) * self.rows + h * hr, 16), hr))

    def up(self, c, zz):
        b = self.block(c, zz, self.y)
        return rcopy(b, b, self.zs.at[c, 0, zz], self.zr.at[c, zz], {"shard": (self.z + 1) * NY + self.y})

    def dn(self, c, zz):
        b = self.block(c, zz, self.y)
        return rcopy(b, b, self.zs.at[c, 1, zz], self.zr.at[c, zz], {"shard": (self.z - 1) * NY + self.y})

    def ycp(self, c, zz, yy, h):
        b = self.half(c, zz, yy, h) if self.cols is None else self.block(c, zz, yy)
        return rcopy(b, b, self.ys.at[c, zz], self.yr.at[c, zz], {"shard": self.z * NY + 1 - self.y})

    def xcp(self, c, zz, h):
        b = self.half(c, zz, 1 - self.y, h)
        return rcopy(b, b, self.xs.at[c, zz], self.xr.at[c, zz], {"ctx": 1 - self.x})

    def own(self, c):
        z, nz = self.z, self.nz

        @pl.when(z < nz - 1)
        def _():
            self.up(c, z).start()

        @pl.when(z > 0)
        def _():
            self.dn(c, z).start()

        self.ycp(c, z, self.y, self.x).start()

    def dirs(self, d):
        return ((self.z - d >= 0, self.z - d, True), (self.z + d < self.nz, self.z + d, False))

    def Z(self, c, d):
        z, nz = self.z, self.nz
        for ok, zz, isup in self.dirs(d):

            @pl.when(ok)
            def _():
                self.up(c, zz).wait_recv()
                if isup:
                    pl.when(z < nz - 1)(lambda: self.up(c, zz).start())
                else:
                    pl.when(z > 0)(lambda: self.dn(c, zz).start())
                self.ycp(c, zz, self.y, self.x).start()

    def each(self, d, f):
        if d == 0:
            f(self.z)
        else:
            for ok, zz, _ in self.dirs(d):
                pl.when(ok)(functools.partial(f, zz))

    def Y(self, c, d):
        def f(zz):
            self.ycp(c, zz, 1 - self.y, self.x).wait_recv()
            if self.cols is None:
                self.xcp(c, zz, self.x).start()

        self.each(d, f)

    def X(self, c, d):
        self.each(d, lambda zz: self.xcp(c, zz, 1 - self.x).wait_recv())

    def stage(self, c, d):
        if d < self.nz:
            self.Z(c, d)
        if d <= self.nz:
            self.Y(c, d - 1)
        if d > 1 and self.cols is None:
            self.X(c, d - 2)

    def finish(self, c):
        z, nz = self.z, self.nz
        pl.when(z < nz - 1)(lambda: self.up(c, z).wait_send())
        pl.when(z > 0)(lambda: self.dn(c, z).wait_send())
        for d in range(1, nz):
            for ok, zz, isup in self.dirs(d):
                if isup:
                    pl.when(both(ok, z < nz - 1))(lambda: self.up(c, zz).wait_send())
                else:
                    pl.when(both(ok, z > 0))(lambda: self.dn(c, zz).wait_send())
        for zz in range(nz):
            self.ycp(c, zz, self.y, self.x).wait_send()
            if self.cols is None:
                self.xcp(c, zz, self.x).wait_send()

    @staticmethod
    def sems(nc, nz):
        D = pltpu.SemaphoreType.DMA
        return [D((nc, 2, nz)), D((nc, nz)), D((nc, nz)), D((nc, nz)), D((nc, nz)), D((nc, nz))]


class Scatter:
    view, block, half = Gather.view, Gather.block, Gather.half

    def __init__(self, ref, bufs, rows, nz, sems):
        self.ref, self.rows, self.nz, self.cols = ref, rows, nz, None
        self.xb, self.yb, self.zb, self.fb = bufs
        self.xs, self.ys, self.zs, self.fs, self.xr, self.yr, self.zr, self.fr = sems
        s = lax.axis_index("shard")
        self.z, self.y, self.x = s // NY, s % NY, lax.axis_index("ctx")

    def xcp(self, c, zz):
        return rcopy(self.half(c, zz, 1 - self.y, 1 - self.x), self.xb.at[c, zz], self.xs.at[c, zz], self.xr.at[c, zz], {"ctx": 1 - self.x})

    def ycp(self, c, zz):
        return rcopy(self.half(c, zz, 1 - self.y, self.x), self.yb.at[c, zz], self.ys.at[c, zz], self.yr.at[c, zz], {"shard": self.z * NY + 1 - self.y})

    def zcp(self, c, i, zz, src):
        to = self.z + 1 if i == 0 else self.z - 1
        slot = zz if i == 0 else jnp.where(zz == to, self.nz, zz)
        return rcopy(src, self.zb.at[c, slot], self.zs.at[c, i, zz], self.zr.at[c, i, zz], {"shard": to * NY + self.y})

    def fcp(self, c):
        return rcopy(self.fb.at[c, 0], self.fb.at[c, 1], self.fs.at[c], self.fr.at[c], {"ctx": 1 - self.x})

    def far(self, j):
        return jnp.where(self.z < self.nz // 2, self.nz - 1 - j, j)

    def start(self, c):
        for j in range(self.nz):
            self.xcp(c, self.far(j)).start()

    def X(self, c, j0=0, count=None):
        for j in range(j0, j0 + (count or self.nz)):
            zz = self.far(j)
            self.xcp(c, zz).wait_recv()
            h = self.half(c, zz, 1 - self.y, self.x)
            h[...] = (h[...].astype(F32) + self.xb[c, zz].astype(F32)).astype(BF)
            self.ycp(c, zz).start()

    def Y(self, c, j0=0, count=None):
        z, nz = self.z, self.nz
        for j in range(j0, j0 + (count or nz)):
            zz = self.far(j)
            self.ycp(c, zz).wait_recv()
            h = self.half(c, zz, self.y, self.x)
            h[...] = (h[...].astype(F32) + self.yb[c, zz].astype(F32)).astype(BF)
            if j < nz - 1:
                pl.when(z == 0)(lambda: self.zcp(c, 0, zz, self.block(c, zz, self.y)).start())
                pl.when(z == nz - 1)(lambda: self.zcp(c, 1, zz, self.block(c, zz, self.y)).start())

    def Z(self, c, k):
        z, nz = self.z, self.nz
        zm = nz - 1 - z
        for i, ok, zz in ((0, both(z >= 1, k >= z), nz - 1 - k + z), (1, both(zm >= 1, k >= zm), k - zm)):

            @pl.when(ok)
            def _():
                slot = zz if i == 0 else jnp.where(zz == z, nz, zz)
                ref = self.zb.at[c, slot]
                rcopy(ref, ref, self.zs.at[c, i, zz], self.zr.at[c, i, zz], {"ctx": self.x}).wait_recv()

                @pl.when(zz != z)
                def _():
                    ref[...] = (ref[...].astype(F32) + self.block(c, zz, self.y)[...].astype(F32)).astype(BF)
                    self.zcp(c, i, zz, ref).start()

    def F(self, c):
        z, nz = self.z, self.nz
        fb0 = self.fb.at[c, 0]
        fb0[...] = self.block(c, z, self.y)[...]

        @pl.when(z > 0)
        def _():
            fb0[...] = (fb0[...].astype(F32) + self.zb[c, z].astype(F32)).astype(BF)

        @pl.when(z < nz - 1)
        def _():
            fb0[...] = (fb0[...].astype(F32) + self.zb[c, nz].astype(F32)).astype(BF)

        self.fcp(c).start()

    def G(self, c):
        self.fcp(c).wait_recv()
        return self.fb[c, 0].astype(F32) + self.fb[c, 1].astype(F32)

    def finish(self, c):
        z, nz = self.z, self.nz
        for zz in range(nz):
            self.xcp(c, zz).wait_send()
            self.ycp(c, zz).wait_send()
            b = self.block(c, zz, self.y)
            pl.when(both(z < nz - 1, zz > z))(lambda: self.zcp(c, 0, zz, b).wait_send())
            pl.when(both(z > 0, zz < z))(lambda: self.zcp(c, 1, zz, b).wait_send())
        self.fcp(c).wait_send()

    @staticmethod
    def sems(nc, nz):
        D = pltpu.SemaphoreType.DMA
        return [D((nc, nz)), D((nc, nz)), D((nc, 2, nz)), D((nc,)), D((nc, nz)), D((nc, nz)), D((nc, 2, nz)), D((nc,))]


def block_kernel(names, nz, NC, half, BQ, *refs):
    w = types.SimpleNamespace(**dict(zip(names, refs)))
    T, D = w.hb.shape
    n = nz * NY
    rows = D // n
    hr = rows // 2
    FC = w.act.shape[2]
    CA = w.attd.shape[1]
    QO = NC
    npair = CA // 128
    nt = T // BQ
    sub = half // BQ
    s, x, t = lax.axis_index("shard"), lax.axis_index("ctx"), lax.axis_index("tp")
    me = x * n + s
    g = Gather(w.G, rows, nz, [getattr(w, f"ga{i}") for i in range(6)])
    gq = Gather(w.G, rows, nz, [getattr(w, f"gc{i}") for i in range(6)], QO, 256)
    r = Scatter(w.GR, (w.xb, w.yb, w.zb, w.fb), rows, nz, [getattr(w, f"sc{i}") for i in range(8)])
    rq = Scatter(w.GQ, (w.xq, w.yq, w.zq, w.fq), rows, nz, [getattr(w, f"sq{i}") for i in range(8)])
    lane = lax.broadcasted_iota(jnp.int32, (BQ, 128), 1)
    low = lane < 64

    def tile(i):
        return pl.ds(pl.multiple_of(i * BQ, BQ), BQ)

    own = pl.ds(pl.multiple_of(s * rows, 16), rows)
    loads = [(w.kv, w.gkv.at[own])]
    for p in range(npair):
        loads.append((w.q.at[:, pl.ds(128 * p, 128)], w.G.at[QO, own, pl.ds(256 * p, 128)]))
        loads.append((w.o.at[:, pl.ds(128 * p, 128)], w.G.at[QO, own, pl.ds(256 * p + 128, 128)]))
    loads += [(w.cot, w.cb), (w.hidden, w.hb)]
    nl = 1 + 2 * npair
    for c in range(NC):
        loads.append((w.up.at[:, pl.ds(c * FC, FC)], w.G.at[c, own, pl.ds(0, FC)]))
        loads.append((w.dw.at[:, pl.ds(c * FC, FC)], w.G.at[c, own, pl.ds(FC, FC)]))
    loads = [pltpu.make_async_copy(a, b, w.lsem.at[i]) for i, (a, b) in enumerate(loads)]
    for c in loads:
        c.start()

    w.lb[s] = jnp.zeros((8, 128), F32)
    for k, ref in enumerate((w.g1, w.b1, w.g2, w.b2)):
        w.lb[s, k : k + 1, 0:rows] = ref[...].astype(F32)

    peers = [(s, 1 - x)] + [(lax.rem(s + k, n), xx) for k in range(1, n) for xx in (x, 1 - x)]
    bar = pltpu.get_barrier_semaphore()
    for ps, px in peers:
        pl.semaphore_signal(bar, inc=1, device_id={"shard": ps, "ctx": px}, device_id_type=MESH)
    pl.semaphore_signal(bar, inc=1, device_id={"tp": 1 - t}, device_id_type=MESH)
    for c in loads[:nl]:
        c.wait()
    pl.semaphore_wait(bar, 2 * n)

    kds = [rcopy(w.gkv.at[own], w.gkv.at[own], w.gb0.at[k - 1], w.gb1.at[s], {"shard": lax.rem(s + k, n)}) for k in range(1, n)]
    for c in kds:
        c.start()
    lns = [rcopy(w.lb.at[s], w.lb.at[s], w.lns.at[k - 1], w.lnr.at[s], {"shard": lax.rem(s + k, n)}) for k in range(1, n)]
    for c in lns:
        c.start()
    for c in range(npair):
        gq.own(c)
    for c in loads[nl:]:
        c.wait()

    first = jnp.minimum(w.bo[2 * x], w.bo[2 * x + 1])
    second = jnp.maximum(w.bo[2 * x], w.bo[2 * x + 1])
    swap = w.bo[2 * x] > w.bo[2 * x + 1]

    def pick(a, b):
        return jnp.where(swap, b, a)

    def flip(i):
        return lax.rem(i + sub, 2 * sub)

    @pl.loop(0, nt)
    def _(i):
        base = jnp.where(i < sub, first, second) * half + lax.rem(i, sub) * BQ
        pos = (base + lax.broadcasted_iota(jnp.int32, (BQ, 128), 0)).astype(F32)
        ang = pos * w.freq[0:1, :]
        l64 = lax.rem(lane, 64)
        w.tc[tile(i), :] = jnp.where(l64 < 16, jnp.cos(ang), 1.0)
        sn = jnp.sin(ang)
        w.ts[tile(i), :] = jnp.where(l64 < 8, -sn, jnp.where(l64 < 16, sn, 0.0))
        w.ct[:, tile(i)] = w.cb[tile(i), :].T

    def rotated(v, i, sign, layout=False):
        sw = jnp.where(lax.rem(lane, 16) < 8, pltpu.roll(v, 120, 1), pltpu.roll(v, 8, 1))
        cs, sn = w.tc[tile(i), :], w.ts[tile(i), :]
        if layout:
            cs, sn = pick(cs, w.tc[tile(flip(i)), :]), pick(sn, w.ts[tile(flip(i)), :])
        turn = sw * sn
        return v * cs + (turn if sign > 0 else -turn)

    for k in range(1, n):
        f = lax.rem(s + n - k, n)
        rcopy(w.lb.at[f], w.lb.at[f], w.lns.at[0], w.lnr.at[f], {"shard": f}).wait_recv()
    prm = None
    for k in range(n):
        piece = jnp.concatenate([w.lb[k], jnp.zeros((8, D - 128), F32)], axis=1)
        piece = pltpu.roll(piece, k * rows, 1) if k else piece
        prm = piece if prm is None else prm + piece
    w.prm[...] = prm

    def standardized(i):
        v = w.hb[tile(i), :].astype(F32)
        v = v - jnp.mean(v, axis=1, keepdims=True)
        rstd = lax.rsqrt(jnp.mean(v * v, axis=1, keepdims=True) + 1e-05)
        return v * rstd, rstd

    @pl.loop(0, nt)
    def _(i):
        xh, _ = standardized(i)
        na = (xh * w.prm[0:1, :] + w.prm[1:2, :]).astype(BF)
        w.na[tile(i), :] = na

    plan = {
        ("h", 0): [(gq.stage, 0, 1), (g.own, 1)],
        ("h", 1): [(gq.stage, 0, 2), (g.own, 0)],
        ("h", 2): [(gq.stage, 0, 3), (gq.stage, 0, 4), (gq.stage, 1, 1), (g.stage, 0, 1)],
    }

    def at(*slot):
        for f, *a in plan.get(slot, []):
            f(*a)

    at("h", 0)
    for k in range(1, n):
        f = lax.rem(s + n - k, n)
        b = w.gkv.at[pl.ds(pl.multiple_of(f * rows, 16), rows)]
        rcopy(b, b, w.gb0.at[0], w.gb1.at[f], {"shard": f}).wait_recv()

    @pl.loop(0, nt)
    def _(i):
        kvp = dot(w.na[tile(i), :], w.gkv[...])
        w.kvb[0, tile(i), :] = jnp.where(low, rotated(kvp, i, 1, True), kvp).astype(BF)

    kvx = rcopy(w.kvb.at[0], w.kvb.at[1], w.es.at[0], w.er.at[0], {"ctx": 1 - x})
    kvx.start()
    kvo = pltpu.make_async_copy(w.kvb.at[0], w.kvout, w.osem.at[0])
    kvo.start()

    lane1 = lax.broadcasted_iota(jnp.int32, (1, 128), 1)

    at("h", 1)

    @pl.loop(0, nt)
    def _(i):
        xh, _ = standardized(i)
        nf = (xh * w.prm[2:3, :] + w.prm[3:4, :]).astype(BF)
        w.nf[tile(i), :] = nf
        w.nft[:, tile(i)] = nf.T
        w.nat[:, tile(i)] = w.na[tile(i), :].T

    def project(p):
        @pl.loop(0, nt)
        def _(i):
            qp = dot(pick(w.na[tile(i), :], w.na[tile(flip(i)), :]), w.G[QO, :, pl.ds(pl.multiple_of(p * 256, 128), 128)])
            gp = dot(pick(w.cb[tile(i), :], w.cb[tile(flip(i)), :]), w.G[QO, :, pl.ds(pl.multiple_of(p * 256 + 128, 128), 128)])
            mine = jnp.where(i < sub, first, second)
            hide = jnp.zeros((1, 128), F32)
            for j in range(2):
                hide = jnp.where(lane1 == 64 + j, jnp.where(w.bo[2 * (1 - x) + j] <= mine, 0.0, NEG), hide)
            qs = rotated(qp, i, 1).astype(BF).astype(F32) * 0.125
            w.qx[i, 0:BQ, :] = jnp.where(low, qs, hide).astype(BF)
            w.qx[i, BQ : 2 * BQ, :] = jnp.where(low, pltpu.roll(qs, 64, 1), hide).astype(BF)
            qt = qs.astype(BF).T
            w.qt[i, :, 0:BQ] = qt[:64]
            w.qt[i, :, BQ : 2 * BQ] = qt[64:]
            w.dox[i, 0:BQ, :] = jnp.where(low, gp, 0.0).astype(BF)
            w.dox[i, BQ : 2 * BQ, :] = jnp.where(low, pltpu.roll(gp, 64, 1), 0.0).astype(BF)
            gt = gp.astype(BF).T
            w.dt[i, :, 0:BQ] = gt[:64]
            w.dt[i, :, BQ : 2 * BQ] = gt[64:]

    def keep_keys(i, kv, hot):
        kvf = kv.astype(F32)
        w.kx[tile(i), :] = jnp.where(low, kvf, hot).astype(BF)
        w.k0[tile(i), :] = jnp.where(low, kvf, 0.0).astype(BF)
        w.v0[tile(i), :] = jnp.where(low, pltpu.roll(kvf, 64, 1), 0.0).astype(BF)

    @pl.loop(0, nt)
    def _(i):
        keep_keys(i, pick(w.kvb[0, tile(i), :], w.kvb[0, tile(flip(i)), :]), 0.0)

    at("h", 2)
    kvx.wait_recv()

    @pl.loop(0, nt)
    def _(i):
        keep_keys(nt + i, w.kvb[1, tile(i), :], jnp.where(lane == 64 + i // sub, 1.0, 0.0))

    w.acc[...] = jnp.zeros_like(w.acc)
    at("h", 3)

    def own_out(c, v):
        cols = pl.ds(pl.multiple_of(c * FC, FC), FC)
        w.ou[:, cols] = v[:, :FC]
        w.od[:, cols] = v[:, FC:]

    def pair_out(p):
        v = rq.G(p)
        w.oq[:, p * 128 : p * 128 + 128] = v[:, :128]
        w.oo[:, p * 128 : p * 128 + 128] = v[:, 128:]

    def pair_grads(p):
        cols = slice(p * 128, p * 128 + 128)
        for ref, src, to in ((w.nat, w.gq, 0), (w.ct, w.attd, 128)):
            a, b = src[0:half, cols], src[half:T, cols]
            v = dot(ref[:, 0:half], pick(a, b)) + dot(ref[:, half:T], pick(b, a))
            w.GQ[p, :, to : to + 128] = v.astype(BF)
        rq.start(p)

    def feed(c, part):
        @pl.loop(0, nt)
        def _(i):
            hp = dot(w.nf[tile(i), :], w.G[c, :, 0:FC])
            da = dot(w.cb[tile(i), :], w.G[c, :, FC : 2 * FC])
            cdf = 0.5 + 0.5 * lax.erf(hp * 0.7071067811865476)
            pdf = jnp.exp(-0.5 * hp * hp) * 0.3989422804014327
            w.act[c, tile(i), :] = (hp * cdf).astype(BF)
            w.dh[c, tile(i), :] = (da * (cdf + hp * pdf)).astype(BF)
            for j in range(nt):
                pl.when(i == j)(functools.partial(part, "i", c, j))

        @pl.loop(0, D // BQ)
        def _(m):
            w.GR[c, tile(m), 0:FC] = dot(w.nft[tile(m), :], w.dh[c]).astype(BF)
            w.GR[c, tile(m), FC : 2 * FC] = dot(w.ct[tile(m), :], w.act[c]).astype(BF)
            for j in range(2):
                pl.when(m == j)(functools.partial(part, "m", c, j))

        r.start(c)

    def out(c):
        own_out(c, r.G(c))

    plan.update({
        ("a", 2): [(r.Y, 0, 2, 2), (r.X, 1, 2, 2)],
        ("b", 0): [(g.stage, 0, 5)],
        ("b", 1): [(g.stage, 1, 5)],
        ("b", 2): [(g.stage, 3, 3)],
        ("b", 3): [(g.stage, 3, 5), (r.Z, 0, 2), (r.X, 2, 2, 2), (rq.Z, 0, 3)],
        ("d", 0): [(r.Z, 1, 3), (r.F, 1), (r.Y, 3, 2, 2), (rq.Z, 1, 2)],
        ("d", 1): [(r.Z, 3, 1), (rq.X, 2)],
        ("d", 2): [(r.Z, 2, 2), (rq.Z, 1, 3), (rq.F, 1)],
        ("i", 0, 0): [(g.stage, 3, 1)],
        ("i", 0, 3): [(g.stage, 1, 4), (g.stage, 2, 3)],
        ("i", 1, 0): [(g.stage, 3, 2), (rq.Y, 0)],
        ("i", 2, 0): [(rq.Z, 0, 1)],
        ("i", 2, 3): [(gq.stage, 2, 3), (r.X, 1, 0, 2), (rq.Z, 0, 2)],
        ("i", 3, 2): [(r.Y, 1, 2, 2), (rq.F, 0)],
        ("l", 0): [(r.Z, 3, 3)],
        ("l", 1): [(r.F, 3)],
        ("l", 2): [(rq.Z, 2, 2), (pair_out, 1)],
        ("m", 0, 1): [(rq.X, 0)],
        ("m", 1, 0): [(g.stage, 2, 4), (r.X, 0, 0, 2)],
        ("m", 1, 1): [(gq.stage, 2, 2)],
        ("m", 3, 0): [(r.Z, 0, 3)],
        ("m", 3, 1): [(r.Z, 1, 1), (rq.X, 1)],
        ("t", 0): [(r.F, 0), (r.Z, 3, 2), (rq.Y, 2), (rq.Z, 2, 1)],
        ("t", 1): [(r.Z, 2, 3), (r.F, 2)],
        ("t", 3): [(rq.Z, 2, 3), (rq.F, 2), (out, 0), (out, 1), (out, 2), (out, 3)],
        ("t", 4): [(pair_out, 2)],
        (0, 0, 0): [(g.own, 2)],
        (0, 0, 1): [(gq.stage, 1, 2)],
        (0, 1, 1): [(g.stage, 1, 1)],
        (0, 2, 0): [(gq.stage, 1, 3), (g.stage, 0, 2)],
        (0, 2, 1): [(g.stage, 2, 1)],
        (0, 3, 0): [(g.stage, 1, 2), (g.own, 3)],
        (0, 3, 1): [(gq.stage, 1, 4), (g.stage, 0, 3)],
        (1, 0, 0): [(g.stage, 0, 4), (g.stage, 2, 2)],
        (1, 1, 0): [(g.stage, 1, 3)],
        (1, 2, 0): [(gq.stage, 2, 1)],
        (1, 2, 1): [(r.X, 0, 2, 2)],
        (1, 3, 0): [(g.stage, 2, 5), (r.Y, 0, 0, 2)],
        (1, 3, 1): [(gq.stage, 2, 4), (g.stage, 3, 4), (r.Z, 0, 1)],
        (2, 0, 0): [(r.Y, 1, 0, 2), (r.X, 2, 0, 2)],
        (2, 0, 1): [(pair_out, 0)],
        (2, 1, 0): [(r.Y, 2, 0, 2)],
        (2, 2, 0): [(r.X, 3, 0, 2)],
        (2, 2, 1): [(r.Z, 1, 2), (rq.Y, 1)],
        (2, 3, 0): [(r.Y, 2, 2, 2)],
        (2, 3, 1): [(r.Z, 2, 1), (r.X, 3, 2, 2), (r.Y, 3, 0, 2), (rq.Z, 1, 1)],
    })

    def chunks(these):
        def part(*slot):
            for cc in these:
                if (slot[0], cc, *slot[2:]) in plan:
                    pl.when(slot[1] == cc)(functools.partial(at, slot[0], cc, *slot[2:]))

        def chunk(c):
            part("b", c)
            feed(c, part)
            part("a", c)

        pl.loop(these[0], these[-1] + 1)(chunk)

    def tick(p, k, m):
        for pp in range(npair):
            if (pp, k, m) in plan:
                pl.when(p == pp)(functools.partial(at, pp, k, m))

    def attention(p, k):
        R = 2 * BQ
        b, rr = k // sub, k % sub
        spans = [(0, half, False)] if b else []
        spans += [(b * half + i * BQ, BQ, False) for i in range(rr)]
        spans += [(b * half + rr * BQ, BQ, True), (2 * half, half, False), (3 * half, half, False)]
        parts, at = [], 0
        for off, size, tri in spans:
            parts.append((slice(off, off + size), slice(at, at + size), tri))
            at += size
        q, do = w.qx[k], w.dox[k]
        m = None
        for ks, cs, tri in parts:
            sc = dot_nt(q, w.kx[ks, :])
            if tri:
                row = lax.rem(lax.broadcasted_iota(jnp.int32, (R, BQ), 0), BQ)
                sc = jnp.where(lax.broadcasted_iota(jnp.int32, (R, BQ), 1) <= row, sc, NEG)
            w.ss[:, cs] = sc
            for j in range(sc.shape[1] // 128):
                mj = sc[:, j * 128 : (j + 1) * 128]
                m = mj if m is None else jnp.maximum(m, mj)
        m = jnp.max(m, axis=1, keepdims=True)
        l = o = None
        for ks, cs, _ in parts:
            e = jnp.exp(w.ss[:, cs] - m)
            w.ss[:, cs] = e
            for j in range(e.shape[1] // 128):
                lj = e[:, j * 128 : (j + 1) * 128]
                l = lj if l is None else l + lj
            eb = e.astype(BF)
            w.ps[:, cs] = eb
            oj = dot(eb, w.v0[ks, :])
            o = oj if o is None else o + oj
        inv = 1.0 / jnp.sum(l, axis=1, keepdims=True)
        o = o * inv
        delta = jnp.sum(o * do.astype(F32), axis=1, keepdims=True)
        inv_row = jnp.transpose(jnp.broadcast_to(inv, (R, 128)))[:1, :]
        qs = (w.qt[k].astype(F32) * inv_row).astype(BF)
        dos = (w.dt[k].astype(F32) * inv_row).astype(BF)
        tick(p, k, 1)
        dq = None
        for ks, cs, _ in parts:
            dp = dot_nt(do, w.v0[ks, :])
            ds = (w.ss[:, cs] * (dp - delta)).astype(BF)
            dj = dot(ds, w.k0[ks, :])
            dq = dj if dq is None else dq + dj
            w.acc[0:64, ks] += dot(qs, ds)
            w.acc[64:128, ks] += dot(dos, w.ps[:, cs])
        dq = dq * (inv * 0.125)
        pair = pl.ds(pl.multiple_of(p * 128, 128), 128)
        at = slice(k * BQ, (k + 1) * BQ)
        w.attd[at, pair] = (o[:BQ] + pltpu.roll(o[BQ:], 64, 1)).astype(BF)
        w.gq[at, pair] = rotated(dq[:BQ] + pltpu.roll(dq[BQ:], 64, 1), k, -1).astype(BF)

    @pl.loop(0, npair)
    def _(p):
        for pp in range(1, npair):
            pl.when(p == pp)(functools.partial(pair_grads, pp - 1))
        project(p)
        for k in range(nt):
            tick(p, k, 0)
            if k == 1:
                pl.when(p == 1)(functools.partial(chunks, [0]))
            if k == 2:
                pl.when(p == 1)(functools.partial(chunks, [1]))
            if k == 3:
                pl.when(p == 1)(functools.partial(chunks, [2]))
            if k == 0:
                pl.when(p == 2)(functools.partial(chunks, [3]))
            attention(p, k)

    for b in (0, 1):
        o = 1 - b
        w.dS[0, :, b * half : (b + 1) * half] = pick(w.acc[:, b * half : (b + 1) * half], w.acc[:, o * half : (o + 1) * half]).astype(BF)
    w.dS[1] = w.acc[:, T : 2 * T].astype(BF)
    dtp = rcopy(w.dS, w.dR, w.es.at[2], w.er.at[2], {"tp": 1 - t})
    dtp.start()
    pair_grads(2)
    dtp.wait_recv()
    w.dX[...] = (w.dS[1].astype(F32) + w.dR[1].astype(F32)).astype(BF)
    dxx = rcopy(w.dX, w.dXR, w.es.at[4], w.er.at[4], {"ctx": 1 - x})
    dxx.start()

    def dnx(i):
        return rcopy(w.na.at[tile(i)], w.dnr.at[tile(i)], w.ts0.at[0, i], w.tr0.at[0, i], {"tp": 1 - t})

    def brx(i):
        return rcopy(w.act.at[pl.ds(0, 2), tile(i)], w.brr.at[:, tile(i)], w.ts0.at[1, i], w.tr0.at[1, i], {"tp": 1 - t})

    def gax(i):
        return rcopy(w.act.at[pl.ds(2, 2), tile(i)], w.gar.at[:, tile(i)], w.ts0.at[2, i], w.tr0.at[2, i], {"tp": 1 - t})

    @pl.loop(0, nt)
    def _(i):
        dn = dot_nt(w.dh[0, tile(i), :], w.G[0, :, 0:FC])
        br = dot_nt(w.act[0, tile(i), :], w.G[0, :, FC : 2 * FC])
        for c in range(1, NC):
            dn = dn + dot_nt(w.dh[c, tile(i), :], w.G[c, :, 0:FC])
            br = br + dot_nt(w.act[c, tile(i), :], w.G[c, :, FC : 2 * FC])
        ga = None
        for p in range(npair):
            cols = slice(128 * p, 128 * p + 128)
            gp = dot_nt(pick(w.gq[tile(i), cols], w.gq[tile(flip(i)), cols]), w.G[QO, :, 256 * p : 256 * p + 128])
            ga = gp if ga is None else ga + gp
            br = br + dot_nt(pick(w.attd[tile(i), cols], w.attd[tile(flip(i)), cols]), w.G[QO, :, 256 * p + 128 : 256 * p + 256])
        w.na[tile(i), :] = dn.astype(BF)
        for k, v in enumerate((br, ga)):
            w.act[2 * k, tile(i), :] = v[:, :FC].astype(BF)
            w.act[2 * k + 1, tile(i), :] = v[:, FC:].astype(BF)
        brx(i).start()
        gax(i).start()
        dnx(i).start()
        for j in range(nt):
            pl.when(i == j)(functools.partial(at, "d", j))

    at("t", 0)

    @pl.loop(0, nt)
    def _(i):
        brx(i).wait_recv()
        for k in range(2):
            cs = slice(k * FC, (k + 1) * FC)
            v = w.act[k, tile(i), :].astype(F32) + w.brr[k, tile(i), :].astype(F32)
            w.nf[tile(i), cs] = (w.hb[tile(i), cs].astype(F32) + v).astype(BF)

    outx = pltpu.make_async_copy(w.nf, w.out_tokens, w.osem.at[1])
    outx.start()
    at("t", 1)
    dxx.wait_recv()

    @pl.loop(0, nt)
    def _(i):
        v = w.dS[0, :, tile(i)].astype(F32) + w.dR[0, :, tile(i)].astype(F32) + w.dXR[:, tile(i)].astype(F32)
        v = v.T
        w.gkb[tile(i), :] = jnp.where(low, rotated(v, i, -1, True), v).astype(BF)

    w.kvS[...] = dot(w.nat[...], w.gkb[...]).astype(BF)

    def kv_rows(owner):
        return pl.ds(pl.multiple_of(owner * rows + t * hr, 16), hr)

    kvs = [rcopy(w.kvS.at[kv_rows(ps)], w.kvR.at[me], w.ks.at[i], w.kr.at[me], {"shard": ps, "ctx": px}) for i, (ps, px) in enumerate(peers)]
    for c in kvs:
        c.start()
    at("t", 2)
    w.lg[...] = jnp.zeros_like(w.lg)

    def hgx(i):
        return pltpu.make_async_copy(w.hgs.at[tile(i)], w.hg.at[tile(i)], w.osem.at[2 + i])

    @pl.loop(0, nt)
    def _(i):
        gax(i).wait_recv()
        dnx(i).wait_recv()
        xh, rstd = standardized(i)
        kvg = dot_nt(w.gkb[tile(i), :], w.gkv[...])
        gn = jnp.concatenate([w.act[2 + k, tile(i), :].astype(F32) + w.gar[k, tile(i), :].astype(F32) for k in (0, 1)], axis=1) + kvg
        gf = w.na[tile(i), :].astype(F32) + w.dnr[tile(i), :].astype(F32)
        e = gn * w.prm[0:1, :] + gf * w.prm[2:3, :]
        e = rstd * (e - jnp.mean(e, axis=1, keepdims=True) - xh * jnp.mean(e * xh, axis=1, keepdims=True))
        w.hgs[tile(i), :] = w.cb[tile(i), :].astype(F32) + e
        hgx(i).start()
        w.lg[0:1, :] += jnp.sum(gn * xh, axis=0, keepdims=True)
        w.lg[1:2, :] += jnp.sum(gn, axis=0, keepdims=True)
        w.lg[2:3, :] += jnp.sum(gf * xh, axis=0, keepdims=True)
        w.lg[3:4, :] += jnp.sum(gf, axis=0, keepdims=True)
        for j in range(nt):
            pl.when(i == j)(functools.partial(at, "l", j))

    lg = w.lg[...]
    keep = lax.broadcasted_iota(jnp.int32, (8, 128), 1) < rows
    for k in range(n):
        v = pltpu.roll(lg, D - k * rows, 1) if k else lg
        w.lS[k] = jnp.where(keep, v[:, :128], 0.0)
    lgs = [rcopy(w.lS.at[ps], w.lR.at[me], w.ls.at[i], w.lr.at[me], {"shard": ps, "ctx": px}) for i, (ps, px) in enumerate(peers)]
    for c in lgs:
        c.start()
    at("t", 3)

    def arrived(ref, sems, i, ps, px):
        k = px * n + ps
        return rcopy(ref.at[k], ref.at[k], sems.at[i], sems.at[k], {"shard": ps, "ctx": px})

    for i, (ps, px) in enumerate(peers):
        arrived(w.kvR, w.kr, i, ps, px).wait_recv()
    w.kvR[me] = w.kvS[kv_rows(s), :]
    v = w.kvR[0].astype(F32)
    for k in range(1, 2 * n):
        v = v + w.kvR[k].astype(F32)
    w.kvF[t] = v
    kfx = rcopy(w.kvF.at[t], w.kvF.at[t], w.es.at[6], w.er.at[6], {"tp": 1 - t})
    kfx.start()
    for i, (ps, px) in enumerate(peers):
        arrived(w.lR, w.lr, i, ps, px).wait_recv()
    w.lR[me] = w.lS[s]
    v = w.lR[0]
    for k in range(1, 2 * n):
        v = v + w.lR[k]
    w.lno[...] = v
    rcopy(w.kvF.at[1 - t], w.kvF.at[1 - t], w.es.at[6], w.er.at[6], {"tp": 1 - t}).wait_recv()
    w.okv[0:hr, :] = w.kvF[0]
    w.okv[hr:rows, :] = w.kvF[1]
    at("t", 4)
    kvo.wait()
    outx.wait()
    for i in range(nt):
        hgx(i).wait()
    for c in lns + kds + [kvx, dtp, dxx, kfx] + kvs + lgs:
        c.wait_send()
    for i in range(nt):
        for f in (dnx, brx, gax):
            f(i).wait_send()
    for c in range(npair):
        gq.finish(c)
        rq.finish(c)
    for c in range(NC):
        g.finish(c)
        r.finish(c)


def block_call(bo, freq, hidden, cot, lns, up, dw, q, o, kv, nz, half, cid):
    T, D = hidden.shape
    rows, CU = up.shape
    CA, CK = q.shape[1], kv.shape[1]
    FC = CA
    NC = CU // FC
    n = nz * NY
    hr = rows // 2
    BQ = 256
    npair = CA // 128
    nt = T // BQ
    A = pl.BlockSpec(memory_space=pl.ANY)
    V = pl.BlockSpec(memory_space=pltpu.VMEM)
    S = pl.BlockSpec(memory_space=pltpu.SMEM)
    Dm = pltpu.SemaphoreType.DMA
    ins = ["bo", "freq", "g1", "b1", "g2", "b2", "hidden", "cot", "up", "dw", "q", "o", "kv"]
    sd = jax.ShapeDtypeStruct
    outs = {
        "out_tokens": (sd((T, D), BF), A), "kvout": (sd((T, CK), BF), A), "hg": (sd((T, D), F32), A),
        "lno": (sd((8, 128), F32), V), "oq": (sd((rows, CA), F32), V), "okv": (sd((rows, CK), F32), V), "oo": (sd((rows, CA), F32), V),
        "ou": (sd((rows, CU), F32), V), "od": (sd((rows, CU), F32), V),
    }
    b = lambda *sh: pltpu.VMEM(sh, BF)
    f = lambda *sh: pltpu.VMEM(sh, F32)
    scr = {
        "hb": b(T, D), "cb": b(T, D), "ct": b(D, T), "na": b(T, D), "nf": b(T, D), "nft": b(D, T), "nat": b(D, T),
        "G": b(NC + 1, D, 2 * FC), "gkv": b(D, CK), "GR": b(NC, D, 2 * FC), "GQ": b(npair, D, 256),
        "xb": b(NC, nz, hr, 2 * FC), "yb": b(NC, nz, hr, 2 * FC), "zb": b(NC, nz + 1, rows, 2 * FC), "fb": b(NC, 2, rows, 2 * FC),
        "xq": b(npair, nz, hr, 256), "yq": b(npair, nz, hr, 256), "zq": b(npair, nz + 1, rows, 256), "fq": b(npair, 2, rows, 256),
        "lb": f(n, 8, 128), "act": b(NC, T, FC), "dh": b(NC, T, FC), "dnr": b(T, D),
        "qx": b(nt, 2 * BQ, 128), "dox": b(nt, 2 * BQ, 128), "qt": b(nt, 64, 2 * BQ), "dt": b(nt, 64, 2 * BQ),
        "brr": b(2, T, FC), "gar": b(2, T, FC), "ts0": Dm((3, nt)), "tr0": Dm((3, nt)), "gb0": Dm((n - 1,)), "gb1": Dm((n,)),
        "kvb": b(2, T, CK), "kx": b(2 * T, 128), "k0": b(2 * T, 128), "v0": b(2 * T, 128),
        "ss": f(2 * BQ, 2 * T), "ps": b(2 * BQ, 2 * T), "attd": b(T, CA), "gq": b(T, CA), "acc": f(128, 2 * T),
        "tc": f(T, 128), "ts": f(T, 128), "dS": b(2, 128, T), "dR": b(2, 128, T), "dX": b(128, T), "dXR": b(128, T), "gkb": b(T, 128),
        "kvS": b(D, CK), "kvR": b(2 * n, hr, CK), "kvF": f(2, hr, CK), "lS": f(n, 8, 128), "lR": f(2 * n, 8, 128), "prm": f(8, D), "lg": f(8, D), "hgs": f(T, D),
        "lsem": Dm((3 + 2 * npair + 2 * NC,)), "lns": Dm((n - 1,)), "lnr": Dm((n,)), "es": Dm((7,)), "er": Dm((7,)), "osem": Dm((2 + T // BQ,)),
        "ks": Dm((2 * n - 1,)), "kr": Dm((2 * n,)), "ls": Dm((2 * n - 1,)), "lr": Dm((2 * n,)),
    }
    scr.update({f"ga{i}": v for i, v in enumerate(Gather.sems(NC, nz))})
    scr.update({f"gc{i}": v for i, v in enumerate(Gather.sems(npair, nz))})
    scr.update({f"sc{i}": v for i, v in enumerate(Scatter.sems(NC, nz))})
    scr.update({f"sq{i}": v for i, v in enumerate(Scatter.sems(npair, nz))})
    names = ins + list(outs) + list(scr)
    res = pl.pallas_call(
        functools.partial(block_kernel, names, nz, NC, half, BQ),
        out_shape=tuple(v[0] for v in outs.values()),
        in_specs=[S, V, V, V, V, V] + [A] * 7,
        out_specs=tuple(v[1] for v in outs.values()),
        scratch_shapes=list(scr.values()),
        compiler_params=pltpu.CompilerParams(collective_id=cid, has_side_effects=True, vmem_limit_bytes=67043328),
        name="block",
    )(bo, freq, *lns, hidden, cot, up, dw, q, o, kv)
    return dict(zip(outs, res))


def results_kernel(nt, tok, hg, kv, lno, oq, okv, oo, ou, od, tok_o, k_o, v_o, hg_o, a_o, b_o, c_o, d_o, oq_o, okv_o, oo_o, ou_o, od_o, tb, hb, sin, sout):
    BQ = tok.shape[0] // nt
    moves = []
    for i in range(nt):
        t = pl.ds(i * BQ, BQ)
        moves.append((hg.at[t], hb.at[t], hg_o.at[t]))
        moves.append((tok.at[t], tb.at[t], tok_o.at[t]))
    ins = [pltpu.make_async_copy(a, b, sin.at[i]) for i, (a, b, _) in enumerate(moves)]
    outs = [pltpu.make_async_copy(b, c, sout.at[i]) for i, (_, b, c) in enumerate(moves)]
    for c in ins:
        c.start()
    for a, b in zip(ins, outs):
        a.wait()
        b.start()
    turned = kv[...].T
    k_o[...] = turned[:64]
    v_o[...] = turned[64:]
    for k, ref in enumerate((a_o, b_o, c_o, d_o)):
        ref[...] = lno[k, : ref.shape[0]]
    for a, b in ((oq, oq_o), (okv, okv_o), (oo, oo_o), (ou, ou_o), (od, od_o)):
        b[...] = a[...]
    for c in outs:
        c.wait()


def results(v, rows):
    T, D = v["hg"].shape
    A = pl.BlockSpec(memory_space=pl.ANY)
    V = pl.BlockSpec(memory_space=pltpu.VMEM)
    sd = jax.ShapeDtypeStruct
    like = lambda k: sd(v[k].shape, v[k].dtype)
    nt = 4
    Dm = pltpu.SemaphoreType.DMA
    order = ("out_tokens", "hg", "kvout", "lno", "oq", "okv", "oo", "ou", "od")
    return pl.pallas_call(
        functools.partial(results_kernel, nt),
        out_shape=(like("out_tokens"), sd((64, T), BF), sd((64, T), BF), like("hg")) + (sd((rows,), F32),) * 4 + tuple(like(k) for k in order[4:]),
        in_specs=[A, A] + [V] * 7,
        out_specs=(A, V, V, A) + (V,) * 9,
        scratch_shapes=[pltpu.VMEM((T, D), BF), pltpu.VMEM((T, D), F32), Dm((2 * nt,)), Dm((2 * nt,))],
        name="results",
    )(*[v[k] for k in order])


def fits(mesh):
    return mesh.shape["shard"] == 8 and mesh.shape["ctx"] == 2


def fast_device(hidden, block_order, ln1_gain, ln1_bias, ln2_gain, ln2_bias, q_weight, kv_weight, o_weight, up_weight, down_weight, cotangent):
    seqs, span, width = hidden.shape
    rows = ln1_gain.shape[0]
    freq = 10000.0 ** (-2.0 * (np.arange(128) % (ROT // 2)) / ROT)
    freq = jnp.asarray(np.broadcast_to(freq, (8, 128)), F32)
    lns = [a.reshape(1, rows) for a in (ln1_gain, ln1_bias, ln2_gain, ln2_bias)]
    v = block_call(block_order, freq, hidden.reshape(span, width), cotangent.reshape(span, width), lns, up_weight, down_weight, q_weight, o_weight, kv_weight, width // rows // NY, span // 2, 1)
    tok, keys, values, hg, a, b, c, d, oq, okv, oo, ou, od = results(v, rows)
    return (tok[None], keys.T[None], values.T[None], hg[None], a, b, c, d, oq, okv, oo, ou, od)


def solution(mesh):
    return jax.shard_map(
        fast_device if fits(mesh) else on_device,
        mesh=mesh,
        in_specs=(
            P("shard", "ctx", None),
            P(),
            P("shard"),
            P("shard"),
            P("shard"),
            P("shard"),
            P("shard", "tp"),
            P("shard", None),
            P("shard", "tp"),
            P("shard", "tp"),
            P("shard", "tp"),
            P("shard", "ctx", None),
        ),
        out_specs=(
            P("shard", "ctx", None),
            P("shard", "ctx", None),
            P("shard", "ctx", None),
            P("shard", "ctx", None),
            P("shard"),
            P("shard"),
            P("shard"),
            P("shard"),
            P("shard", "tp"),
            P("shard", None),
            P("shard", "tp"),
            P("shard", "tp"),
            P("shard", "tp"),
        ),
        check_vma=False,
    )
```

```python
import functools
import types

import jax
import jax.numpy as jnp
import numpy as np
from jax import lax
from jax.experimental import pallas as pl
from jax.experimental.pallas import tpu as pltpu
from jax.sharding import PartitionSpec as P

F32 = jnp.float32
BF = jnp.bfloat16
MESH = pl.DeviceIdType.MESH

ROT = 16


def layer_norm(values, gain, shift):
    center = values - jnp.mean(values, axis=-1, keepdims=True)
    spread = jnp.mean(center * center, axis=-1, keepdims=True)
    return center * lax.rsqrt(spread + 1e-05) * gain + shift


def gelu_exact(values):
    return jax.nn.gelu(values, approximate=False)


def rotate(tensor, places, sign):
    half_rot = ROT // 2
    freq = jnp.power(10000.0, -2.0 * jnp.arange(half_rot, dtype=jnp.float32) / ROT)
    angle = places.astype(jnp.float32)[:, None] * freq[None, :]
    cosine = jnp.cos(angle)[:, None, :]
    sine = sign * jnp.sin(angle)[:, None, :]
    first = tensor[..., :half_rot]
    second = tensor[..., half_rot:ROT]
    return jnp.concatenate(
        [first * cosine - second * sine, second * cosine + first * sine, tensor[..., ROT:]], axis=-1
    )


def tok_positions(block_order, rows, half_block):
    index = rows // half_block
    table = jnp.arange(block_order.shape[0], dtype=jnp.int32)
    picked = jnp.sum(jnp.where(index[:, None] == table[None, :], block_order[None, :], 0), axis=1)
    return picked * half_block + rows % half_block


def right_product(left, right):
    return lax.dot_general(
        left, right, (((1,), (1,)), ((), ())), preferred_element_type=jnp.float32
    )


def left_product(left, right):
    return lax.dot_general(
        left, right, (((0,), (0,)), ((), ())), preferred_element_type=jnp.float32
    )


def on_device(
    hidden,
    block_order,
    ln1_gain,
    ln1_bias,
    ln2_gain,
    ln2_bias,
    q_weight,
    kv_weight,
    o_weight,
    up_weight,
    down_weight,
    cotangent,
):
    seqs, span, width = hidden.shape
    half_block = span // 2
    head_size = kv_weight.shape[1] // 2
    local_heads = q_weight.shape[1] // head_size
    row_count = seqs * span
    query_rows = span * local_heads
    scale = head_size ** (-0.5)
    gathered = (
        lax.all_gather(ln1_gain, "shard", axis=0, tiled=True),
        lax.all_gather(ln1_bias, "shard", axis=0, tiled=True),
        lax.all_gather(ln2_gain, "shard", axis=0, tiled=True),
        lax.all_gather(ln2_bias, "shard", axis=0, tiled=True),
        lax.all_gather(q_weight, "shard", axis=0, tiled=True),
        lax.all_gather(kv_weight, "shard", axis=0, tiled=True),
        lax.all_gather(o_weight, "shard", axis=0, tiled=True),
        lax.all_gather(up_weight, "shard", axis=0, tiled=True),
        lax.all_gather(down_weight, "shard", axis=0, tiled=True),
    )
    gain_attn, bias_attn, gain_ffn, bias_ffn, w_query, w_keyval, w_output, w_up, w_down = gathered
    offset = lax.axis_index("ctx") * span
    query_places = tok_positions(
        block_order, offset + jnp.arange(span, dtype=jnp.int32), half_block
    )
    row_places = jnp.repeat(query_places, local_heads)
    tokens = hidden.astype(jnp.float32).reshape(row_count, width)
    norm_attn = layer_norm(
        tokens, gain_attn.astype(jnp.float32), bias_attn.astype(jnp.float32)
    ).astype(jnp.bfloat16)
    norm_ffn = layer_norm(
        tokens, gain_ffn.astype(jnp.float32), bias_ffn.astype(jnp.float32)
    ).astype(jnp.bfloat16)
    query_pre = jnp.dot(norm_attn, w_query, preferred_element_type=jnp.float32).reshape(
        seqs, span, local_heads, head_size
    )
    queries = (
        rotate(query_pre, query_places, 1.0)
        .astype(jnp.bfloat16)
        .reshape(seqs, query_rows, head_size)
    )
    keyval_pre = jnp.dot(norm_attn, w_keyval, preferred_element_type=jnp.float32).reshape(
        seqs, span, 2 * head_size
    )
    keys = rotate(keyval_pre[:, :, None, :head_size], query_places, 1.0)[:, :, 0, :].astype(
        jnp.bfloat16
    )
    values = keyval_pre[:, :, head_size:].astype(jnp.bfloat16)
    start_state = (
        jnp.full((seqs, query_rows), -1e30, jnp.float32),
        jnp.zeros((seqs, query_rows), jnp.float32),
        jnp.zeros((seqs, query_rows, head_size), jnp.float32),
    )
    key_piece = lax.all_gather(keys, "ctx", axis=1, tiled=True)
    value_piece = lax.all_gather(values, "ctx", axis=1, tiled=True)
    count = key_piece.shape[1]
    key_places = tok_positions(block_order, jnp.arange(count, dtype=jnp.int32), half_block)
    visible = key_places[None, :] <= row_places[:, None]

    def one_block(args):
        peak, total, accum, query_block, key_block, value_block = args
        scores = (
            jnp.einsum("qd,kd->qk", query_block, key_block, preferred_element_type=jnp.float32)
            * scale
        )
        scores = jnp.where(visible, scores, -1e30)
        new_peak = jnp.maximum(peak, jnp.max(scores, axis=1))
        factor = jnp.exp(peak - new_peak)
        weights = jnp.where(visible, jnp.exp(scores - new_peak[:, None]), 0.0)
        total = total * factor + jnp.sum(weights, axis=1)
        accum = accum * factor[:, None] + jnp.einsum(
            "qk,kd->qd",
            weights.astype(jnp.bfloat16),
            value_block,
            preferred_element_type=jnp.float32,
        )
        return (new_peak, total, accum)

    peak, total, accum = lax.map(
        one_block, (start_state[0], start_state[1], start_state[2], queries, key_piece, value_piece)
    )
    attended = (
        (accum / total[:, :, None]).astype(jnp.bfloat16).reshape(row_count, local_heads * head_size)
    )
    log_total = peak + jnp.log(total)
    hidden_pre = jnp.dot(norm_ffn, w_up, preferred_element_type=jnp.float32)
    activation_full, gelu_pull = jax.vjp(gelu_exact, hidden_pre)
    activation = activation_full.astype(jnp.bfloat16)
    branch = right_product(attended, w_output) + right_product(activation, w_down)
    branch = lax.psum(branch.astype(jnp.bfloat16), "tp").astype(jnp.float32)
    mixed = (tokens + branch).astype(jnp.bfloat16).reshape(seqs, span, width)
    regathered = (
        lax.all_gather(ln1_gain, "shard", axis=0, tiled=True),
        lax.all_gather(ln2_gain, "shard", axis=0, tiled=True),
        lax.all_gather(q_weight, "shard", axis=0, tiled=True),
        lax.all_gather(kv_weight, "shard", axis=0, tiled=True),
        lax.all_gather(o_weight, "shard", axis=0, tiled=True),
        lax.all_gather(up_weight, "shard", axis=0, tiled=True),
        lax.all_gather(down_weight, "shard", axis=0, tiled=True),
    )
    gain_attn, gain_ffn, w_query, w_keyval, w_output, w_up, w_down = regathered
    grad_out = cotangent.reshape(row_count, width)
    grad_attended = (
        jnp.dot(grad_out, w_output, preferred_element_type=jnp.float32)
        .astype(jnp.bfloat16)
        .reshape(seqs, query_rows, head_size)
    )
    grad_activation = jnp.dot(grad_out, w_down, preferred_element_type=jnp.float32)
    grad_hidden = gelu_pull(grad_activation)[0].astype(jnp.bfloat16)
    grad_w_output = left_product(grad_out, attended)
    grad_w_down = left_product(grad_out, activation)
    grad_w_up = left_product(norm_ffn, grad_hidden)
    grad_norm_ffn = right_product(grad_hidden, w_up)
    all_keys, all_values = (
        lax.all_gather(keys, "ctx", axis=1, tiled=True),
        lax.all_gather(values, "ctx", axis=1, tiled=True),
    )
    key_count = all_keys.shape[1]
    key_places = tok_positions(block_order, jnp.arange(key_count, dtype=jnp.int32), half_block)
    visible_all = key_places[None, :] <= row_places[:, None]

    def backward_one(args):
        query_block, key_block, value_block, grad_block, log_block = args
        scores = (
            jnp.einsum("qd,kd->qk", query_block, key_block, preferred_element_type=jnp.float32)
            * scale
        )
        probs = jnp.where(visible_all, jnp.exp(scores - log_block[:, None]), 0.0)
        grad_probs = jnp.einsum(
            "qd,kd->qk", grad_block, value_block, preferred_element_type=jnp.float32
        )
        delta = jnp.sum(probs * grad_probs, axis=1, keepdims=True)
        grad_scores = (probs * (grad_probs - delta)).astype(jnp.bfloat16)
        grad_query = (
            jnp.einsum("qk,kd->qd", grad_scores, key_block, preferred_element_type=jnp.float32)
            * scale
        )
        grad_key = (
            jnp.einsum("qk,qd->kd", grad_scores, query_block, preferred_element_type=jnp.float32)
            * scale
        )
        grad_value = jnp.einsum(
            "qk,qd->kd", probs.astype(jnp.bfloat16), grad_block, preferred_element_type=jnp.float32
        )
        return (grad_query, jnp.concatenate([grad_key, grad_value], axis=1))

    grad_queries, grad_keyvals = lax.map(
        backward_one, (queries, all_keys, all_values, grad_attended, log_total)
    )
    grad_keyvals = lax.psum_scatter(
        grad_keyvals.astype(jnp.bfloat16), "ctx", scatter_dimension=1, tiled=True
    ).astype(jnp.float32)
    grad_keyvals = lax.psum(grad_keyvals.astype(jnp.bfloat16), "tp").astype(jnp.float32)
    grad_key_pre = rotate(grad_keyvals[:, :, None, :head_size], query_places, -1.0)[:, :, 0, :]
    grad_keyval_pre = (
        jnp.concatenate([grad_key_pre, grad_keyvals[:, :, head_size:]], axis=2)
        .astype(jnp.bfloat16)
        .reshape(row_count, 2 * head_size)
    )
    grad_query_pre = (
        rotate(grad_queries.reshape(seqs, span, local_heads, head_size), query_places, -1.0)
        .astype(jnp.bfloat16)
        .reshape(row_count, local_heads * head_size)
    )
    grad_w_query = left_product(norm_attn, grad_query_pre)
    grad_w_keyval = left_product(norm_attn, grad_keyval_pre)
    grad_norm_attn = right_product(grad_query_pre, w_query)
    shared_term = right_product(grad_keyval_pre, w_keyval)
    zero_shift = jnp.zeros((width,), jnp.float32)
    attn_pull = jax.vjp(layer_norm, tokens, gain_attn.astype(jnp.float32), zero_shift)[1]
    ffn_pull = jax.vjp(layer_norm, tokens, gain_ffn.astype(jnp.float32), zero_shift)[1]
    grad_norm_attn, grad_norm_ffn = (
        lax.psum(grad_norm_attn.astype(jnp.bfloat16), "tp").astype(jnp.float32),
        lax.psum(grad_norm_ffn.astype(jnp.bfloat16), "tp").astype(jnp.float32),
    )
    grad_norm_attn = grad_norm_attn + shared_term
    grad_tok_attn, grad_gain_attn, grad_shift_attn = attn_pull(grad_norm_attn)
    grad_tok_ffn, grad_gain_ffn, grad_shift_ffn = ffn_pull(grad_norm_ffn)
    grad_tok_norms = grad_tok_attn + grad_tok_ffn
    grad_tokens = (grad_out.astype(jnp.float32) + grad_tok_norms).reshape(seqs, span, width)
    grads = (
        grad_gain_attn,
        grad_shift_attn,
        grad_gain_ffn,
        grad_shift_ffn,
        grad_w_query,
        grad_w_keyval,
        grad_w_output,
        grad_w_up,
        grad_w_down,
    )
    owned = (
        lax.psum_scatter(
            grads[0].astype(jnp.bfloat16), "shard", scatter_dimension=0, tiled=True
        ).astype(jnp.float32),
        lax.psum_scatter(
            grads[1].astype(jnp.bfloat16), "shard", scatter_dimension=0, tiled=True
        ).astype(jnp.float32),
        lax.psum_scatter(
            grads[2].astype(jnp.bfloat16), "shard", scatter_dimension=0, tiled=True
        ).astype(jnp.float32),
        lax.psum_scatter(
            grads[3].astype(jnp.bfloat16), "shard", scatter_dimension=0, tiled=True
        ).astype(jnp.float32),
        lax.psum_scatter(
            grads[4].astype(jnp.bfloat16), "shard", scatter_dimension=0, tiled=True
        ).astype(jnp.float32),
        lax.psum_scatter(
            grads[5].astype(jnp.bfloat16), "shard", scatter_dimension=0, tiled=True
        ).astype(jnp.float32),
        lax.psum_scatter(
            grads[6].astype(jnp.bfloat16), "shard", scatter_dimension=0, tiled=True
        ).astype(jnp.float32),
        lax.psum_scatter(
            grads[7].astype(jnp.bfloat16), "shard", scatter_dimension=0, tiled=True
        ).astype(jnp.float32),
        lax.psum_scatter(
            grads[8].astype(jnp.bfloat16), "shard", scatter_dimension=0, tiled=True
        ).astype(jnp.float32),
    )
    owned = (
        lax.psum(owned[0].astype(jnp.bfloat16), "ctx").astype(jnp.float32),
        lax.psum(owned[1].astype(jnp.bfloat16), "ctx").astype(jnp.float32),
        lax.psum(owned[2].astype(jnp.bfloat16), "ctx").astype(jnp.float32),
        lax.psum(owned[3].astype(jnp.bfloat16), "ctx").astype(jnp.float32),
        lax.psum(owned[4].astype(jnp.bfloat16), "ctx").astype(jnp.float32),
        lax.psum(owned[5].astype(jnp.bfloat16), "ctx").astype(jnp.float32),
        lax.psum(owned[6].astype(jnp.bfloat16), "ctx").astype(jnp.float32),
        lax.psum(owned[7].astype(jnp.bfloat16), "ctx").astype(jnp.float32),
        lax.psum(owned[8].astype(jnp.bfloat16), "ctx").astype(jnp.float32),
    )
    return (
        mixed,
        keys,
        values,
        grad_tokens,
        owned[0],
        owned[1],
        owned[2],
        owned[3],
        owned[4],
        owned[5],
        owned[6],
        owned[7],
        owned[8],
    )


NY = 2
WHOLE = (3,)
NEG = -1e30


def rcopy(src, dst, ss, rs, dev):
    return pltpu.make_async_remote_copy(src_ref=src, dst_ref=dst, send_sem=ss, recv_sem=rs, device_id=dev, device_id_type=MESH)


def dot_nt(a, b):
    return lax.dot_general(a, b, (((1,), (1,)), ((), ())), preferred_element_type=F32)


def dot(a, b):
    return lax.dot_general(a, b, (((1,), (0,)), ((), ())), preferred_element_type=F32)


def both(a, b):
    return jnp.logical_and(a, b)


class Gather:
    def __init__(self, ref, rows, nz, sems, fixed=None, cols=None):
        self.ref, self.rows, self.nz, self.fixed, self.cols = ref, rows, nz, fixed, cols
        self.zs, self.ys, self.xs, self.zr, self.yr, self.xr = sems
        s = lax.axis_index("shard")
        self.z, self.y, self.x = s // NY, s % NY, lax.axis_index("ctx")

    def view(self, c, rows):
        if self.cols is None:
            return self.ref.at[c, rows]
        return self.ref.at[self.fixed, rows, pl.ds(c * self.cols, self.cols)]

    def block(self, c, zz, yy):
        return self.view(c, pl.ds(pl.multiple_of((zz * NY + yy) * self.rows, 16), self.rows))

    def half(self, c, zz, yy, h):
        hr = self.rows // 2
        return self.view(c, pl.ds(pl.multiple_of((zz * NY + yy) * self.rows + h * hr, 16), hr))

    def up(self, c, zz):
        b = self.block(c, zz, self.y)
        return rcopy(b, b, self.zs.at[c, 0, zz], self.zr.at[c, zz], {"shard": (self.z + 1) * NY + self.y})

    def dn(self, c, zz):
        b = self.block(c, zz, self.y)
        return rcopy(b, b, self.zs.at[c, 1, zz], self.zr.at[c, zz], {"shard": (self.z - 1) * NY + self.y})

    def direct(self, c):
        return self.cols is not None or c in WHOLE

    def ycp(self, c, zz, yy, h):
        b = self.block(c, zz, yy) if self.direct(c) else self.half(c, zz, yy, h)
        return rcopy(b, b, self.ys.at[c, zz], self.yr.at[c, zz], {"shard": self.z * NY + 1 - self.y})

    def xcp(self, c, zz, h):
        b = self.half(c, zz, 1 - self.y, h)
        return rcopy(b, b, self.xs.at[c, zz], self.xr.at[c, zz], {"ctx": 1 - self.x})

    def own(self, c):
        z, nz = self.z, self.nz

        @pl.when(z < nz - 1)
        def _():
            self.up(c, z).start()

        @pl.when(z > 0)
        def _():
            self.dn(c, z).start()

        self.ycp(c, z, self.y, self.x).start()

    def dirs(self, d):
        return ((self.z - d >= 0, self.z - d, True), (self.z + d < self.nz, self.z + d, False))

    def Z(self, c, d):
        z, nz = self.z, self.nz
        for ok, zz, isup in self.dirs(d):

            @pl.when(ok)
            def _():
                self.up(c, zz).wait_recv()
                if isup:
                    pl.when(z < nz - 1)(lambda: self.up(c, zz).start())
                else:
                    pl.when(z > 0)(lambda: self.dn(c, zz).start())
                self.ycp(c, zz, self.y, self.x).start()

    def each(self, d, f):
        if d == 0:
            f(self.z)
        else:
            for ok, zz, _ in self.dirs(d):
                pl.when(ok)(functools.partial(f, zz))

    def Y(self, c, d):
        def f(zz):
            self.ycp(c, zz, 1 - self.y, self.x).wait_recv()
            if not self.direct(c):
                self.xcp(c, zz, self.x).start()

        self.each(d, f)

    def X(self, c, d):
        self.each(d, lambda zz: self.xcp(c, zz, 1 - self.x).wait_recv())

    def stage(self, c, d):
        if d < self.nz:
            self.Z(c, d)
        if d <= self.nz:
            self.Y(c, d - 1)
        if d > 1 and not self.direct(c):
            self.X(c, d - 2)

    def finish(self, c):
        z, nz = self.z, self.nz
        pl.when(z < nz - 1)(lambda: self.up(c, z).wait_send())
        pl.when(z > 0)(lambda: self.dn(c, z).wait_send())
        for d in range(1, nz):
            for ok, zz, isup in self.dirs(d):
                if isup:
                    pl.when(both(ok, z < nz - 1))(lambda: self.up(c, zz).wait_send())
                else:
                    pl.when(both(ok, z > 0))(lambda: self.dn(c, zz).wait_send())
        for zz in range(nz):
            self.ycp(c, zz, self.y, self.x).wait_send()
            if not self.direct(c):
                self.xcp(c, zz, self.x).wait_send()

    @staticmethod
    def sems(nc, nz):
        D = pltpu.SemaphoreType.DMA
        return [D((nc, 2, nz)), D((nc, nz)), D((nc, nz)), D((nc, nz)), D((nc, nz)), D((nc, nz))]


class Scatter:
    view, block, half = Gather.view, Gather.block, Gather.half

    def __init__(self, ref, bufs, rows, nz, sems):
        self.ref, self.rows, self.nz, self.cols = ref, rows, nz, None
        self.xb, self.yb, self.zb, self.fb = bufs
        self.xs, self.ys, self.zs, self.fs, self.xr, self.yr, self.zr, self.fr = sems
        s = lax.axis_index("shard")
        self.z, self.y, self.x = s // NY, s % NY, lax.axis_index("ctx")

    def xcp(self, c, zz):
        return rcopy(self.half(c, zz, 1 - self.y, 1 - self.x), self.xb.at[c, zz], self.xs.at[c, zz], self.xr.at[c, zz], {"ctx": 1 - self.x})

    def ycp(self, c, zz):
        return rcopy(self.half(c, zz, 1 - self.y, self.x), self.yb.at[c, zz], self.ys.at[c, zz], self.yr.at[c, zz], {"shard": self.z * NY + 1 - self.y})

    def zcp(self, c, i, zz, src):
        to = self.z + 1 if i == 0 else self.z - 1
        slot = zz if i == 0 else jnp.where(zz == to, self.nz, zz)
        return rcopy(src, self.zb.at[c, slot], self.zs.at[c, i, zz], self.zr.at[c, i, zz], {"shard": to * NY + self.y})

    def fcp(self, c):
        return rcopy(self.fb.at[c, 0], self.fb.at[c, 1], self.fs.at[c], self.fr.at[c], {"ctx": 1 - self.x})

    def far(self, j):
        return jnp.where(self.z < self.nz // 2, self.nz - 1 - j, j)

    def start(self, c):
        for j in range(self.nz):
            self.xcp(c, self.far(j)).start()

    def X(self, c, j0=0, count=None):
        for j in range(j0, j0 + (count or self.nz)):
            zz = self.far(j)
            self.xcp(c, zz).wait_recv()
            h = self.half(c, zz, 1 - self.y, self.x)
            h[...] = (h[...].astype(F32) + self.xb[c, zz].astype(F32)).astype(BF)
            self.ycp(c, zz).start()

    def Y(self, c, j0=0, count=None):
        z, nz = self.z, self.nz
        for j in range(j0, j0 + (count or nz)):
            zz = self.far(j)
            self.ycp(c, zz).wait_recv()
            h = self.half(c, zz, self.y, self.x)
            h[...] = (h[...].astype(F32) + self.yb[c, zz].astype(F32)).astype(BF)
            if j < nz - 1:
                pl.when(z == 0)(lambda: self.zcp(c, 0, zz, self.block(c, zz, self.y)).start())
                pl.when(z == nz - 1)(lambda: self.zcp(c, 1, zz, self.block(c, zz, self.y)).start())

    def Z(self, c, k):
        z, nz = self.z, self.nz
        zm = nz - 1 - z
        for i, ok, zz in ((0, both(z >= 1, k >= z), nz - 1 - k + z), (1, both(zm >= 1, k >= zm), k - zm)):

            @pl.when(ok)
            def _():
                slot = zz if i == 0 else jnp.where(zz == z, nz, zz)
                ref = self.zb.at[c, slot]
                rcopy(ref, ref, self.zs.at[c, i, zz], self.zr.at[c, i, zz], {"ctx": self.x}).wait_recv()

                @pl.when(zz != z)
                def _():
                    ref[...] = (ref[...].astype(F32) + self.block(c, zz, self.y)[...].astype(F32)).astype(BF)
                    self.zcp(c, i, zz, ref).start()

    def F(self, c):
        z, nz = self.z, self.nz
        fb0 = self.fb.at[c, 0]
        fb0[...] = self.block(c, z, self.y)[...]

        @pl.when(z > 0)
        def _():
            fb0[...] = (fb0[...].astype(F32) + self.zb[c, z].astype(F32)).astype(BF)

        @pl.when(z < nz - 1)
        def _():
            fb0[...] = (fb0[...].astype(F32) + self.zb[c, nz].astype(F32)).astype(BF)

        self.fcp(c).start()

    def G(self, c):
        self.fcp(c).wait_recv()
        return self.fb[c, 0].astype(F32) + self.fb[c, 1].astype(F32)

    def finish(self, c):
        z, nz = self.z, self.nz
        for zz in range(nz):
            self.xcp(c, zz).wait_send()
            self.ycp(c, zz).wait_send()
            b = self.block(c, zz, self.y)
            pl.when(both(z < nz - 1, zz > z))(lambda: self.zcp(c, 0, zz, b).wait_send())
            pl.when(both(z > 0, zz < z))(lambda: self.zcp(c, 1, zz, b).wait_send())
        self.fcp(c).wait_send()

    @staticmethod
    def sems(nc, nz):
        D = pltpu.SemaphoreType.DMA
        return [D((nc, nz)), D((nc, nz)), D((nc, 2, nz)), D((nc,)), D((nc, nz)), D((nc, nz)), D((nc, 2, nz)), D((nc,))]


def block_kernel(names, nz, NC, half, BQ, *refs):
    w = types.SimpleNamespace(**dict(zip(names, refs)))
    T, D = w.hb.shape
    n = nz * NY
    rows = D // n
    hr = rows // 2
    FC = w.act.shape[2]
    CA = w.attd.shape[1]
    QO = NC
    npair = CA // 128
    nt = T // BQ
    sub = half // BQ
    s, x, t = lax.axis_index("shard"), lax.axis_index("ctx"), lax.axis_index("tp")
    me = x * n + s
    g = Gather(w.G, rows, nz, [getattr(w, f"ga{i}") for i in range(6)])
    gq = Gather(w.G, rows, nz, [getattr(w, f"gc{i}") for i in range(6)], QO, 256)
    r = Scatter(w.GR, (w.xb, w.yb, w.zb, w.fb), rows, nz, [getattr(w, f"sc{i}") for i in range(8)])
    rq = Scatter(w.GQ, (w.xq, w.yq, w.zq, w.fq), rows, nz, [getattr(w, f"sq{i}") for i in range(8)])
    lane = lax.broadcasted_iota(jnp.int32, (BQ, 128), 1)
    low = lane < 64

    def tile(i):
        return pl.ds(pl.multiple_of(i * BQ, BQ), BQ)

    own = pl.ds(pl.multiple_of(s * rows, 16), rows)
    loads = [(w.kv, w.gkv.at[own])]
    for p in range(npair):
        loads.append((w.q.at[:, pl.ds(128 * p, 128)], w.G.at[QO, own, pl.ds(256 * p, 128)]))
        loads.append((w.o.at[:, pl.ds(128 * p, 128)], w.G.at[QO, own, pl.ds(256 * p + 128, 128)]))
    loads += [(w.cot, w.cb), (w.hidden, w.hb)]
    nl = 1 + 2 * npair
    for c in range(NC):
        loads.append((w.up.at[:, pl.ds(c * FC, FC)], w.G.at[c, own, pl.ds(0, FC)]))
        loads.append((w.dw.at[:, pl.ds(c * FC, FC)], w.G.at[c, own, pl.ds(FC, FC)]))
    loads = [pltpu.make_async_copy(a, b, w.lsem.at[i]) for i, (a, b) in enumerate(loads)]
    for c in loads:
        c.start()

    w.lb[s] = jnp.zeros((8, 128), F32)
    for k, ref in enumerate((w.g1, w.b1, w.g2, w.b2)):
        w.lb[s, k : k + 1, 0:rows] = ref[...].astype(F32)

    peers = [(s, 1 - x)] + [(lax.rem(s + k, n), xx) for k in range(1, n) for xx in (x, 1 - x)]
    bar = pltpu.get_barrier_semaphore()
    for ps, px in peers:
        pl.semaphore_signal(bar, inc=1, device_id={"shard": ps, "ctx": px}, device_id_type=MESH)
    pl.semaphore_signal(bar, inc=1, device_id={"tp": 1 - t}, device_id_type=MESH)
    for c in loads[:nl]:
        c.wait()
    pl.semaphore_wait(bar, 2 * n)

    kds = [rcopy(w.gkv.at[own], w.gkv.at[own], w.gb0.at[k - 1], w.gb1.at[s], {"shard": lax.rem(s + k, n)}) for k in range(1, n)]
    for c in kds:
        c.start()
    lns = [rcopy(w.lb.at[s], w.lb.at[s], w.lns.at[k - 1], w.lnr.at[s], {"shard": lax.rem(s + k, n)}) for k in range(1, n)]
    for c in lns:
        c.start()
    for c in range(npair):
        gq.own(c)
    for c in loads[nl:]:
        c.wait()

    first = jnp.minimum(w.bo[2 * x], w.bo[2 * x + 1])
    second = jnp.maximum(w.bo[2 * x], w.bo[2 * x + 1])
    swap = w.bo[2 * x] > w.bo[2 * x + 1]

    def pick(a, b):
        return jnp.where(swap, b, a)

    def flip(i):
        return lax.rem(i + sub, 2 * sub)

    @pl.loop(0, nt)
    def _(i):
        base = jnp.where(i < sub, first, second) * half + lax.rem(i, sub) * BQ
        pos = (base + lax.broadcasted_iota(jnp.int32, (BQ, 128), 0)).astype(F32)
        ang = pos * w.freq[0:1, :]
        l64 = lax.rem(lane, 64)
        w.tc[tile(i), :] = jnp.where(l64 < 16, jnp.cos(ang), 1.0)
        sn = jnp.sin(ang)
        w.ts[tile(i), :] = jnp.where(l64 < 8, -sn, jnp.where(l64 < 16, sn, 0.0))
        w.ct[:, tile(i)] = w.cb[tile(i), :].T

    def rotated(v, i, sign, layout=False):
        sw = jnp.where(lax.rem(lane, 16) < 8, pltpu.roll(v, 120, 1), pltpu.roll(v, 8, 1))
        cs, sn = w.tc[tile(i), :], w.ts[tile(i), :]
        if layout:
            cs, sn = pick(cs, w.tc[tile(flip(i)), :]), pick(sn, w.ts[tile(flip(i)), :])
        turn = sw * sn
        return v * cs + (turn if sign > 0 else -turn)

    for k in range(1, n):
        f = lax.rem(s + n - k, n)
        rcopy(w.lb.at[f], w.lb.at[f], w.lns.at[0], w.lnr.at[f], {"shard": f}).wait_recv()
    prm = None
    for k in range(n):
        piece = jnp.concatenate([w.lb[k], jnp.zeros((8, D - 128), F32)], axis=1)
        piece = pltpu.roll(piece, k * rows, 1) if k else piece
        prm = piece if prm is None else prm + piece
    w.prm[...] = prm

    def standardized(i):
        v = w.hb[tile(i), :].astype(F32)
        v = v - jnp.mean(v, axis=1, keepdims=True)
        rstd = lax.rsqrt(jnp.mean(v * v, axis=1, keepdims=True) + 1e-05)
        return v * rstd, rstd

    @pl.loop(0, nt)
    def _(i):
        xh, _ = standardized(i)
        na = (xh * w.prm[0:1, :] + w.prm[1:2, :]).astype(BF)
        w.na[tile(i), :] = na

    plan = {
        ("h", 0): [(gq.stage, 0, 1)],
        ("h", 1): [(g.own, 0)],
        ("h", 2): [(gq.stage, 0, 2), (gq.stage, 1, 1), (g.own, 1)],
        ("h", 3): [(gq.stage, 0, 3), (gq.stage, 0, 4), (gq.stage, 1, 2), (g.stage, 0, 1)],
    }

    def at(*slot):
        for f, *a in plan.get(slot, []):
            f(*a)

    at("h", 0)
    for k in range(1, n):
        f = lax.rem(s + n - k, n)
        b = w.gkv.at[pl.ds(pl.multiple_of(f * rows, 16), rows)]
        rcopy(b, b, w.gb0.at[0], w.gb1.at[f], {"shard": f}).wait_recv()

    @pl.loop(0, nt)
    def _(i):
        kvp = dot(w.na[tile(i), :], w.gkv[...])
        w.kvb[0, tile(i), :] = jnp.where(low, rotated(kvp, i, 1, True), kvp).astype(BF)

    kvx = rcopy(w.kvb.at[0], w.kvb.at[1], w.es.at[0], w.er.at[0], {"ctx": 1 - x})
    kvx.start()
    kvo = pltpu.make_async_copy(w.kvb.at[0], w.kvout, w.osem.at[0])
    kvo.start()

    lane1 = lax.broadcasted_iota(jnp.int32, (1, 128), 1)

    at("h", 1)

    @pl.loop(0, nt)
    def _(i):
        xh, _ = standardized(i)
        nf = (xh * w.prm[2:3, :] + w.prm[3:4, :]).astype(BF)
        w.nf[tile(i), :] = nf
        w.nft[:, tile(i)] = nf.T
        w.nat[:, tile(i)] = w.na[tile(i), :].T

    def project(p):
        @pl.loop(0, nt)
        def _(i):
            qp = dot(pick(w.na[tile(i), :], w.na[tile(flip(i)), :]), w.G[QO, :, pl.ds(pl.multiple_of(p * 256, 128), 128)])
            gp = dot(pick(w.cb[tile(i), :], w.cb[tile(flip(i)), :]), w.G[QO, :, pl.ds(pl.multiple_of(p * 256 + 128, 128), 128)])
            mine = jnp.where(i < sub, first, second)
            hide = jnp.zeros((1, 128), F32)
            for j in range(2):
                hide = jnp.where(lane1 == 64 + j, jnp.where(w.bo[2 * (1 - x) + j] <= mine, 0.0, NEG), hide)
            qs = rotated(qp, i, 1).astype(BF).astype(F32) * 0.125
            w.qx[i, 0:BQ, :] = jnp.where(low, qs, hide).astype(BF)
            w.qx[i, BQ : 2 * BQ, :] = jnp.where(low, pltpu.roll(qs, 64, 1), hide).astype(BF)
            qt = qs.astype(BF).T
            w.qt[i, :, 0:BQ] = qt[:64]
            w.qt[i, :, BQ : 2 * BQ] = qt[64:]
            w.dox[i, 0:BQ, :] = jnp.where(low, gp, 0.0).astype(BF)
            w.dox[i, BQ : 2 * BQ, :] = jnp.where(low, pltpu.roll(gp, 64, 1), 0.0).astype(BF)
            gt = gp.astype(BF).T
            w.dt[i, :, 0:BQ] = gt[:64]
            w.dt[i, :, BQ : 2 * BQ] = gt[64:]

    def keep_keys(i, kv, hot):
        kvf = kv.astype(F32)
        w.kx[tile(i), :] = jnp.where(low, kvf, hot).astype(BF)
        w.k0[tile(i), :] = jnp.where(low, kvf, 0.0).astype(BF)
        w.v0[tile(i), :] = jnp.where(low, pltpu.roll(kvf, 64, 1), 0.0).astype(BF)

    @pl.loop(0, nt)
    def _(i):
        keep_keys(i, pick(w.kvb[0, tile(i), :], w.kvb[0, tile(flip(i)), :]), 0.0)

    at("h", 2)
    kvx.wait_recv()

    @pl.loop(0, nt)
    def _(i):
        keep_keys(nt + i, w.kvb[1, tile(i), :], jnp.where(lane == 64 + i // sub, 1.0, 0.0))

    w.acc[...] = jnp.zeros_like(w.acc)
    at("h", 3)

    def own_out(c, v):
        cols = pl.ds(pl.multiple_of(c * FC, FC), FC)
        w.ou[:, cols] = v[:, :FC]
        w.od[:, cols] = v[:, FC:]

    def pair_out(p):
        v = rq.G(p)
        w.oq[:, p * 128 : p * 128 + 128] = v[:, :128]
        w.oo[:, p * 128 : p * 128 + 128] = v[:, 128:]

    def pair_grads(p):
        cols = slice(p * 128, p * 128 + 128)
        for ref, src, to in ((w.nat, w.gq, 0), (w.ct, w.attd, 128)):
            a, b = src[0:half, cols], src[half:T, cols]
            v = dot(ref[:, 0:half], pick(a, b)) + dot(ref[:, half:T], pick(b, a))
            w.GQ[p, :, to : to + 128] = v.astype(BF)
        rq.start(p)

    def feed(c, part):
        @pl.loop(0, nt)
        def _(i):
            hp = dot(w.nf[tile(i), :], w.G[c, :, 0:FC])
            da = dot(w.cb[tile(i), :], w.G[c, :, FC : 2 * FC])
            cdf = 0.5 + 0.5 * lax.erf(hp * 0.7071067811865476)
            pdf = jnp.exp(-0.5 * hp * hp) * 0.3989422804014327
            w.act[c, tile(i), :] = (hp * cdf).astype(BF)
            w.dh[c, tile(i), :] = (da * (cdf + hp * pdf)).astype(BF)
            for j in range(nt):
                pl.when(i == j)(functools.partial(part, "i", c, j))

        @pl.loop(0, D // BQ)
        def _(m):
            w.GR[c, tile(m), 0:FC] = dot(w.nft[tile(m), :], w.dh[c]).astype(BF)
            w.GR[c, tile(m), FC : 2 * FC] = dot(w.ct[tile(m), :], w.act[c]).astype(BF)
            for j in range(2):
                pl.when(m == j)(functools.partial(part, "m", c, j))

        r.start(c)

    def out(c):
        own_out(c, r.G(c))

    plan.update({
        ("a", 2): [(r.Y, 0, 2, 2)],
        ("a", 3): [(rq.Z, 0, 2)],
        ("b", 0): [(g.stage, 0, 5)],
        ("b", 1): [(g.stage, 1, 5), (rq.Y, 0)],
        ("b", 2): [(g.stage, 2, 5)],
        ("b", 3): [(g.stage, 3, 4), (g.stage, 3, 5), (r.X, 2, 0, 2)],
        ("d", 0): [(r.Z, 2, 2), (r.Y, 3, 2, 2), (out, 1)],
        ("d", 1): [(r.Z, 0, 3), (r.Z, 3, 1), (rq.X, 2)],
        ("d", 2): [(r.F, 0), (r.Z, 2, 3)],
        ("d", 3): [(rq.Z, 1, 2), (rq.Y, 2)],
        ("i", 0, 1): [(g.stage, 1, 4)],
        ("i", 0, 2): [(gq.stage, 2, 2), (g.stage, 3, 1)],
        ("i", 1, 0): [(r.X, 0, 0, 2)],
        ("i", 1, 2): [(gq.stage, 2, 3)],
        ("i", 2, 1): [(r.X, 1, 0, 2)],
        ("i", 3, 0): [(r.Z, 0, 1)],
        ("i", 3, 1): [(r.X, 2, 2, 2)],
        ("i", 3, 3): [(r.Y, 1, 2, 2)],
        ("l", 1): [(rq.Z, 2, 2)],
        ("m", 1, 0): [(g.stage, 3, 2), (r.X, 0, 2, 2)],
        ("m", 1, 1): [(g.stage, 2, 4)],
        ("m", 2, 0): [(gq.stage, 2, 4)],
        ("m", 2, 1): [(g.stage, 3, 3)],
        ("m", 3, 1): [(r.Z, 1, 1)],
        ("t", 0): [(r.Z, 3, 2)],
        ("t", 1): [(r.F, 2), (rq.Z, 2, 1), (pair_out, 0)],
        ("t", 2): [(rq.Z, 1, 3), (rq.F, 1)],
        ("t", 3): [(r.Z, 3, 3), (r.F, 3), (rq.Z, 2, 3), (rq.F, 2), (out, 0), (out, 2), (pair_out, 1)],
        ("t", 4): [(out, 3), (pair_out, 2)],
        (0, 1, 0): [(g.stage, 1, 1), (g.own, 2)],
        (0, 1, 1): [(gq.stage, 1, 3)],
        (0, 2, 0): [(g.stage, 0, 2)],
        (0, 2, 1): [(g.stage, 1, 2)],
        (0, 3, 0): [(g.stage, 2, 1)],
        (0, 3, 1): [(gq.stage, 1, 4), (g.stage, 0, 3), (g.own, 3)],
        (1, 0, 0): [(gq.stage, 2, 1), (g.stage, 0, 4), (g.stage, 1, 3), (g.stage, 2, 2)],
        (1, 1, 0): [(rq.X, 0)],
        (1, 2, 0): [(g.stage, 2, 3)],
        (1, 2, 1): [(r.Y, 0, 0, 2), (rq.Z, 0, 1)],
        (1, 3, 1): [(r.X, 1, 2, 2), (r.Y, 1, 0, 2)],
        (2, 0, 1): [(r.Y, 2, 0, 2), (rq.X, 1)],
        (2, 1, 1): [(r.Z, 0, 2), (r.Z, 1, 2), (r.X, 3, 0, 2)],
        (2, 2, 0): [(rq.Y, 1)],
        (2, 2, 1): [(r.Y, 2, 2, 2), (r.X, 3, 2, 2)],
        (2, 3, 0): [(r.Z, 2, 1), (r.Y, 3, 0, 2), (rq.Z, 0, 3), (rq.F, 0)],
        (2, 3, 1): [(r.Z, 1, 3), (r.F, 1), (rq.Z, 1, 1)],
    })

    def chunks(these):
        def part(*slot):
            for cc in these:
                if (slot[0], cc, *slot[2:]) in plan:
                    pl.when(slot[1] == cc)(functools.partial(at, slot[0], cc, *slot[2:]))

        def chunk(c):
            part("b", c)
            feed(c, part)
            part("a", c)

        pl.loop(these[0], these[-1] + 1)(chunk)

    def tick(p, k, m):
        for pp in range(npair):
            if (pp, k, m) in plan:
                pl.when(p == pp)(functools.partial(at, pp, k, m))

    def attention(p, k):
        R = 2 * BQ
        b, rr = k // sub, k % sub
        spans = [(0, half, False)] if b else []
        spans += [(b * half + i * BQ, BQ, False) for i in range(rr)]
        spans += [(b * half + rr * BQ, BQ, True), (2 * half, half, False), (3 * half, half, False)]
        parts, at = [], 0
        for off, size, tri in spans:
            parts.append((slice(off, off + size), slice(at, at + size), tri))
            at += size
        q, do = w.qx[k], w.dox[k]
        m = None
        for ks, cs, tri in parts:
            sc = dot_nt(q, w.kx[ks, :])
            if tri:
                row = lax.rem(lax.broadcasted_iota(jnp.int32, (R, BQ), 0), BQ)
                sc = jnp.where(lax.broadcasted_iota(jnp.int32, (R, BQ), 1) <= row, sc, NEG)
            w.ss[:, cs] = sc
            for j in range(sc.shape[1] // 128):
                mj = sc[:, j * 128 : (j + 1) * 128]
                m = mj if m is None else jnp.maximum(m, mj)
        m = jnp.max(m, axis=1, keepdims=True)
        l = o = None
        for ks, cs, _ in parts:
            e = jnp.exp(w.ss[:, cs] - m)
            w.ss[:, cs] = e
            for j in range(e.shape[1] // 128):
                lj = e[:, j * 128 : (j + 1) * 128]
                l = lj if l is None else l + lj
            eb = e.astype(BF)
            w.ps[:, cs] = eb
            oj = dot(eb, w.v0[ks, :])
            o = oj if o is None else o + oj
        inv = 1.0 / jnp.sum(l, axis=1, keepdims=True)
        o = o * inv
        delta = jnp.sum(o * do.astype(F32), axis=1, keepdims=True)
        inv_row = jnp.transpose(jnp.broadcast_to(inv, (R, 128)))[:1, :]
        qs = (w.qt[k].astype(F32) * inv_row).astype(BF)
        dos = (w.dt[k].astype(F32) * inv_row).astype(BF)
        tick(p, k, 1)
        dq = None
        for ks, cs, _ in parts:
            dp = dot_nt(do, w.v0[ks, :])
            ds = (w.ss[:, cs] * (dp - delta)).astype(BF)
            dj = dot(ds, w.k0[ks, :])
            dq = dj if dq is None else dq + dj
            w.acc[0:64, ks] += dot(qs, ds)
            w.acc[64:128, ks] += dot(dos, w.ps[:, cs])
        dq = dq * (inv * 0.125)
        pair = pl.ds(pl.multiple_of(p * 128, 128), 128)
        at = slice(k * BQ, (k + 1) * BQ)
        w.attd[at, pair] = (o[:BQ] + pltpu.roll(o[BQ:], 64, 1)).astype(BF)
        w.gq[at, pair] = rotated(dq[:BQ] + pltpu.roll(dq[BQ:], 64, 1), k, -1).astype(BF)

    @pl.loop(0, npair)
    def _(p):
        for pp in range(1, npair):
            pl.when(p == pp)(functools.partial(pair_grads, pp - 1))
        project(p)
        for k in range(nt):
            tick(p, k, 0)
            if k == 1:
                pl.when(p == 1)(functools.partial(chunks, [0]))
            if k == 2:
                pl.when(p == 1)(functools.partial(chunks, [1]))
            if k == 3:
                pl.when(p == 1)(functools.partial(chunks, [2]))
            if k == 0:
                pl.when(p == 2)(functools.partial(chunks, [3]))
            attention(p, k)

    for b in (0, 1):
        o = 1 - b
        w.dS[0, :, b * half : (b + 1) * half] = pick(w.acc[:, b * half : (b + 1) * half], w.acc[:, o * half : (o + 1) * half]).astype(BF)
    w.dS[1] = w.acc[:, T : 2 * T].astype(BF)
    dtp = rcopy(w.dS, w.dR, w.es.at[2], w.er.at[2], {"tp": 1 - t})
    dtp.start()
    pair_grads(2)
    dtp.wait_recv()
    w.dX[...] = (w.dS[1].astype(F32) + w.dR[1].astype(F32)).astype(BF)
    dxx = rcopy(w.dX, w.dXR, w.es.at[4], w.er.at[4], {"ctx": 1 - x})
    dxx.start()

    def part(i):
        return tile(lax.rem(i, nt // 2))

    def dnx(i):
        return rcopy(w.na.at[tile(i)], w.dnr.at[part(i)], w.ts0.at[0, i], w.tr0.at[0, i], {"tp": 1 - t})

    def brx(i):
        return rcopy(w.act.at[pl.ds(0, 2), tile(i)], w.brr.at[:, part(i)], w.ts0.at[1, i], w.tr0.at[1, i], {"tp": 1 - t})

    def gax(i):
        return rcopy(w.act.at[pl.ds(2, 2), tile(i)], w.gar.at[:, part(i)], w.ts0.at[2, i], w.tr0.at[2, i], {"tp": 1 - t})

    ht = nt // 2
    ours = pl.ds(pl.multiple_of(t * (T // 2), BQ), T // 2)
    theirs = pl.ds(pl.multiple_of((1 - t) * (T // 2), BQ), T // 2)

    @pl.loop(0, nt)
    def _(step):
        i = lax.rem(step + (1 - t) * ht, nt)
        dn = dot_nt(w.dh[0, tile(i), :], w.G[0, :, 0:FC])
        br = dot_nt(w.act[0, tile(i), :], w.G[0, :, FC : 2 * FC])
        for c in range(1, NC):
            dn = dn + dot_nt(w.dh[c, tile(i), :], w.G[c, :, 0:FC])
            br = br + dot_nt(w.act[c, tile(i), :], w.G[c, :, FC : 2 * FC])
        ga = None
        for p in range(npair):
            cols = slice(128 * p, 128 * p + 128)
            gp = dot_nt(pick(w.gq[tile(i), cols], w.gq[tile(flip(i)), cols]), w.G[QO, :, 256 * p : 256 * p + 128])
            ga = gp if ga is None else ga + gp
            br = br + dot_nt(pick(w.attd[tile(i), cols], w.attd[tile(flip(i)), cols]), w.G[QO, :, 256 * p + 128 : 256 * p + 256])
        w.na[tile(i), :] = dn.astype(BF)
        for k, v in enumerate((br, ga)):
            w.act[2 * k, tile(i), :] = v[:, :FC].astype(BF)
            w.act[2 * k + 1, tile(i), :] = v[:, FC:].astype(BF)

        @pl.when(step < ht)
        def _():
            brx(i).start()
            gax(i).start()
            dnx(i).start()

        for j in range(nt):
            pl.when(step == j)(functools.partial(at, "d", j))

    at("t", 0)

    @pl.loop(0, ht)
    def _(j):
        i = t * ht + j
        brx(i).wait_recv()
        for k in range(2):
            cs = slice(k * FC, (k + 1) * FC)
            v = w.act[k, tile(i), :].astype(F32) + w.brr[k, tile(j), :].astype(F32)
            w.nf[tile(i), cs] = (w.hb[tile(i), cs].astype(F32) + v).astype(BF)

    outx = pltpu.make_async_copy(w.nf.at[ours], w.out_tokens.at[ours], w.osem.at[1])
    outx.start()

    def outr(rows):
        return rcopy(w.nf.at[rows], w.out_tokens.at[rows], w.es.at[1], w.er.at[1], {"tp": 1 - t})

    outr(ours).start()
    at("t", 1)
    dxx.wait_recv()

    @pl.loop(0, nt)
    def _(i):
        v = w.dS[0, :, tile(i)].astype(F32) + w.dR[0, :, tile(i)].astype(F32) + w.dXR[:, tile(i)].astype(F32)
        v = v.T
        w.gkb[tile(i), :] = jnp.where(low, rotated(v, i, -1, True), v).astype(BF)

    w.kvS[...] = dot(w.nat[...], w.gkb[...]).astype(BF)

    def kv_rows(owner):
        return pl.ds(pl.multiple_of(owner * rows + t * hr, 16), hr)

    kvs = [rcopy(w.kvS.at[kv_rows(ps)], w.kvR.at[me], w.ks.at[i], w.kr.at[me], {"shard": ps, "ctx": px}) for i, (ps, px) in enumerate(peers)]
    for c in kvs:
        c.start()
    at("t", 2)
    w.lg[...] = jnp.zeros_like(w.lg)

    def hgx(i):
        return pltpu.make_async_copy(w.hgs.at[part(i)], w.hg.at[tile(i)], w.osem.at[2 + i])

    def hgr(i):
        return rcopy(w.hgs.at[part(i)], w.hg.at[tile(i)], w.ts0.at[3, i], w.tr0.at[3, i], {"tp": 1 - t})

    @pl.loop(0, ht)
    def _(j):
        i = t * ht + j
        gax(i).wait_recv()
        dnx(i).wait_recv()
        xh, rstd = standardized(i)
        kvg = dot_nt(w.gkb[tile(i), :], w.gkv[...])
        gn = jnp.concatenate([w.act[2 + k, tile(i), :].astype(F32) + w.gar[k, tile(j), :].astype(F32) for k in (0, 1)], axis=1) + kvg
        gf = w.na[tile(i), :].astype(F32) + w.dnr[tile(j), :].astype(F32)
        e = gn * w.prm[0:1, :] + gf * w.prm[2:3, :]
        e = rstd * (e - jnp.mean(e, axis=1, keepdims=True) - xh * jnp.mean(e * xh, axis=1, keepdims=True))
        w.hgs[tile(j), :] = w.cb[tile(i), :].astype(F32) + e
        hgx(i).start()
        hgr(i).start()
        w.lg[0:1, :] += jnp.sum(gn * xh, axis=0, keepdims=True)
        w.lg[1:2, :] += jnp.sum(gn, axis=0, keepdims=True)
        w.lg[2:3, :] += jnp.sum(gf * xh, axis=0, keepdims=True)
        w.lg[3:4, :] += jnp.sum(gf, axis=0, keepdims=True)
        for k in range(ht):
            pl.when(j == k)(functools.partial(at, "l", k))

    lg = w.lg[...]
    keep = lax.broadcasted_iota(jnp.int32, (8, 128), 1) < rows
    for k in range(n):
        v = pltpu.roll(lg, D - k * rows, 1) if k else lg
        w.lS[k] = jnp.where(keep, v[:, :128], 0.0)
    lgs = [rcopy(w.lS.at[ps], w.lR.at[me], w.ls.at[i], w.lr.at[me], {"shard": ps, "ctx": px}) for i, (ps, px) in enumerate(peers)]
    for c in lgs:
        c.start()
    at("t", 3)

    def arrived(ref, sems, i, ps, px):
        k = px * n + ps
        return rcopy(ref.at[k], ref.at[k], sems.at[i], sems.at[k], {"shard": ps, "ctx": px})

    for i, (ps, px) in enumerate(peers):
        arrived(w.kvR, w.kr, i, ps, px).wait_recv()
    w.kvR[me] = w.kvS[kv_rows(s), :]
    v = w.kvR[0].astype(F32)
    for k in range(1, 2 * n):
        v = v + w.kvR[k].astype(F32)
    w.kvF[t] = v
    kfx = rcopy(w.kvF.at[t], w.kvF.at[t], w.es.at[6], w.er.at[6], {"tp": 1 - t})
    kfx.start()
    for i, (ps, px) in enumerate(peers):
        arrived(w.lR, w.lr, i, ps, px).wait_recv()
    w.lR[me] = w.lS[s]
    v = w.lR[0]
    for k in range(1, 2 * n):
        v = v + w.lR[k]
    w.lF[t] = v
    lfx = rcopy(w.lF.at[t], w.lF.at[t], w.es.at[3], w.er.at[3], {"tp": 1 - t})
    lfx.start()
    rcopy(w.kvF.at[1 - t], w.kvF.at[1 - t], w.es.at[6], w.er.at[6], {"tp": 1 - t}).wait_recv()
    w.okv[0:hr, :] = w.kvF[0]
    w.okv[hr:rows, :] = w.kvF[1]
    at("t", 4)
    rcopy(w.lF.at[1 - t], w.lF.at[1 - t], w.es.at[3], w.er.at[3], {"tp": 1 - t}).wait_recv()
    w.lno[...] = w.lF[0] + w.lF[1]
    kvo.wait()
    outx.wait()
    outr(theirs).wait_recv()
    for j in range(ht):
        hgx(t * ht + j).wait()
        hgr((1 - t) * ht + j).wait_recv()
    for c in lns + kds + [kvx, dtp, dxx, kfx, lfx, outr(ours)] + kvs + lgs:
        c.wait_send()
    for j in range(ht):
        for f in (dnx, brx, gax):
            f((1 - t) * ht + j).wait_send()
        hgr(t * ht + j).wait_send()
    for c in range(npair):
        gq.finish(c)
        rq.finish(c)
    for c in range(NC):
        g.finish(c)
        r.finish(c)


def block_call(bo, freq, hidden, cot, lns, up, dw, q, o, kv, nz, half, cid):
    T, D = hidden.shape
    rows, CU = up.shape
    CA, CK = q.shape[1], kv.shape[1]
    FC = CA
    NC = CU // FC
    n = nz * NY
    hr = rows // 2
    BQ = 256
    npair = CA // 128
    nt = T // BQ
    A = pl.BlockSpec(memory_space=pl.ANY)
    V = pl.BlockSpec(memory_space=pltpu.VMEM)
    S = pl.BlockSpec(memory_space=pltpu.SMEM)
    Dm = pltpu.SemaphoreType.DMA
    ins = ["bo", "freq", "g1", "b1", "g2", "b2", "hidden", "cot", "up", "dw", "q", "o", "kv"]
    sd = jax.ShapeDtypeStruct
    outs = {
        "out_tokens": (sd((T, D), BF), A), "kvout": (sd((T, CK), BF), A), "hg": (sd((T, D), F32), A),
        "lno": (sd((8, 128), F32), V), "oq": (sd((rows, CA), F32), V), "okv": (sd((rows, CK), F32), V), "oo": (sd((rows, CA), F32), V),
        "ou": (sd((rows, CU), F32), V), "od": (sd((rows, CU), F32), V),
    }
    b = lambda *sh: pltpu.VMEM(sh, BF)
    f = lambda *sh: pltpu.VMEM(sh, F32)
    scr = {
        "hb": b(T, D), "cb": b(T, D), "ct": b(D, T), "na": b(T, D), "nf": b(T, D), "nft": b(D, T), "nat": b(D, T),
        "G": b(NC + 1, D, 2 * FC), "gkv": b(D, CK), "GR": b(NC, D, 2 * FC), "GQ": b(npair, D, 256),
        "xb": b(NC, nz, hr, 2 * FC), "yb": b(NC, nz, hr, 2 * FC), "zb": b(NC, nz + 1, rows, 2 * FC), "fb": b(NC, 2, rows, 2 * FC),
        "xq": b(npair, nz, hr, 256), "yq": b(npair, nz, hr, 256), "zq": b(npair, nz + 1, rows, 256), "fq": b(npair, 2, rows, 256),
        "lb": f(n, 8, 128), "act": b(NC, T, FC), "dh": b(NC, T, FC), "dnr": b(T // 2, D),
        "qx": b(nt, 2 * BQ, 128), "dox": b(nt, 2 * BQ, 128), "qt": b(nt, 64, 2 * BQ), "dt": b(nt, 64, 2 * BQ),
        "brr": b(2, T // 2, FC), "gar": b(2, T // 2, FC), "ts0": Dm((4, nt)), "tr0": Dm((4, nt)), "lF": f(2, 8, 128), "gb0": Dm((n - 1,)), "gb1": Dm((n,)),
        "kvb": b(2, T, CK), "kx": b(2 * T, 128), "k0": b(2 * T, 128), "v0": b(2 * T, 128),
        "ss": f(2 * BQ, 2 * T), "ps": b(2 * BQ, 2 * T), "attd": b(T, CA), "gq": b(T, CA), "acc": f(128, 2 * T),
        "tc": f(T, 128), "ts": f(T, 128), "dS": b(2, 128, T), "dR": b(2, 128, T), "dX": b(128, T), "dXR": b(128, T), "gkb": b(T, 128),
        "kvS": b(D, CK), "kvR": b(2 * n, hr, CK), "kvF": f(2, hr, CK), "lS": f(n, 8, 128), "lR": f(2 * n, 8, 128), "prm": f(8, D), "lg": f(8, D), "hgs": f(T // 2, D),
        "lsem": Dm((3 + 2 * npair + 2 * NC,)), "lns": Dm((n - 1,)), "lnr": Dm((n,)), "es": Dm((7,)), "er": Dm((7,)), "osem": Dm((2 + T // BQ,)),
        "ks": Dm((2 * n - 1,)), "kr": Dm((2 * n,)), "ls": Dm((2 * n - 1,)), "lr": Dm((2 * n,)),
    }
    scr.update({f"ga{i}": v for i, v in enumerate(Gather.sems(NC, nz))})
    scr.update({f"gc{i}": v for i, v in enumerate(Gather.sems(npair, nz))})
    scr.update({f"sc{i}": v for i, v in enumerate(Scatter.sems(NC, nz))})
    scr.update({f"sq{i}": v for i, v in enumerate(Scatter.sems(npair, nz))})
    names = ins + list(outs) + list(scr)
    res = pl.pallas_call(
        functools.partial(block_kernel, names, nz, NC, half, BQ),
        out_shape=tuple(v[0] for v in outs.values()),
        in_specs=[S, V, V, V, V, V] + [A] * 7,
        out_specs=tuple(v[1] for v in outs.values()),
        scratch_shapes=list(scr.values()),
        compiler_params=pltpu.CompilerParams(collective_id=cid, has_side_effects=True, vmem_limit_bytes=67043328),
        name="block",
    )(bo, freq, *lns, hidden, cot, up, dw, q, o, kv)
    return dict(zip(outs, res))


def results_kernel(nt, tok, hg, kv, lno, oq, okv, oo, ou, od, tok_o, k_o, v_o, hg_o, a_o, b_o, c_o, d_o, oq_o, okv_o, oo_o, ou_o, od_o, tb, hb, kb, kt, lb, b0, b1, b2, b3, b4, sin, sout):
    BQ = tok.shape[0] // nt
    moves = []
    for i in range(nt):
        t = pl.ds(i * BQ, BQ)
        moves.append((hg.at[t], hb.at[t], hg_o.at[t]))
        moves.append((tok.at[t], tb.at[t], tok_o.at[t]))
    moves += [(ou, b3, ou_o), (od, b4, od_o), (oq, b0, oq_o), (oo, b2, oo_o), (okv, b1, okv_o)]
    n = len(moves)
    ins = [pltpu.make_async_copy(a, b, sin.at[i]) for i, (a, b, _) in enumerate(moves)]
    outs = [pltpu.make_async_copy(b, c, sout.at[i]) for i, (_, b, c) in enumerate(moves)]
    small = [pltpu.make_async_copy(kv, kb, sin.at[n]), pltpu.make_async_copy(lno, lb, sin.at[n + 1])]
    turned = [pltpu.make_async_copy(kt.at[pl.ds(0, 64)], k_o, sout.at[n]), pltpu.make_async_copy(kt.at[pl.ds(64, 64)], v_o, sout.at[n + 1])]
    for c in small + ins:
        c.start()
    for c in small:
        c.wait()
    kt[...] = kb[...].T
    for c in turned:
        c.start()
    for k, ref in enumerate((a_o, b_o, c_o, d_o)):
        ref[...] = lb[k, : ref.shape[0]]
    for a, b in zip(ins, outs):
        a.wait()
        b.start()
    for c in outs + turned:
        c.wait()


def results(v, rows):
    T, D = v["hg"].shape
    A = pl.BlockSpec(memory_space=pl.ANY)
    V = pl.BlockSpec(memory_space=pltpu.VMEM)
    sd = jax.ShapeDtypeStruct
    like = lambda k: sd(v[k].shape, v[k].dtype)
    vm = lambda k: pltpu.VMEM(v[k].shape, v[k].dtype)
    nt = 4
    Dm = pltpu.SemaphoreType.DMA
    order = ("out_tokens", "hg", "kvout", "lno", "oq", "okv", "oo", "ou", "od")
    return pl.pallas_call(
        functools.partial(results_kernel, nt),
        out_shape=(like("out_tokens"), sd((64, T), BF), sd((64, T), BF), like("hg")) + (sd((rows,), F32),) * 4 + tuple(like(k) for k in order[4:]),
        in_specs=[A] * 9,
        out_specs=(A,) * 4 + (V,) * 4 + (A,) * 5,
        scratch_shapes=[vm("out_tokens"), vm("hg"), vm("kvout"), pltpu.VMEM((128, T), BF), vm("lno")] + [vm(k) for k in order[4:]] + [Dm((2 * nt + 7,)), Dm((2 * nt + 7,))],
        name="results",
    )(*[v[k] for k in order])


def fits(mesh):
    return mesh.shape["shard"] == 8 and mesh.shape["ctx"] == 2


def fast_device(hidden, block_order, ln1_gain, ln1_bias, ln2_gain, ln2_bias, q_weight, kv_weight, o_weight, up_weight, down_weight, cotangent):
    seqs, span, width = hidden.shape
    rows = ln1_gain.shape[0]
    freq = 10000.0 ** (-2.0 * (np.arange(128) % (ROT // 2)) / ROT)
    freq = jnp.asarray(np.broadcast_to(freq, (8, 128)), F32)
    lns = [a.reshape(1, rows) for a in (ln1_gain, ln1_bias, ln2_gain, ln2_bias)]
    v = block_call(block_order, freq, hidden.reshape(span, width), cotangent.reshape(span, width), lns, up_weight, down_weight, q_weight, o_weight, kv_weight, width // rows // NY, span // 2, 1)
    tok, keys, values, hg, a, b, c, d, oq, okv, oo, ou, od = results(v, rows)
    return (tok[None], keys.T[None], values.T[None], hg[None], a, b, c, d, oq, okv, oo, ou, od)


def solution(mesh):
    return jax.shard_map(
        fast_device if fits(mesh) else on_device,
        mesh=mesh,
        in_specs=(
            P("shard", "ctx", None),
            P(),
            P("shard"),
            P("shard"),
            P("shard"),
            P("shard"),
            P("shard", "tp"),
            P("shard", None),
            P("shard", "tp"),
            P("shard", "tp"),
            P("shard", "tp"),
            P("shard", "ctx", None),
        ),
        out_specs=(
            P("shard", "ctx", None),
            P("shard", "ctx", None),
            P("shard", "ctx", None),
            P("shard", "ctx", None),
            P("shard"),
            P("shard"),
            P("shard"),
            P("shard"),
            P("shard", "tp"),
            P("shard", None),
            P("shard", "tp"),
            P("shard", "tp"),
            P("shard", "tp"),
        ),
        check_vma=False,
    )
```
